32 devices in a mesh: fsdp: 4 (over y, x), expert: 8 (over z, core).
Axes of the slice: x: 2, y: 2, z: 4, core: 2. Of those that a mesh axis runs over, the one named last changes fastest.
Arguments:
- inputs: bfloat16 [8, 512, 2048], P('expert', 'fsdp'), may hold values from -6 to 6
- teacher: bfloat16 [8, 512, 2048], P('expert', 'fsdp'), may hold values from -6 to 6
- lengths: int32 [16], replicated, may hold values from 1 to 448, as said below
- deal_order: int32 [16], replicated, may hold values from 0 to 15, as said below
- routes: int32 [8, 512, 4], P('expert', 'fsdp'), may hold values from 0 to 7, all different within a row; in each aligned block of 128 rows (0 to 127, 128 to 255, ..., all dimensions but the last counted through in order) at most 96 rows name the same one
- route_weights: float32 [8, 512, 4], P('expert', 'fsdp'), may hold values from 0.4 to 1.2
- norm_gains: bfloat16 [2, 2048], P(None, ('fsdp', 'expert')), may hold values from 0.5 to 1.5
- mixer_weights: bfloat16 [2048, 4, 2048], P('expert', None, 'fsdp')
- shared_weights: bfloat16 [2048, 3, 5632], P('expert', None, 'fsdp')
- shared_gate: bfloat16 [2048], P(('fsdp', 'expert')), may hold values from -0.125 to 0.125
- expert_gate: bfloat16 [8, 2048, 1408], P('expert', 'fsdp'), may hold values from -0.125 to 0.125
- expert_up: bfloat16 [8, 2048, 1408], P('expert', 'fsdp'), may hold values from -0.125 to 0.125
- expert_down: bfloat16 [8, 1408, 2048], P('expert', 'fsdp'), may hold values from -0.15625 to 0.15625
Outputs:
- out_block: bfloat16 [8, 512, 2048], P('expert', 'fsdp')
- grad_input: float32 [8, 512, 2048], P('expert', 'fsdp')
- grad_gains: float32 [2, 2048], P(None, ('fsdp', 'expert'))
- grad_mixer: float32 [2048, 4, 2048], P('expert', None, 'fsdp')
- grad_shared: float32 [2048, 3, 5632], P('expert', None, 'fsdp')
- grad_shared_gate: float32 [2048], P(('fsdp', 'expert'))
- grad_expert_gate: float32 [8, 2048, 1408], P('expert', 'fsdp')
- grad_expert_up: float32 [8, 2048, 1408], P('expert', 'fsdp')
- grad_expert_down: float32 [8, 1408, 2048], P('expert', 'fsdp')
The draws below stay inside these ranges and needn't reach their ends.
Inputs may be any that keep to these rules, and one draw needn't show every extreme that they name: `routes`: A token's 4 experts differ; the 128 tokens of one device name each expert at most 96 times, and some device names some expert exactly 96 times. `lengths`: the two sequences that one row holds have at most 512 tokens together; some sequence has exactly 448 tokens. A permutation of the 16 sequences: row g holds sequence deal_order[2g] and then deal_order[2g+1], packed from its start; the rest of the row is padding.
All inputs are finite; a program needn't handle non-finite values.
Results may differ from the reference program's by a relative error of at most 0.02.
Values may be sent and summed in bfloat16 or wider, within the bound.
A program may use at most 256 MiB of HBM per device.

```python
import math
import jax
import jax.numpy as jnp
import numpy as np
from jax import lax

D = 2048
HEADS = 16
HD = 128
EFF = 1408
SFF = 5632
TOP = 4
TOK_DEV = 128
ROW = 512
GROUPS = 8
SEQS = 16
TOKENS = 4096
EXPERTS = 8
CAP = 96
LEN_MAX = 448
N_FSDP = 4
N_EXPERT = 8


def dealt_sizes(key):
    subkeys = jax.random.split(jax.random.fold_in(key, 11), 4)
    first_len = jax.random.randint(subkeys[0], (GROUPS,), ROW // 4, LEN_MAX + 1)
    forced = jax.random.randint(subkeys[1], (), 0, GROUPS)
    first_len = jnp.where(jnp.arange(GROUPS) == forced, LEN_MAX, first_len)
    spread_raw = jax.random.randint(subkeys[2], (GROUPS,), 0, 1048576)
    second_len = ROW // 16 + spread_raw % (ROW - first_len - ROW // 16 + 1)
    dealing = jax.random.permutation(subkeys[3], SEQS).astype(jnp.int32)
    paired = jnp.stack([first_len, second_len], axis=1).reshape(SEQS).astype(jnp.int32)
    sizes_out = jnp.zeros((SEQS,), jnp.int32).at[dealing].set(paired)
    return (dealing, sizes_out)


def draw_lengths(key, part):
    return dealt_sizes(key)[1]


def draw_deal_order(key, part):
    return dealt_sizes(key)[0]


def draw_mixer_weights(key, part):
    noise = jax.random.normal(jax.random.fold_in(key, 3), (D, 4, D), jnp.float32)
    factor = jnp.array([1.0, 1.0, 1.0, 4.0], jnp.float32)[None, :, None] / math.sqrt(D)
    return (noise * factor).astype(jnp.bfloat16)


def draw_shared_weights(key, part):
    noise = jax.random.normal(jax.random.fold_in(key, 5), (D, 3, SFF), jnp.float32)
    factor = jnp.array([1.0 / math.sqrt(D), 1.0 / math.sqrt(D), 2.0 / math.sqrt(SFF)], jnp.float32)[None, :, None]
    return (noise * factor).astype(jnp.bfloat16)


def steps_of(stream_key, extent, cuts, low, high):
    def one(dim, blocks):
        heights = jax.random.uniform(jax.random.fold_in(jax.random.fold_in(stream_key, 6), dim), (blocks,), jnp.float32, low / len(cuts), high / len(cuts))
        return jnp.repeat(jnp.exp(heights), extent[dim] // blocks).reshape((-1,) + (1,) * (len(extent) - dim - 1))

    loudness = one(*cuts[0])
    for cut in cuts[1:]:
        loudness = loudness * one(*cut)
    return loudness


def deal_out(rng, own, number, rows, amount, top, reach, lean):
    sequence = jax.random.permutation(rng, amount)
    crowded, common = portions_of(amount, rows * top, reach, lean, True), portions_of(amount, rows * top, reach, lean, False)
    places = jnp.arange(amount)

    def named(sizes, offset_by):
        used = int((sizes > 0).sum())
        fixed = max(1, used // 4)
        passed = fixed + (places - fixed + offset_by * (used - fixed)) % max(1, amount - fixed)
        return jnp.zeros((amount,), jnp.int32).at[sequence[jnp.where(places < fixed, places, passed)]].set(jnp.asarray(sizes, jnp.int32))

    sizes = jnp.where(number % 4 == 0, named(crowded, number // 4), named(common, number - number // 4 - 1))
    mixed = jax.random.permutation(jax.random.fold_in(own, 3), amount)
    giver, receiver = mixed[0:amount // 2 * 2:2], mixed[1:amount // 2 * 2:2]
    margin = jnp.minimum(sizes[giver] - 1, reach - sizes[receiver]) // 2
    margin = jnp.where((giver == sequence[0]) | (receiver == sequence[0]) | (sizes[receiver] == 0), 0, jnp.maximum(margin, 0))
    passed = jax.random.randint(jax.random.fold_in(own, 4), (amount // 2,), 0, 1 << 20) % (margin + 1)
    sizes = sizes.at[giver].add(-passed).at[receiver].add(passed)
    members = jnp.searchsorted(jnp.cumsum(sizes), jnp.arange(rows * top), side="right").astype(jnp.int32)
    grid = members.reshape(top, rows).T
    grid = grid[jax.random.permutation(jax.random.fold_in(own, 1), rows)]
    offset_by = jax.random.randint(jax.random.fold_in(own, 2), (rows, 1), 0, top)
    return jnp.take_along_axis(grid, (jnp.arange(top)[None, :] + offset_by) % top, axis=1)


def portions_of(amount, total, limit, skew, full):
    portions = [(1 << 20) // math.isqrt(rank ** skew) + 1 for rank in range(1, amount + 1)]
    largest = limit if full else min(limit, max(-(-total // amount), total * portions[0] // sum(portions)))
    least = 1 if total - largest >= amount - 1 else 0
    holding, spare = [largest] + [least] * (amount - 1), total - largest - least * (amount - 1)
    while spare > 0:
        candidates = [i for i in range(1, amount) if holding[i] < largest] or [i for i in range(1, amount) if holding[i] < limit]
        mass, budget = sum([portions[i] for i in candidates]), spare
        for i in candidates:
            addition = min(limit - holding[i], max(1, budget * portions[i] // mass), spare)
            holding[i] = holding[i] + addition
            spare = spare - addition
    return np.array(holding)


def scatter_about(stream_key, dims, deviation, most, shards=(), kind=jnp.bfloat16):
    drawn = jax.random.normal(stream_key, dims, jnp.float32) * deviation
    if len(shards) > 0:
        drawn = steps_of(stream_key, dims, shards, -0.22, 0.18) * drawn
    return jnp.clip(drawn, min=-most, max=most).astype(kind)


def setup_inputs(seed: int = 0) -> dict:
    key_list = jax.random.split(jax.random.key(seed), 14)
    inputs = scatter_about(key_list[0], (GROUPS, ROW, D), 1.0, 6.0, ((0, 8), (1, 4)))
    teacher = scatter_about(key_list[1], (GROUPS, ROW, D), 1.0, 6.0, ((0, 8), (1, 4)))
    lengths = draw_lengths(jax.random.fold_in(key_list[13], 71), 0)
    deal_order = draw_deal_order(jax.random.fold_in(key_list[13], 71), 0)
    routes_keys = jax.random.split(jax.random.fold_in(key_list[4], 1), GROUPS * ROW // TOK_DEV)
    routes_turns = jax.random.permutation(jax.random.fold_in(key_list[4], 3), GROUPS * ROW // TOK_DEV)
    routes = jax.vmap(lambda own, number: deal_out(jax.random.fold_in(key_list[4], 2), own, number, TOK_DEV, EXPERTS, TOP, CAP, 1))(routes_keys, routes_turns).reshape((GROUPS, ROW, TOP))
    route_weights = jnp.clip(0.4 + 0.800000042 * jax.random.uniform(key_list[5], (GROUPS, ROW, TOP), jnp.float32) ** steps_of(key_list[5], (GROUPS, ROW, TOP), ((0, 8), (1, 4)), -0.2, 0.2), 0.4, 1.2)
    norm_gains = jnp.clip(1.0 + 0.1 * jax.random.normal(key_list[6], (2, D), jnp.float32), 0.5, 1.5).astype(jnp.bfloat16)
    mixer_weights = draw_mixer_weights(jax.random.fold_in(key_list[13], 71), 0)
    shared_weights = draw_shared_weights(jax.random.fold_in(key_list[13], 71), 0)
    shared_gate = scatter_about(key_list[9], (D,), D ** -0.5, 0.125, ((0, 32),))
    expert_gate = scatter_about(key_list[10], (EXPERTS, D, EFF), D ** -0.5, 0.125, ((0, 8), (1, 4)))
    expert_up = scatter_about(key_list[11], (EXPERTS, D, EFF), D ** -0.5, 0.125, ((0, 8), (1, 4)))
    expert_down = scatter_about(key_list[12], (EXPERTS, EFF, D), EFF ** -0.5, 0.15625, ((0, 8), (1, 4)))
    return {"inputs": inputs, "teacher": teacher, "lengths": lengths, "deal_order": deal_order, "routes": routes, "route_weights": route_weights, "norm_gains": norm_gains, "mixer_weights": mixer_weights, "shared_weights": shared_weights, "shared_gate": shared_gate, "expert_gate": expert_gate, "expert_up": expert_up, "expert_down": expert_down}


THETA = 1000000.0
EPSILON = 1e-06
NEG_LARGE = -1e+30
HIGHEST = lax.Precision.HIGHEST

@jax.custom_vjp
def low(v):
    return lax.optimization_barrier(v.astype(jnp.bfloat16)).astype(jnp.float32)

@jax.custom_vjp
def low_back(v):
    return v

def low_keep(v):
    return (low(v), None)

def low_pass(kept, grad):
    return (grad,)

def back_keep(v):
    return (v, None)

def back_low(kept, grad):
    return (low(grad),)
low.defvjp(low_keep, low_pass)
low_back.defvjp(back_keep, back_low)

def rope_tables(positions):
    half_size = HD // 2
    inverse = THETA ** (-(jnp.arange(half_size, dtype=jnp.float32) * 2.0) / HD)
    angles = positions.astype(jnp.float32)[:, None] * inverse[None, :]
    cosine_table = jnp.concatenate([jnp.cos(angles), jnp.cos(angles)], axis=1)[:, None, :]
    sine_table = jnp.concatenate([jnp.sin(angles), jnp.sin(angles)], axis=1)[:, None, :]
    return (cosine_table, sine_table)

def rotary(values, cosine_table, sine_table):
    half_size = values.shape[-1] // 2
    turned = jnp.concatenate([-values[..., half_size:], values[..., :half_size]], axis=-1)
    return values * cosine_table + turned * sine_table

def layout_rows(lengths, deal_order):
    firsts = lengths[deal_order[0::2]].astype(jnp.int32)
    seconds = lengths[deal_order[1::2]].astype(jnp.int32)
    places = jnp.arange(ROW, dtype=jnp.int32)[None, :]
    segment = (places >= firsts[:, None]).astype(jnp.int32) + (places >= (firsts + seconds)[:, None]).astype(jnp.int32)
    position = places - firsts[:, None] * (segment >= 1).astype(jnp.int32) - seconds[:, None] * (segment >= 2).astype(jnp.int32)
    return (segment, position)

def attend(pieces):
    group_queries, group_keys, group_values, group_segment = pieces
    places = jnp.arange(ROW, dtype=jnp.int32)
    allowed = (group_segment[:, None] == group_segment[None, :]) & (places[None, :] <= places[:, None])
    scores = low_back(HD ** (-0.5) * jnp.einsum('qhd,khd->hqk', group_queries, group_keys, precision=HIGHEST))
    scores = jnp.where(allowed[None], scores, NEG_LARGE)
    probabilities = jax.nn.softmax(scores, axis=2)
    return jnp.einsum('hqk,khd->qhd', low(probabilities), group_values, precision=HIGHEST)

def reference(inputs, teacher, lengths, deal_order, routes, route_weights, norm_gains, mixer_weights, shared_weights, shared_gate, expert_gate, expert_up, expert_down):
    segment, position = layout_rows(lengths, deal_order)
    flat_segment = segment.reshape(TOKENS)
    cosine_table, sine_table = rope_tables(position.reshape(TOKENS))
    chosen = routes.reshape(TOKENS * TOP).astype(jnp.int32)
    sort_order = jnp.argsort(chosen, stable=True).astype(jnp.int32)
    arranged = chosen[sort_order]
    counts = lax.optimization_barrier(jnp.sum((chosen[:, None] == jnp.arange(EXPERTS, dtype=jnp.int32)[None, :]).astype(jnp.int32), axis=0))
    starts = (jnp.cumsum(counts) - counts).astype(jnp.int32)
    offsets = (jnp.arange(TOKENS * TOP, dtype=jnp.int32) - starts[arranged]).astype(jnp.int32)
    window_rows = min(TOKENS * TOP, CAP * N_FSDP * N_EXPERT)
    weights_route = route_weights.reshape(TOKENS, TOP).astype(jnp.float32)

    def block_forward(flat_inputs, gains, mixer, shared, gate_vector, in_gate, in_up, out_down):
        first_scale = lax.rsqrt(lax.optimization_barrier(jnp.mean(flat_inputs * flat_inputs, axis=1, keepdims=True)) + EPSILON)
        normed = low(flat_inputs * first_scale * gains[0][None, :])
        projected = jnp.einsum('td,dke->tke', normed, mixer[:, :3], precision=HIGHEST)
        query_raw = low_back(projected[:, 0]).reshape(TOKENS, HEADS, HD)
        key_raw = low_back(projected[:, 1]).reshape(TOKENS, HEADS, HD)
        values = low_back(low(projected[:, 2])).reshape(GROUPS, ROW, HEADS, HD)
        queries = low(rotary(query_raw, cosine_table, sine_table)).reshape(GROUPS, ROW, HEADS, HD)
        keys_all = low(rotary(key_raw, cosine_table, sine_table)).reshape(GROUPS, ROW, HEADS, HD)
        context = lax.map(jax.checkpoint(attend), (queries, keys_all, values, segment))
        context = low_back(low(context.reshape(TOKENS, D)))
        residual = flat_inputs + low_back(jnp.einsum('tc,dc->td', context, mixer[:, 3], precision=HIGHEST))
        second_scale = lax.rsqrt(lax.optimization_barrier(jnp.mean(residual * residual, axis=1, keepdims=True)) + EPSILON)
        mixed_in = low(residual * second_scale * gains[1][None, :])
        shared_pre = jnp.einsum('td,dkf->tkf', mixed_in, shared[:, :2], precision=HIGHEST)
        shared_hidden = low(jax.nn.silu(low_back(shared_pre[:, 0])) * low_back(shared_pre[:, 1]))
        shared_out = low_back(jnp.einsum('tf,df->td', shared_hidden, shared[:, 2], precision=HIGHEST))
        gate_value = jax.nn.sigmoid(jnp.dot(mixed_in, gate_vector, precision=HIGHEST))
        copies = low_back(jnp.broadcast_to(mixed_in[:, None, :], (TOKENS, TOP, D))).reshape(TOKENS * TOP, D)
        padded = jnp.concatenate([copies[sort_order], jnp.zeros((window_rows, D), jnp.float32)], axis=0)

        def run_expert(expert_index):
            rows_in = lax.dynamic_slice_in_dim(padded, starts[expert_index], window_rows, 0)
            gate_pre = low_back(jnp.dot(rows_in, in_gate[expert_index], precision=HIGHEST))
            up_pre = low_back(jnp.dot(rows_in, in_up[expert_index], precision=HIGHEST))
            hidden = low(jax.nn.silu(gate_pre) * up_pre)
            return low_back(low(jnp.dot(hidden, out_down[expert_index], precision=HIGHEST)))
        results = lax.map(jax.checkpoint(run_expert), jnp.arange(EXPERTS, dtype=jnp.int32))
        picked = results[arranged, offsets]
        expert_out = jnp.zeros((TOKENS * TOP, D), jnp.float32).at[sort_order].set(picked).reshape(TOKENS, TOP, D)
        routed_sum = lax.optimization_barrier(jnp.sum(weights_route[:, :, None] * expert_out, axis=1))
        return residual + gate_value[:, None] * shared_out + routed_sum
    block_total, pullback = jax.vjp(block_forward, inputs.reshape(TOKENS, D).astype(jnp.float32), norm_gains.astype(jnp.float32), mixer_weights.astype(jnp.float32), shared_weights.astype(jnp.float32), shared_gate.astype(jnp.float32), expert_gate.astype(jnp.float32), expert_up.astype(jnp.float32), expert_down.astype(jnp.float32))
    valid_count = jnp.sum(lengths).astype(jnp.float32)
    valid_mask = (flat_segment < 2).astype(jnp.float32)
    cotangent = TOKENS / valid_count * valid_mask[:, None] * (block_total - teacher.reshape(TOKENS, D).astype(jnp.float32))
    gradients = pullback(cotangent)
    return (block_total.astype(jnp.bfloat16).reshape(GROUPS, ROW, D), gradients[0].reshape(GROUPS, ROW, D), gradients[1], gradients[2], gradients[3], gradients[4], gradients[5], gradients[6], gradients[7])
```

```python
import functools

import jax
import jax.numpy as jnp
from jax import lax
from jax.experimental import pallas as pl
from jax.experimental.pallas import tpu as pltpu
from jax.sharding import PartitionSpec as P

HD = 128
TOP = 4
THETA = 1000000.0
EPSILON = 1e-06
NEG_LARGE = -1e30
MESH = pl.DeviceIdType.MESH
F32 = jnp.float32
BF16 = jnp.bfloat16


def turn(values):
    half = values.shape[-1] // 2
    return jnp.concatenate([-values[..., half:], values[..., :half]], axis=-1)


def turn_back(values):
    half = values.shape[-1] // 2
    return jnp.concatenate([values[..., half:], -values[..., :half]], axis=-1)


def norm_back(incoming, values, scale_rows, gain_row):
    unit_rows = values * scale_rows[:, None]
    gain_grad = jnp.sum(incoming * unit_rows, axis=0)
    dunit = incoming * gain_row[None, :]
    back_rows = scale_rows[:, None] * (
        dunit - unit_rows * jnp.mean(dunit * unit_rows, axis=1, keepdims=True)
    )
    return (back_rows, gain_grad)


def dot(form, left, right):
    return jnp.einsum(form, left, right, preferred_element_type=F32)


def swap_x(values):
    return lax.ppermute(values, "fsdp", [(0, 1), (1, 0), (2, 3), (3, 2)])


def swap_y(values):
    return lax.ppermute(values, "fsdp", [(0, 2), (2, 0), (1, 3), (3, 1)])


def square_gather(block):
    half = block.shape[0] // 2
    from_x = swap_x(block)
    from_y = swap_y(block)
    low = swap_y(from_x[:half])
    high = swap_x(from_y[half:])
    return [block, from_x, from_y, low, high]


def square_scatter(parts):
    half = parts[0].shape[0] // 2
    low_send = parts[3][:half].astype(BF16)
    high_send = parts[3][half:].astype(BF16)
    low = swap_x(low_send)
    high = swap_y(high_send)
    to_y = jnp.concatenate(
        [(parts[2][:half].astype(F32) + low.astype(F32)).astype(BF16), parts[2][half:].astype(BF16)]
    )
    to_x = jnp.concatenate(
        [parts[1][:half].astype(BF16), (parts[1][half:].astype(F32) + high.astype(F32)).astype(BF16)]
    )
    from_x = swap_x(to_x)
    from_y = swap_y(to_y)
    return parts[0].astype(F32) + from_x.astype(F32) + from_y.astype(F32)


def row_tokens(block):
    return jnp.concatenate(square_gather(block), axis=0)


def row_scatter(product):
    quarter = product.shape[0] // 4
    return square_scatter([product[j * quarter : (j + 1) * quarter] for j in range(4)])


def gather_shards(shard, index):
    rows = shard.shape[0]
    half = rows // 2
    own, from_x, from_y, low, high = square_gather(shard)
    whole = jnp.zeros((4 * rows,) + shard.shape[1:], shard.dtype)
    for piece, start in (
        (own, index * rows),
        (from_x, (index ^ 1) * rows),
        (from_y, (index ^ 2) * rows),
        (low, (index ^ 3) * rows),
        (high, (index ^ 3) * rows + half),
    ):
        whole = lax.dynamic_update_slice(whole, piece, (start, 0))
    return whole


def scatter_shards(whole, index):
    rows = whole.shape[0] // 4
    return square_scatter(
        [lax.dynamic_slice_in_dim(whole, (index ^ j) * rows, rows) for j in range(4)]
    )


def opening_kernel(
    chips,
    x_ref, vector_ref, routed_ref, mixer_ref, gate_ref,
    gains_ref, tables_ref, row_ref, mixers_ref, gates_ref,
    vectors, send_v, receive_v, send_t, receive_t,
    send_n, receive_n, send_g, receive_g,
    up_sem, down_sem, in_low, in_high, to_partner, in_partner, local,
):
    nf, ne = lax.axis_size("fsdp"), lax.axis_size("expert")
    total = nf * ne
    f, e = lax.axis_index("fsdp"), lax.axis_index("expert")
    me = f * ne + e
    z, c = e // 2, lax.rem(e, 2)
    xn, yn = f ^ 1, f ^ 2
    up = (f, jnp.minimum(z + 1, chips - 1) * 2 + c)
    down = (f, jnp.maximum(z - 1, 0) * 2 + c)
    partner = (f, z * 2 + 1 - c)
    own_mixer = pltpu.make_async_copy(mixer_ref, mixers_ref.at[:, e], local.at[0])
    own_gate = pltpu.make_async_copy(gate_ref, gates_ref.at[f], local.at[1])
    own_mixer.start()
    own_gate.start()
    barrier = pltpu.get_barrier_semaphore()

    def greet(step, carry):
        peer = lax.rem(me + step, total)
        pl.semaphore_signal(
            barrier, inc=1, device_id=(peer // ne, lax.rem(peer, ne)), device_id_type=MESH
        )
        return carry

    lax.fori_loop(1, total, greet, 0)
    pl.semaphore_wait(barrier, total - 1)

    def remote(source, target, send, receive, device):
        return pltpu.make_async_remote_copy(
            src_ref=source,
            dst_ref=target,
            send_sem=send,
            recv_sem=receive,
            device_id=device,
            device_id_type=MESH,
        )

    def vector_copy(slot, peer):
        return remote(
            vector_ref, vectors.at[slot], send_v.at[peer], receive_v.at[slot],
            (peer // ne, lax.rem(peer, ne)),
        )

    def table_copy(slot, peer):
        return remote(routed_ref, tables_ref.at[slot], send_t.at[peer], receive_t.at[slot], (f, peer))

    def start_vector(step, carry):
        vector_copy(me, lax.rem(me + step, total)).start()
        return carry

    def start_table(step, carry):
        table_copy(e, lax.rem(e + step, ne)).start()
        return carry

    lax.fori_loop(1, total, start_vector, 0)
    lax.fori_loop(1, ne, start_table, 0)
    vectors[me] = vector_ref[...]
    tables_ref[e] = routed_ref[...]

    def shard(origin, target, send, receive, own):
        place = mixers_ref.at[:, origin * 2 + c]
        return remote(mixer_ref if own else place, place, send, receive, target)

    def upward(origin, r, own=False):
        return shard(origin, up, up_sem.at[r], in_low.at[r], own)

    def downward(origin, r, own=False):
        return shard(origin, down, down_sem.at[r], in_high.at[r], own)

    def across(origin, own=False):
        return shard(origin, partner, to_partner.at[origin], in_partner.at[origin], own)

    @pl.when(z < chips - 1)
    def _():
        upward(z, 0, True).start()

    @pl.when(z > 0)
    def _():
        downward(z, 0, True).start()

    across(z, True).start()

    def end_vector(step, carry):
        peer = lax.rem(me + step, total)
        vector_copy(peer, peer).wait_recv()
        return carry

    lax.fori_loop(1, total, end_vector, 0)
    blocks = gains_ref.shape[1] // 128
    per = total // blocks
    for block in range(blocks):
        gains_ref[:, block * 128 : (block + 1) * 128] = jnp.sum(
            vectors[block * per : (block + 1) * per], axis=0
        )
    half = x_ref.shape[0] // 2
    low, high = pl.ds(0, half), pl.ds(half, half)

    def piece(index, ref, origin, rows, device, slot):
        place = ref.at[origin, rows]
        send, receive = (send_n, receive_n) if index == 0 else (send_g, receive_g)
        return remote(place, place, send.at[slot], receive.at[slot], (device, e))

    def outgoing(index, ref, first, second):
        return [
            piece(index, ref, f, first, xn, 0),
            piece(index, ref, f, second, yn, 1),
            piece(index, ref, f, second, xn, 2),
            piece(index, ref, f, first, yn, 3),
        ]

    def relays(index, ref, first, second):
        return [piece(index, ref, xn, first, yn, 4), piece(index, ref, yn, second, xn, 5)]

    for rows in (low, high):
        values = x_ref[rows].astype(F32)
        scale = lax.rsqrt(jnp.mean(values * values, axis=1, keepdims=True) + EPSILON)
        row_ref[f, rows] = (values * scale * gains_ref[0:1]).astype(BF16)
    own_gate.wait()
    row_out = outgoing(0, row_ref, low, high)
    row_relay = relays(0, row_ref, low, high)
    depth = gate_ref.shape[0] // 2
    first, second = pl.ds(0, depth), pl.ds(depth, depth)
    gate_out = outgoing(1, gates_ref, first, second)
    gate_relay = relays(1, gates_ref, first, second)
    for copy in row_out + gate_out:
        copy.start()
    piece(0, row_ref, xn, low, xn, 0).wait_recv()
    row_relay[0].start()
    piece(0, row_ref, yn, high, yn, 1).wait_recv()
    row_relay[1].start()

    def hop(r, carry):
        before, after = z - r, z + r

        @pl.when(before >= 0)
        def _():
            upward(before, r - 1).wait_recv()

            @pl.when(z < chips - 1)
            def _():
                upward(before, r).start()

            across(before).start()

        @pl.when(after < chips)
        def _():
            downward(after, r - 1).wait_recv()

            @pl.when(z > 0)
            def _():
                downward(after, r).start()

            across(after).start()

        return carry

    lax.fori_loop(1, 3, hop, 0)
    piece(1, gates_ref, xn, first, xn, 0).wait_recv()
    gate_relay[0].start()
    piece(1, gates_ref, yn, second, yn, 1).wait_recv()
    gate_relay[1].start()
    lax.fori_loop(3, chips, hop, 0)

    for index, ref, (one, two) in ((0, row_ref, (low, high)), (1, gates_ref, (first, second))):
        piece(index, ref, xn, two, xn, 2).wait_recv()
        piece(index, ref, yn, one, yn, 3).wait_recv()
        piece(index, ref, f ^ 3, one, yn, 4).wait_recv()
        piece(index, ref, f ^ 3, two, xn, 5).wait_recv()
    for copy in row_out + gate_out + row_relay + gate_relay:
        copy.wait_send()
    own_mixer.wait()

    @pl.when(z < chips - 1)
    def _():
        upward(z, 0, True).wait_send()

    @pl.when(z > 0)
    def _():
        downward(z, 0, True).wait_send()

    def finish(r, carry):
        before, after = z - r, z + r

        @pl.when((before >= 0) & (z < chips - 1))
        def _():
            upward(before, r).wait_send()

        @pl.when((after < chips) & (z > 0))
        def _():
            downward(after, r).wait_send()

        return carry

    lax.fori_loop(1, chips, finish, 0)

    def shared(origin, carry):
        across(origin).wait_send()
        across(origin).wait_recv()
        return carry

    lax.fori_loop(0, chips, shared, 0)

    def sent_vector(step, carry):
        peer = lax.rem(me + step, total)
        vector_copy(peer, peer).wait_send()
        return carry

    def end_table(step, carry):
        peer = lax.rem(e + step, ne)
        copy = table_copy(peer, peer)
        copy.wait_recv()
        copy.wait_send()
        return carry

    lax.fori_loop(1, total, sent_vector, 0)
    lax.fori_loop(1, ne, end_table, 0)


def opening(x, vector, routed, mixer, gate, nf):
    ne = routed.shape[0]
    chips, devices = ne // 2, nf * ne
    whole = pl.BlockSpec(memory_space=pltpu.VMEM)
    far = pl.BlockSpec(memory_space=pl.ANY)
    dma = pltpu.SemaphoreType.DMA
    return pl.pallas_call(
        functools.partial(opening_kernel, chips),
        out_shape=[
            jax.ShapeDtypeStruct((8, x.shape[1]), F32),
            jax.ShapeDtypeStruct((ne,) + routed.shape, F32),
            jax.ShapeDtypeStruct((nf,) + x.shape, BF16),
            jax.ShapeDtypeStruct((mixer.shape[0], ne) + mixer.shape[1:], BF16),
            jax.ShapeDtypeStruct((nf,) + gate.shape, BF16),
        ],
        in_specs=[whole] * 5,
        out_specs=[whole, whole, whole, far, far],
        scratch_shapes=[pltpu.VMEM((devices,) + vector.shape, F32)]
        + [dma((devices,))] * 2
        + [dma((ne,))] * 2
        + [dma((6,))] * 4
        + [dma((chips,))] * 6
        + [dma((2,))],
        compiler_params=pltpu.CompilerParams(
            collective_id=1, has_side_effects=True, vmem_limit_bytes=24 * 1024 * 1024
        ),
        name="opening",
    )(x, vector, routed, mixer, gate)


def collect_kernel(terms_ref, sum_ref, arrived, send, receive):
    nf, ne = lax.axis_size("fsdp"), lax.axis_size("expert")
    total = nf * ne
    me = lax.axis_index("fsdp") * ne + lax.axis_index("expert")
    barrier = pltpu.get_barrier_semaphore()

    def greet(step, carry):
        peer = lax.rem(me + step, total)
        pl.semaphore_signal(
            barrier, inc=1, device_id=(peer // ne, lax.rem(peer, ne)), device_id_type=MESH
        )
        return carry

    lax.fori_loop(1, total, greet, 0)
    pl.semaphore_wait(barrier, total - 1)

    def copy_of(slot, peer):
        return pltpu.make_async_remote_copy(
            src_ref=terms_ref.at[peer],
            dst_ref=arrived.at[slot],
            send_sem=send.at[peer],
            recv_sem=receive.at[slot],
            device_id=(peer // ne, lax.rem(peer, ne)),
            device_id_type=MESH,
        )

    def begin(step, carry):
        copy_of(me, lax.rem(me + step, total)).start()
        return carry

    lax.fori_loop(1, total, begin, 0)
    arrived[me] = terms_ref[me]

    def end(step, carry):
        peer = lax.rem(me + step, total)
        copy = copy_of(peer, peer)
        copy.wait_recv()
        copy.wait_send()
        return carry

    lax.fori_loop(1, total, end, 0)
    sum_ref[...] = jnp.sum(arrived[...], axis=0)


def collect(terms):
    devices = terms.shape[0]
    return pl.pallas_call(
        collect_kernel,
        out_shape=jax.ShapeDtypeStruct(terms.shape[1:], terms.dtype),
        in_specs=[pl.BlockSpec(memory_space=pltpu.VMEM)],
        out_specs=pl.BlockSpec(memory_space=pltpu.VMEM),
        scratch_shapes=[pltpu.VMEM(terms.shape, terms.dtype)]
        + [pltpu.SemaphoreType.DMA((devices,))] * 2,
        compiler_params=pltpu.CompilerParams(collective_id=2, has_side_effects=True),
        name="collect",
    )(terms)


def line_entry(f, z, c, chips):
    up = (f, jnp.minimum(z + 1, chips - 1) * 2 + c)
    down = (f, jnp.maximum(z - 1, 0) * 2 + c)
    partner = (f, z * 2 + 1 - c)
    barrier = pltpu.get_barrier_semaphore()
    pl.semaphore_signal(barrier, inc=1, device_id=partner, device_id_type=MESH)

    @pl.when(z < chips - 1)
    def _():
        pl.semaphore_signal(barrier, inc=1, device_id=up, device_id_type=MESH)

    @pl.when(z > 0)
    def _():
        pl.semaphore_signal(barrier, inc=1, device_id=down, device_id_type=MESH)

    known = 1 + jnp.where(z < chips - 1, 1, 0) + jnp.where(z > 0, 1, 0)
    pl.semaphore_wait(barrier, known)
    return up, down, partner


def line_gather_kernel(chips, block_ref, all_ref, up_sem, down_sem, in_low, in_high, to_partner, in_partner, own_sem):
    f, e = lax.axis_index("fsdp"), lax.axis_index("expert")
    z, c = e // 2, lax.rem(e, 2)
    own = pltpu.make_async_copy(block_ref, all_ref.at[e], own_sem)
    own.start()
    up, down, partner = line_entry(f, z, c, chips)

    def copy(origin, target, send, receive):
        place = all_ref.at[origin * 2 + c]
        return pltpu.make_async_remote_copy(
            src_ref=place,
            dst_ref=place,
            send_sem=send,
            recv_sem=receive,
            device_id=target,
            device_id_type=MESH,
        )

    def upward(origin, r):
        return copy(origin, up, up_sem.at[r], in_low.at[r])

    def downward(origin, r):
        return copy(origin, down, down_sem.at[r], in_high.at[r])

    def across(origin):
        return copy(origin, partner, to_partner.at[origin], in_partner.at[origin])

    own.wait()

    @pl.when(z < chips - 1)
    def _():
        upward(z, 0).start()

    @pl.when(z > 0)
    def _():
        downward(z, 0).start()

    across(z).start()

    def hop(r, carry):
        low, high = z - r, z + r

        @pl.when(low >= 0)
        def _():
            upward(low, r - 1).wait_recv()

            @pl.when(z < chips - 1)
            def _():
                upward(low, r).start()

            across(low).start()

        @pl.when(high < chips)
        def _():
            downward(high, r - 1).wait_recv()

            @pl.when(z > 0)
            def _():
                downward(high, r).start()

            across(high).start()

        return carry

    lax.fori_loop(1, chips, hop, 0)

    def finish(r, carry):
        low, high = z - r, z + r

        @pl.when((low >= 0) & (z < chips - 1))
        def _():
            upward(low, r).wait_send()

        @pl.when((high < chips) & (z > 0))
        def _():
            downward(high, r).wait_send()

        return carry

    lax.fori_loop(0, chips, finish, 0)

    def shared(origin, carry):
        across(origin).wait_send()
        across(origin).wait_recv()
        return carry

    lax.fori_loop(0, chips, shared, 0)


def line_gather(block, ne, cid):
    chips = ne // 2
    return pl.pallas_call(
        functools.partial(line_gather_kernel, chips),
        out_shape=jax.ShapeDtypeStruct((ne,) + block.shape, block.dtype),
        in_specs=[pl.BlockSpec(memory_space=pltpu.VMEM)],
        out_specs=pl.BlockSpec(memory_space=pltpu.VMEM),
        scratch_shapes=[pltpu.SemaphoreType.DMA((chips,))] * 6 + [pltpu.SemaphoreType.DMA],
        compiler_params=pltpu.CompilerParams(collective_id=cid, has_side_effects=True),
        name=f"line_gather{cid}",
    )(block)


def line_scatter_kernel(
    chips, terms_ref, sum_ref, theirs, going_up, going_down, from_low, from_high,
    up_sem, down_sem, in_low, in_high, to_partner, in_partner,
):
    f, e = lax.axis_index("fsdp"), lax.axis_index("expert")
    z, c = e // 2, lax.rem(e, 2)
    up, down, partner = line_entry(f, z, c, chips)

    def across(target):
        return pltpu.make_async_remote_copy(
            src_ref=terms_ref.at[target * 2 + 1 - c],
            dst_ref=theirs.at[target],
            send_sem=to_partner.at[target],
            recv_sem=in_partner.at[target],
            device_id=partner,
            device_id_type=MESH,
        )

    def upward(target):
        return pltpu.make_async_remote_copy(
            src_ref=going_up.at[target],
            dst_ref=from_low.at[target],
            send_sem=up_sem.at[target],
            recv_sem=in_low.at[target],
            device_id=up,
            device_id_type=MESH,
        )

    def downward(target):
        return pltpu.make_async_remote_copy(
            src_ref=going_down.at[target],
            dst_ref=from_high.at[target],
            send_sem=down_sem.at[target],
            recv_sem=in_high.at[target],
            device_id=down,
            device_id_type=MESH,
        )

    def offer(r, carry):
        across(r).start()
        across(chips - 1 - r).start()
        return carry

    lax.fori_loop(0, chips // 2, offer, 0)

    def chip_term(target):
        return terms_ref[target * 2 + c].astype(F32) + theirs[target].astype(F32)

    def pass_on(r, carry):
        high, low = chips - 1 - r, r

        @pl.when(high > z)
        def _():
            across(high).wait_recv()

            @pl.when(z > 0)
            def _():
                upward(high).wait_recv()
                going_up[high] = (chip_term(high) + from_low[high].astype(F32)).astype(BF16)

            @pl.when(z == 0)
            def _():
                going_up[high] = chip_term(high).astype(BF16)

            upward(high).start()

        @pl.when(low < z)
        def _():
            across(low).wait_recv()

            @pl.when(z < chips - 1)
            def _():
                downward(low).wait_recv()
                going_down[low] = (chip_term(low) + from_high[low].astype(F32)).astype(BF16)

            @pl.when(z == chips - 1)
            def _():
                going_down[low] = chip_term(low).astype(BF16)

            downward(low).start()

        return carry

    lax.fori_loop(0, chips, pass_on, 0)
    across(z).wait_recv()
    sum_ref[...] = chip_term(z)

    @pl.when(z > 0)
    def _():
        upward(z).wait_recv()
        sum_ref[...] += from_low[z].astype(F32)

    @pl.when(z < chips - 1)
    def _():
        downward(z).wait_recv()
        sum_ref[...] += from_high[z].astype(F32)

    def finish(target, carry):
        across(target).wait_send()

        @pl.when(target > z)
        def _():
            upward(target).wait_send()

        @pl.when(target < z)
        def _():
            downward(target).wait_send()

        return carry

    lax.fori_loop(0, chips, finish, 0)


def line_scatter(terms, cid):
    ne = terms.shape[0]
    chips = ne // 2
    blocks = (chips,) + terms.shape[1:]
    return pl.pallas_call(
        functools.partial(line_scatter_kernel, chips),
        out_shape=jax.ShapeDtypeStruct(terms.shape[1:], F32),
        in_specs=[pl.BlockSpec(memory_space=pltpu.VMEM)],
        out_specs=pl.BlockSpec(memory_space=pltpu.VMEM),
        scratch_shapes=[pltpu.VMEM(blocks, terms.dtype)] * 5
        + [pltpu.SemaphoreType.DMA((chips,))] * 6,
        compiler_params=pltpu.CompilerParams(
            collective_id=cid, has_side_effects=True, vmem_limit_bytes=60 * 1024 * 1024
        ),
        name=f"line_scatter{cid}",
    )(terms)


def on_device(
    inputs,
    teacher,
    lengths,
    deal_order,
    routes,
    route_weights,
    norm_gains,
    mixer_weights,
    shared_weights,
    shared_gate,
    expert_gate,
    expert_up,
    expert_down,
):
    tokens_dev = inputs.shape[1]
    width = inputs.shape[2]
    nf = lax.axis_size("fsdp")
    ne = lax.axis_size("expert")
    devices = nf * ne
    row_len = tokens_dev * nf
    capacity = 3 * tokens_dev * TOP // (2 * ne)
    total_tokens = row_len * ne
    columns = mixer_weights.shape[2]
    heads_local = columns // HD
    f_index = lax.axis_index("fsdp")
    e_index = lax.axis_index("expert")

    piece = norm_gains.shape[1]
    slot = (f_index * ne + e_index) % (128 // piece)
    vector = jnp.concatenate([norm_gains, shared_gate[None]], axis=0).astype(F32)
    vector = lax.dynamic_update_slice(jnp.zeros((8, 128), F32), vector, (0, slot * piece))
    chosen = routes[0]
    weights_route = route_weights[0]
    expert_ids = jnp.arange(ne, dtype=jnp.int32)
    routed = jnp.sum(
        jnp.where(chosen.T[None] == expert_ids[:, None, None], weights_route.T[None], 0.0), axis=1
    )
    mixer_shard = jnp.transpose(mixer_weights, (1, 0, 2))
    gains, tables, row_blocks, mixers, gates = opening(
        inputs[0], vector, routed, mixer_shard, expert_gate[0], nf
    )
    first_gain, second_gain, gate_vector = gains[0], gains[1], gains[2]
    token_weight = lax.dynamic_index_in_dim(tables, e_index, axis=1, keepdims=False)
    mixers = mixers.reshape(4, width, columns)
    mixer_in, mixer_out = mixers[:3], mixers[3]
    gate_rows = gates.reshape(width, gates.shape[2])
    order_x = f_index ^ jnp.arange(nf, dtype=jnp.int32)
    row_normed = row_blocks[order_x].reshape(row_len, width)

    shared_shard, up_shard, down_shard, gains = lax.optimization_barrier(
        (shared_weights, expert_up[0], expert_down[0], gains)
    )
    shared_shard = jnp.transpose(shared_shard, (1, 0, 2))
    shared_in = lax.all_gather(shared_shard[:2], "expert", axis=1, tiled=True)
    shared_down = lax.all_gather(shared_shard[2], "expert", axis=0, tiled=True)
    up_rows = gather_shards(up_shard, f_index)
    down_rows = gather_shards(down_shard, f_index)

    first_len = lengths[deal_order[2 * e_index]]
    second_len = lengths[deal_order[2 * e_index + 1]]
    row_places = (
        (f_index ^ jnp.arange(nf, dtype=jnp.int32))[:, None] * tokens_dev
        + jnp.arange(tokens_dev, dtype=jnp.int32)[None]
    ).reshape(row_len)
    row_segment = (row_places >= first_len).astype(jnp.int32) + (
        row_places >= first_len + second_len
    ).astype(jnp.int32)
    row_position = (
        row_places
        - first_len * (row_segment >= 1).astype(jnp.int32)
        - second_len * (row_segment >= 2).astype(jnp.int32)
    )
    own_segment = row_segment[:tokens_dev]
    allowed = (row_segment[:, None] == row_segment[None, :]) & (
        row_places[None, :] <= row_places[:, None]
    )
    inverse = THETA ** (-(jnp.arange(HD // 2, dtype=F32) * 2.0) / HD)
    angles = row_position.astype(F32)[:, None] * inverse[None, :]
    cosine = jnp.concatenate([jnp.cos(angles)] * 2, axis=1)[:, None, :]
    sine = jnp.concatenate([jnp.sin(angles)] * 2, axis=1)[:, None, :]

    flat_inputs = inputs[0].astype(F32)
    first_scale = lax.rsqrt(jnp.mean(flat_inputs * flat_inputs, axis=1) + EPSILON)
    projected = dot("td,kde->kte", row_normed, mixer_in)

    def heads(values):
        return values.reshape(row_len, heads_local, HD)

    raw_query, raw_key = heads(projected[0]), heads(projected[1])
    queries = (raw_query * cosine + turn(raw_query) * sine).astype(BF16)
    keys = (raw_key * cosine + turn(raw_key) * sine).astype(BF16)
    values = heads(projected[2].astype(BF16))
    score_factor = HD ** (-0.5)

    def score():
        raw = dot("qhd,khd->hqk", queries, keys)
        return jnp.where(allowed[None], raw * score_factor, NEG_LARGE)

    scores = score()
    top_score = jnp.max(scores, axis=2, keepdims=True)
    shifted = jnp.exp(scores - top_score)
    row_total = jnp.sum(shifted, axis=2, keepdims=True)
    probabilities = shifted / row_total
    log_total = top_score + jnp.log(row_total)
    context = dot("hqk,khd->qhd", probabilities.astype(BF16), values)
    context = context.reshape(row_len, columns).astype(BF16)
    attn_out = row_scatter(dot("tc,dc->td", context, mixer_out))
    residual = flat_inputs + attn_out
    second_scale = lax.rsqrt(jnp.mean(residual * residual, axis=1) + EPSILON)
    mixed_in = (residual * second_scale[:, None] * second_gain[None, :]).astype(BF16)

    tokens_all = line_gather(mixed_in, ne, 3)
    routed_here = token_weight > 0.0
    marks = routed_here.astype(BF16)
    upper = (
        jnp.arange(tokens_dev, dtype=jnp.int32)[:, None]
        <= jnp.arange(tokens_dev, dtype=jnp.int32)[None, :]
    ).astype(BF16)
    order = dot("st,tu->su", marks, upper) - 1.0
    slots = jnp.arange(capacity, dtype=jnp.int32).astype(F32)
    hit = (order[:, None, :] == slots[None, :, None]) & routed_here[:, None, :]
    picker = hit.astype(BF16)
    slot_weight = jnp.sum(jnp.where(hit, token_weight[:, None, :], 0.0), axis=2).reshape(
        ne * capacity, 1
    )

    def pick(blocks):
        return dot("srt,std->srd", picker, blocks).reshape(ne * capacity, width)

    def unpick(rows):
        return dot("srt,srd->std", picker, rows.reshape(ne, capacity, width)).astype(BF16)

    rows_in = pick(tokens_all).astype(BF16)
    gate_pre = dot("rd,df->rf", rows_in, gate_rows)
    up_pre = dot("rd,df->rf", rows_in, up_rows)
    hidden = (jax.nn.silu(gate_pre) * up_pre).astype(BF16)
    result = (slot_weight * dot("rf,fd->rd", hidden, down_rows)).astype(BF16)
    routed_sum = line_scatter(unpick(result), 4)

    row_mixed = row_tokens(mixed_in)
    shared_pre = dot("td,kdf->ktf", row_mixed, shared_in)
    shared_hidden = (jax.nn.silu(shared_pre[0]) * shared_pre[1]).astype(BF16)
    shared_out = row_scatter(dot("tf,df->td", shared_hidden, shared_down))
    gate_value = jax.nn.sigmoid(
        jnp.sum(mixed_in.astype(F32) * gate_vector[None, :], axis=1)
    )

    block_total = residual + gate_value[:, None] * shared_out + routed_sum
    out_block = block_total.astype(BF16)[None]
    valid_mask = (own_segment < 2).astype(F32)
    valid_count = jnp.sum(lengths).astype(F32)
    dtotal = (
        total_tokens
        / valid_count
        * valid_mask[:, None]
        * (block_total - teacher[0].astype(F32))
    )

    dshared_out = (gate_value[:, None] * dtotal).astype(BF16)
    dlogit = jnp.sum(dtotal * shared_out, axis=1) * gate_value * (1.0 - gate_value)
    row_dout = row_tokens(dshared_out)
    shared_sigmoid = jax.nn.sigmoid(shared_pre[0])
    dshared_hidden = dot("td,df->tf", row_dout, shared_down)
    dshared_gate = (
        dshared_hidden * shared_pre[1] * shared_sigmoid * (1.0 + shared_pre[0] * (1.0 - shared_sigmoid))
    ).astype(BF16)
    dshared_up = (dshared_hidden * shared_pre[0] * shared_sigmoid).astype(BF16)
    dmixed_shared = row_scatter(
        dot("tf,df->td", dshared_gate, shared_in[0]) + dot("tf,df->td", dshared_up, shared_in[1])
    )

    def scatter_columns(term):
        return lax.psum_scatter(term.astype(BF16), "expert", scatter_dimension=0, tiled=True)

    grad_shared_down = scatter_columns(dot("td,tf->df", row_dout, shared_hidden))
    grad_shared_gates = scatter_columns(dot("td,tf->df", row_mixed, dshared_gate))
    grad_shared_ups = scatter_columns(dot("td,tf->df", row_mixed, dshared_up))

    dtotal_all = line_gather(dtotal.astype(BF16), ne, 5)
    dresult = (slot_weight * pick(dtotal_all)).astype(BF16)
    gate_sigmoid = jax.nn.sigmoid(gate_pre)
    activated = gate_pre * gate_sigmoid
    dhidden = dot("rd,fd->rf", dresult, down_rows)
    dgate = (dhidden * up_pre * gate_sigmoid * (1.0 + gate_pre * (1.0 - gate_sigmoid))).astype(BF16)
    dup = (dhidden * activated).astype(BF16)
    dreturn = (dot("rf,df->rd", dgate, gate_rows) + dot("rf,df->rd", dup, up_rows)).astype(BF16)
    grad_gate_term = dot("rd,rf->df", rows_in, dgate).astype(BF16)
    grad_up_term = dot("rd,rf->df", rows_in, dup).astype(BF16)
    grad_down_term = dot("rf,rd->fd", hidden, dresult).astype(BF16)
    dreturn, grad_gate_term, grad_up_term, grad_down_term = lax.optimization_barrier(
        (dreturn, grad_gate_term, grad_up_term, grad_down_term)
    )
    from_experts = line_scatter(unpick(dreturn), 6)
    grad_expert_down = scatter_shards(grad_down_term, f_index)[None]
    grad_expert_gate = scatter_shards(grad_gate_term, f_index)[None]
    grad_expert_up = scatter_shards(grad_up_term, f_index)[None]

    dmixed = dmixed_shared + dlogit[:, None] * gate_vector[None, :] + from_experts
    vector_term = jnp.sum(dlogit[:, None] * mixed_in.astype(F32), axis=0)
    dresidual_norm, second_gain_grad = norm_back(dmixed, residual, second_scale, second_gain)
    dresidual = dtotal + dresidual_norm
    dattn = dresidual.astype(BF16)
    row_dattn = row_tokens(dattn)

    dcontext = dot("td,dc->tc", row_dattn, mixer_out).astype(BF16)
    grad_mixer_out = scatter_columns(dot("td,tc->dc", row_dattn, context))
    dcontext = heads(dcontext)
    probabilities_again = jnp.exp(score() - log_total)
    dprobs = dot("qhd,khd->hqk", dcontext, values)
    delta_rows = jnp.sum(probabilities_again * dprobs, axis=2, keepdims=True)
    dscores = (probabilities_again * (dprobs - delta_rows)).astype(BF16)
    dqueries = dot("hqk,khd->qhd", dscores, keys) * score_factor
    dkeys = dot("hqk,qhd->khd", dscores, queries) * score_factor
    dvalues = dot("hqk,qhd->khd", probabilities_again.astype(BF16), dcontext)

    def back(incoming):
        return (incoming * cosine + turn_back(incoming * sine)).reshape(row_len, columns)

    dprojected = jnp.stack(
        [back(dqueries), back(dkeys), dvalues.reshape(row_len, columns)], axis=0
    ).astype(BF16)
    grad_mixer_in = lax.psum_scatter(
        dot("td,kte->kde", row_normed, dprojected).astype(BF16),
        "expert",
        scatter_dimension=1,
        tiled=True,
    )
    dnormed = row_scatter(dot("kte,kde->td", dprojected, mixer_in))
    dflat, first_gain_grad = norm_back(dnormed, flat_inputs, first_scale, first_gain)
    grad_input = (dresidual + dflat)[None]

    grad_mixer = jnp.concatenate([grad_mixer_in, grad_mixer_out[None]], axis=0)
    grad_mixer = jnp.transpose(grad_mixer, (1, 0, 2)).astype(F32)
    grad_shared = jnp.stack([grad_shared_gates, grad_shared_ups, grad_shared_down], axis=1)
    grad_shared = grad_shared.astype(F32)
    terms = jnp.stack([first_gain_grad, second_gain_grad, vector_term]).reshape(3, devices, piece)
    terms = jnp.pad(jnp.transpose(terms, (1, 0, 2)), ((0, 0), (0, 5), (0, 128 - piece)))
    sums = collect(terms)
    grad_gains = sums[:2, :piece]
    grad_shared_gate = sums[2, :piece]
    return (
        out_block,
        grad_input,
        grad_gains,
        grad_mixer,
        grad_shared,
        grad_shared_gate,
        grad_expert_gate,
        grad_expert_up,
        grad_expert_down,
    )


def solution(mesh):
    rows = P("expert", "fsdp", None)
    both = P(("fsdp", "expert"))
    gains = P(None, ("fsdp", "expert"))
    shared = P("expert", None, "fsdp")
    return jax.shard_map(
        on_device,
        mesh=mesh,
        in_specs=(rows, rows, P(), P(), rows, rows, gains, shared, shared, both, rows, rows, rows),
        out_specs=(rows, rows, gains, shared, shared, both, rows, rows, rows),
        check_vma=False,
    )
```

```python
import functools

import jax
import jax.numpy as jnp
from jax import lax
from jax.experimental import pallas as pl
from jax.experimental.pallas import tpu as pltpu
from jax.sharding import PartitionSpec as P

HD = 128
TOP = 4
THETA = 1000000.0
EPSILON = 1e-06
NEG_LARGE = -1e30
MESH = pl.DeviceIdType.MESH
WIRE = pl.CostEstimate(flops=0, bytes_accessed=120_000_000, transcendentals=0)
F32 = jnp.float32
BF16 = jnp.bfloat16


def turn(values):
    half = values.shape[-1] // 2
    return jnp.concatenate([-values[..., half:], values[..., :half]], axis=-1)


def turn_back(values):
    half = values.shape[-1] // 2
    return jnp.concatenate([values[..., half:], -values[..., :half]], axis=-1)


def norm_back(incoming, values, scale_rows, gain_row):
    unit_rows = values * scale_rows[:, None]
    gain_grad = jnp.sum(incoming * unit_rows, axis=0)
    dunit = incoming * gain_row[None, :]
    back_rows = scale_rows[:, None] * (
        dunit - unit_rows * jnp.mean(dunit * unit_rows, axis=1, keepdims=True)
    )
    return (back_rows, gain_grad)


def dot(form, left, right):
    return jnp.einsum(form, left, right, preferred_element_type=F32)


def swap_x(values):
    return lax.ppermute(values, "fsdp", [(0, 1), (1, 0), (2, 3), (3, 2)])


def swap_y(values):
    return lax.ppermute(values, "fsdp", [(0, 2), (2, 0), (1, 3), (3, 1)])


def gather_sides(block):
    return [swap_x(block), swap_y(block)]


def gather_rest(block, sides):
    half = block.shape[0] // 2
    return [block, *sides, swap_y(sides[0][:half]), swap_x(sides[1][half:])]


def scatter_corner(parts):
    half = parts[0].shape[0] // 2
    return [swap_x(parts[3][:half].astype(BF16)), swap_y(parts[3][half:].astype(BF16))]


def scatter_sides(parts, corner):
    half = parts[0].shape[0] // 2
    low, high = corner
    to_y = jnp.concatenate(
        [(parts[2][:half].astype(F32) + low.astype(F32)).astype(BF16), parts[2][half:].astype(BF16)]
    )
    to_x = jnp.concatenate(
        [parts[1][:half].astype(BF16), (parts[1][half:].astype(F32) + high.astype(F32)).astype(BF16)]
    )
    return [swap_x(to_x), swap_y(to_y)]


def scatter_end(parts, sides):
    return parts[0].astype(F32) + sides[0].astype(F32) + sides[1].astype(F32)


def square_scatter(parts):
    return scatter_end(parts, scatter_sides(parts, scatter_corner(parts)))


def row_tokens(block):
    return jnp.concatenate(gather_rest(block, gather_sides(block)), axis=0)


def row_scatter(product):
    quarter = product.shape[0] // 4
    return square_scatter([product[j * quarter : (j + 1) * quarter] for j in range(4)])


def gather_shards(shard, sides, index):
    rows = shard.shape[0]
    half = rows // 2
    own, from_x, from_y, low, high = gather_rest(shard, sides)
    whole = jnp.zeros((4 * rows,) + shard.shape[1:], shard.dtype)
    for piece, start in (
        (own, index * rows),
        (from_x, (index ^ 1) * rows),
        (from_y, (index ^ 2) * rows),
        (low, (index ^ 3) * rows),
        (high, (index ^ 3) * rows + half),
    ):
        whole = lax.dynamic_update_slice(whole, piece, (start, 0))
    return whole


def scatter_terms(whole, index):
    rows = whole.shape[0] // 4
    return [lax.dynamic_slice_in_dim(whole, (index ^ j) * rows, rows) for j in range(4)]


def opening_kernel(
    chips,
    x_ref, vector_ref, routed_ref, mixer_ref, gate_ref,
    gains_ref, tables_ref, row_ref, mixers_ref, last_ref, gates_ref,
    vectors, send_v, receive_v, send_t, receive_t,
    send_n, receive_n, send_g, receive_g,
    up_sem, down_sem, in_low, in_high, to_partner, in_partner, local,
):
    nf, ne = lax.axis_size("fsdp"), lax.axis_size("expert")
    total = nf * ne
    f, e = lax.axis_index("fsdp"), lax.axis_index("expert")
    me = f * ne + e
    z, c = e // 2, lax.rem(e, 2)
    xn, yn = f ^ 1, f ^ 2
    up = (f, jnp.minimum(z + 1, chips - 1) * 2 + c)
    down = (f, jnp.maximum(z - 1, 0) * 2 + c)
    partner = (f, z * 2 + 1 - c)
    parts = ((pl.ds(0, 3), mixers_ref), (pl.ds(3, 1), last_ref))
    own_gate = pltpu.make_async_copy(gate_ref, gates_ref.at[f], local.at[2])
    own_mixer = [
        pltpu.make_async_copy(mixer_ref.at[span], ref.at[:, e], local.at[k])
        for k, (span, ref) in enumerate(parts)
    ]
    for copy in own_mixer + [own_gate]:
        copy.start()
    barrier = pltpu.get_barrier_semaphore()

    def greet(step, carry):
        peer = lax.rem(me + step, total)
        pl.semaphore_signal(
            barrier, inc=1, device_id=(peer // ne, lax.rem(peer, ne)), device_id_type=MESH
        )
        return carry

    lax.fori_loop(1, total, greet, 0)
    pl.semaphore_wait(barrier, total - 1)

    def remote(source, target, send, receive, device):
        return pltpu.make_async_remote_copy(
            src_ref=source,
            dst_ref=target,
            send_sem=send,
            recv_sem=receive,
            device_id=device,
            device_id_type=MESH,
        )

    def vector_copy(slot, peer):
        return remote(
            vector_ref, vectors.at[slot], send_v.at[peer], receive_v.at[slot],
            (peer // ne, lax.rem(peer, ne)),
        )

    def table_copy(slot, peer):
        return remote(routed_ref, tables_ref.at[slot], send_t.at[peer], receive_t.at[slot], (f, peer))

    def start_vector(step, carry):
        vector_copy(me, lax.rem(me + step, total)).start()
        return carry

    def start_table(step, carry):
        table_copy(e, lax.rem(e + step, ne)).start()
        return carry

    lax.fori_loop(1, total, start_vector, 0)
    lax.fori_loop(1, ne, start_table, 0)
    vectors[me] = vector_ref[...]
    tables_ref[e] = routed_ref[...]

    def shard(k, origin, target, send, receive, own):
        span, ref = parts[k]
        place = ref.at[:, origin * 2 + c]
        return remote(mixer_ref.at[span] if own else place, place, send, receive, target)

    def upward(k, origin, r, own=False):
        return shard(k, origin, up, up_sem.at[k, r], in_low.at[k, r], own)

    def downward(k, origin, r, own=False):
        return shard(k, origin, down, down_sem.at[k, r], in_high.at[k, r], own)

    def across(k, origin, own=False):
        return shard(k, origin, partner, to_partner.at[k, origin], in_partner.at[k, origin], own)

    for k in (0, 1):

        @pl.when(z < chips - 1)
        def _():
            upward(k, z, 0, True).start()

        @pl.when(z > 0)
        def _():
            downward(k, z, 0, True).start()

        across(k, z, True).start()

    def end_vector(step, carry):
        peer = lax.rem(me + step, total)
        vector_copy(peer, peer).wait_recv()
        return carry

    lax.fori_loop(1, total, end_vector, 0)
    blocks = gains_ref.shape[1] // 128
    per = total // blocks
    for block in range(blocks):
        gains_ref[:, block * 128 : (block + 1) * 128] = jnp.sum(
            vectors[block * per : (block + 1) * per], axis=0
        )
    half = x_ref.shape[0] // 2
    low, high = pl.ds(0, half), pl.ds(half, half)

    def piece(index, ref, origin, rows, device, slot):
        send, receive = (send_n, receive_n) if index == 0 else (send_g, receive_g)
        here, there = (origin ^ f, origin ^ device) if index == 0 else (origin, origin)
        return remote(
            ref.at[here, rows], ref.at[there, rows], send.at[slot], receive.at[slot], (device, e)
        )

    def arrived(index, ref, origin, rows, slot):
        send, receive = (send_n, receive_n) if index == 0 else (send_g, receive_g)
        place = ref.at[origin ^ f if index == 0 else origin, rows]
        return remote(place, place, send.at[slot], receive.at[slot], (xn, e))

    def outgoing(index, ref, first, second):
        return [
            piece(index, ref, f, first, xn, 0),
            piece(index, ref, f, second, yn, 1),
            piece(index, ref, f, second, xn, 2),
            piece(index, ref, f, first, yn, 3),
        ]

    def relays(index, ref, first, second):
        return [piece(index, ref, xn, first, yn, 4), piece(index, ref, yn, second, xn, 5)]

    for rows in (low, high):
        values = x_ref[rows].astype(F32)
        scale = lax.rsqrt(jnp.mean(values * values, axis=1, keepdims=True) + EPSILON)
        row_ref[0, rows] = (values * scale * gains_ref[0:1]).astype(BF16)
    own_gate.wait()
    row_out = outgoing(0, row_ref, low, high)
    row_relay = relays(0, row_ref, low, high)
    depth = gate_ref.shape[0] // 2
    first, second = pl.ds(0, depth), pl.ds(depth, depth)
    gate_out = outgoing(1, gates_ref, first, second)
    gate_relay = relays(1, gates_ref, first, second)
    for copy in row_out + gate_out:
        copy.start()
    arrived(0, row_ref, xn, low, 0).wait_recv()
    row_relay[0].start()
    arrived(0, row_ref, yn, high, 1).wait_recv()
    row_relay[1].start()

    def hop(r, carry):
        before, after = z - r, z + r
        for k in (0, 1):

            @pl.when(before >= 0)
            def _():
                upward(k, before, r - 1).wait_recv()

                @pl.when(z < chips - 1)
                def _():
                    upward(k, before, r).start()

                across(k, before).start()

            @pl.when(after < chips)
            def _():
                downward(k, after, r - 1).wait_recv()

                @pl.when(z > 0)
                def _():
                    downward(k, after, r).start()

                across(k, after).start()

        return carry

    lax.fori_loop(1, 3, hop, 0)
    arrived(1, gates_ref, xn, first, 0).wait_recv()
    gate_relay[0].start()
    arrived(1, gates_ref, yn, second, 1).wait_recv()
    gate_relay[1].start()
    lax.fori_loop(3, chips, hop, 0)

    for index, ref, (one, two) in ((0, row_ref, (low, high)), (1, gates_ref, (first, second))):
        arrived(index, ref, xn, two, 2).wait_recv()
        arrived(index, ref, yn, one, 3).wait_recv()
        arrived(index, ref, f ^ 3, one, 4).wait_recv()
        arrived(index, ref, f ^ 3, two, 5).wait_recv()
    for copy in row_out + gate_out + row_relay + gate_relay:
        copy.wait_send()
    for k in (0, 1):
        own_mixer[k].wait()

        @pl.when(z < chips - 1)
        def _():
            upward(k, z, 0, True).wait_send()

        @pl.when(z > 0)
        def _():
            downward(k, z, 0, True).wait_send()

    def finish(r, carry):
        before, after = z - r, z + r
        for k in (0, 1):

            @pl.when((before >= 0) & (z < chips - 1))
            def _():
                upward(k, before, r).wait_send()

            @pl.when((after < chips) & (z > 0))
            def _():
                downward(k, after, r).wait_send()

        return carry

    lax.fori_loop(1, chips, finish, 0)

    def shared(origin, carry):
        for k in (0, 1):
            across(k, origin).wait_send()
            across(k, origin).wait_recv()
        return carry

    lax.fori_loop(0, chips, shared, 0)

    def sent_vector(step, carry):
        peer = lax.rem(me + step, total)
        vector_copy(peer, peer).wait_send()
        return carry

    def end_table(step, carry):
        peer = lax.rem(e + step, ne)
        copy = table_copy(peer, peer)
        copy.wait_recv()
        copy.wait_send()
        return carry

    lax.fori_loop(1, total, sent_vector, 0)
    lax.fori_loop(1, ne, end_table, 0)


def opening(x, vector, routed, mixer, gate, nf):
    ne = routed.shape[0]
    chips, devices = ne // 2, nf * ne
    whole = pl.BlockSpec(memory_space=pltpu.VMEM)
    far = pl.BlockSpec(memory_space=pl.ANY)
    dma = pltpu.SemaphoreType.DMA
    return pl.pallas_call(
        functools.partial(opening_kernel, chips),
        out_shape=[
            jax.ShapeDtypeStruct((8, x.shape[1]), F32),
            jax.ShapeDtypeStruct((ne,) + routed.shape, F32),
            jax.ShapeDtypeStruct((nf,) + x.shape, BF16),
            jax.ShapeDtypeStruct((3, ne) + mixer.shape[1:], BF16),
            jax.ShapeDtypeStruct((1, ne) + mixer.shape[1:], BF16),
            jax.ShapeDtypeStruct((nf,) + gate.shape, BF16),
        ],
        in_specs=[whole] * 5,
        out_specs=[whole, whole, whole, far, far, far],
        scratch_shapes=[pltpu.VMEM((devices,) + vector.shape, F32)]
        + [dma((devices,))] * 2
        + [dma((ne,))] * 2
        + [dma((6,))] * 4
        + [dma((2, chips))] * 6
        + [dma((3,))],
        compiler_params=pltpu.CompilerParams(
            collective_id=1, has_side_effects=True, vmem_limit_bytes=24 * 1024 * 1024
        ),
        name="opening",
    )(x, vector, routed, mixer, gate)


def collect_kernel(terms_ref, sum_ref, arrived, send, receive):
    nf, ne = lax.axis_size("fsdp"), lax.axis_size("expert")
    total = nf * ne
    me = lax.axis_index("fsdp") * ne + lax.axis_index("expert")
    barrier = pltpu.get_barrier_semaphore()

    def greet(step, carry):
        peer = lax.rem(me + step, total)
        pl.semaphore_signal(
            barrier, inc=1, device_id=(peer // ne, lax.rem(peer, ne)), device_id_type=MESH
        )
        return carry

    lax.fori_loop(1, total, greet, 0)
    pl.semaphore_wait(barrier, total - 1)

    def copy_of(slot, peer):
        return pltpu.make_async_remote_copy(
            src_ref=terms_ref.at[peer],
            dst_ref=arrived.at[slot],
            send_sem=send.at[peer],
            recv_sem=receive.at[slot],
            device_id=(peer // ne, lax.rem(peer, ne)),
            device_id_type=MESH,
        )

    def begin(step, carry):
        copy_of(me, lax.rem(me + step, total)).start()
        return carry

    lax.fori_loop(1, total, begin, 0)
    arrived[me] = terms_ref[me]

    def end(step, carry):
        peer = lax.rem(me + step, total)
        copy = copy_of(peer, peer)
        copy.wait_recv()
        copy.wait_send()
        return carry

    lax.fori_loop(1, total, end, 0)
    sum_ref[...] = jnp.sum(arrived[...], axis=0)


def collect(terms):
    devices = terms.shape[0]
    return pl.pallas_call(
        collect_kernel,
        out_shape=jax.ShapeDtypeStruct(terms.shape[1:], terms.dtype),
        in_specs=[pl.BlockSpec(memory_space=pltpu.VMEM)],
        out_specs=pl.BlockSpec(memory_space=pltpu.VMEM),
        scratch_shapes=[pltpu.VMEM(terms.shape, terms.dtype)]
        + [pltpu.SemaphoreType.DMA((devices,))] * 2,
        compiler_params=pltpu.CompilerParams(collective_id=2, has_side_effects=True),
        name="collect",
    )(terms)


def places(chips):
    f, e = lax.axis_index("fsdp"), lax.axis_index("expert")
    z, c = e // 2, lax.rem(e, 2)
    up = (f, jnp.minimum(z + 1, chips - 1) * 2 + c)
    down = (f, jnp.maximum(z - 1, 0) * 2 + c)
    return f, e, z, c, up, down, (f, z * 2 + 1 - c), (f ^ 1, e), (f ^ 2, e)


def meet(chips, z, up, down, others):
    barrier = pltpu.get_barrier_semaphore()
    for peer in others:
        pl.semaphore_signal(barrier, inc=1, device_id=peer, device_id_type=MESH)

    @pl.when(z < chips - 1)
    def _():
        pl.semaphore_signal(barrier, inc=1, device_id=up, device_id_type=MESH)

    @pl.when(z > 0)
    def _():
        pl.semaphore_signal(barrier, inc=1, device_id=down, device_id_type=MESH)

    known = len(others) + jnp.where(z < chips - 1, 1, 0) + jnp.where(z > 0, 1, 0)
    pl.semaphore_wait(barrier, known)


def remote_copy(source, target, send, receive, device):
    return pltpu.make_async_remote_copy(
        src_ref=source,
        dst_ref=target,
        send_sem=send,
        recv_sem=receive,
        device_id=device,
        device_id_type=MESH,
    )


def spread_kernel(
    chips, block_ref, tokens_ref, all_ref, row_ref,
    up_sem, down_sem, in_low, in_high, to_partner, in_partner, send_n, receive_n, local,
):
    f, e, z, c, up, down, partner, side_x, side_y = places(chips)
    xn, yn = f ^ 1, f ^ 2
    own = [
        pltpu.make_async_copy(block_ref, all_ref.at[e], local.at[0]),
        pltpu.make_async_copy(tokens_ref, row_ref.at[0], local.at[1]),
    ]
    for copy in own:
        copy.start()
    meet(chips, z, up, down, (partner, side_x, side_y))

    def shard(origin, target, send, receive, first):
        place = all_ref.at[origin * 2 + c]
        return remote_copy(block_ref if first else place, place, send, receive, target)

    def upward(origin, r, first=False):
        return shard(origin, up, up_sem.at[r], in_low.at[r], first)

    def downward(origin, r, first=False):
        return shard(origin, down, down_sem.at[r], in_high.at[r], first)

    def across(origin, first=False):
        return shard(origin, partner, to_partner.at[origin], in_partner.at[origin], first)

    @pl.when(z < chips - 1)
    def _():
        upward(z, 0, True).start()

    @pl.when(z > 0)
    def _():
        downward(z, 0, True).start()

    across(z, True).start()
    half = tokens_ref.shape[0] // 2
    low, high = pl.ds(0, half), pl.ds(half, half)

    def piece(origin, rows, device, slot):
        source = tokens_ref.at[rows] if slot < 4 else row_ref.at[origin ^ f, rows]
        return remote_copy(
            source, row_ref.at[origin ^ device, rows], send_n.at[slot], receive_n.at[slot], (device, e)
        )

    def arrived(origin, rows, slot):
        place = row_ref.at[origin ^ f, rows]
        return remote_copy(place, place, send_n.at[slot], receive_n.at[slot], side_x)

    copies = [piece(f, low, xn, 0), piece(f, high, yn, 1), piece(f, high, xn, 2), piece(f, low, yn, 3)]
    relays = [piece(xn, low, yn, 4), piece(yn, high, xn, 5)]
    for copy in copies:
        copy.start()
    arrived(xn, low, 0).wait_recv()
    relays[0].start()
    arrived(yn, high, 1).wait_recv()
    relays[1].start()

    def hop(r, carry):
        before, after = z - r, z + r

        @pl.when(before >= 0)
        def _():
            upward(before, r - 1).wait_recv()

            @pl.when(z < chips - 1)
            def _():
                upward(before, r).start()

            across(before).start()

        @pl.when(after < chips)
        def _():
            downward(after, r - 1).wait_recv()

            @pl.when(z > 0)
            def _():
                downward(after, r).start()

            across(after).start()

        return carry

    lax.fori_loop(1, chips, hop, 0)
    arrived(xn, high, 2).wait_recv()
    arrived(yn, low, 3).wait_recv()
    arrived(f ^ 3, low, 4).wait_recv()
    arrived(f ^ 3, high, 5).wait_recv()
    for copy in copies + relays:
        copy.wait_send()
    for copy in own:
        copy.wait()

    @pl.when(z < chips - 1)
    def _():
        upward(z, 0, True).wait_send()

    @pl.when(z > 0)
    def _():
        downward(z, 0, True).wait_send()

    def finish(r, carry):
        before, after = z - r, z + r

        @pl.when((before >= 0) & (z < chips - 1))
        def _():
            upward(before, r).wait_send()

        @pl.when((after < chips) & (z > 0))
        def _():
            downward(after, r).wait_send()

        return carry

    lax.fori_loop(1, chips, finish, 0)

    def shared(origin, carry):
        across(origin).wait_send()
        across(origin).wait_recv()
        return carry

    lax.fori_loop(0, chips, shared, 0)


def spread(block, tokens, nf, ne, cid):
    chips = ne // 2
    dma = pltpu.SemaphoreType.DMA
    return pl.pallas_call(
        functools.partial(spread_kernel, chips),
        out_shape=[
            jax.ShapeDtypeStruct((ne,) + block.shape, block.dtype),
            jax.ShapeDtypeStruct((nf,) + tokens.shape, tokens.dtype),
        ],
        in_specs=[pl.BlockSpec(memory_space=pltpu.VMEM)] * 2,
        out_specs=[pl.BlockSpec(memory_space=pltpu.VMEM)] * 2,
        scratch_shapes=[dma((chips,))] * 6 + [dma((6,))] * 2 + [dma((2,))],
        compiler_params=pltpu.CompilerParams(
            collective_id=cid, has_side_effects=True, vmem_limit_bytes=40 * 1024 * 1024
        ),
        cost_estimate=WIRE,
        name=f"spread{cid}",
    )(block, tokens)


def combine_kernel(
    chips, terms_ref, parts_ref, sum_ref, row_sum_ref,
    theirs, going, coming, corner, onward, from_side,
    up_sem, down_sem, in_low, in_high, to_partner, in_partner, send_n, receive_n,
):
    f, e, z, c, up, down, partner, side_x, side_y = places(chips)
    meet(chips, z, up, down, (partner, side_x, side_y))

    def across(target):
        return remote_copy(
            terms_ref.at[target * 2 + 1 - c], theirs.at[target],
            to_partner.at[target], in_partner.at[target], partner,
        )

    def upward(target):
        return remote_copy(
            going.at[target], coming.at[target], up_sem.at[target], in_low.at[target], up
        )

    def downward(target, receiver):
        place = coming.at[jnp.where(target == receiver, chips, target)]
        return remote_copy(
            going.at[target], place, down_sem.at[target], in_high.at[target], down
        )

    def offer(r, carry):
        across(r).start()
        across(chips - 1 - r).start()
        return carry

    lax.fori_loop(0, chips // 2, offer, 0)
    half = parts_ref.shape[1] // 2
    low, high = pl.ds(0, half), pl.ds(half, half)

    def side(slot, source, target, device):
        return remote_copy(source, target, send_n.at[slot], receive_n.at[slot], device)

    copies = [
        side(0, parts_ref.at[3, low], corner.at[0], side_x),
        side(1, parts_ref.at[3, high], corner.at[1], side_y),
        side(2, parts_ref.at[1, low], from_side.at[0, low], side_x),
        side(3, parts_ref.at[2, high], from_side.at[1, high], side_y),
        side(4, onward.at[0], from_side.at[0, high], side_x),
        side(5, onward.at[1], from_side.at[1, low], side_y),
    ]
    for copy in copies[:4]:
        copy.start()

    def chip_term(target):
        return terms_ref[target * 2 + c].astype(F32) + theirs[target].astype(F32)

    def rise(r):
        target = chips - 1 - r

        @pl.when(target > z)
        def _():
            across(target).wait_recv()

            @pl.when(z > 0)
            def _():
                upward(target).wait_recv()
                going[target] = (chip_term(target) + coming[target].astype(F32)).astype(BF16)

            @pl.when(z == 0)
            def _():
                going[target] = chip_term(target).astype(BF16)

            upward(target).start()

    def fall(r):
        @pl.when(r < z)
        def _():
            across(r).wait_recv()

            @pl.when(z < chips - 1)
            def _():
                downward(r, z).wait_recv()
                going[r] = (chip_term(r) + coming[r].astype(F32)).astype(BF16)

            @pl.when(z == chips - 1)
            def _():
                going[r] = chip_term(r).astype(BF16)

            downward(r, z - 1).start()

    def pass_on(r, carry):
        @pl.when(z < chips // 2)
        def _():
            rise(r)

        fall(r)

        @pl.when(z >= chips // 2)
        def _():
            rise(r)

        return carry

    lax.fori_loop(0, 1, pass_on, 0)
    copies[1].wait_recv()
    onward[0] = (parts_ref[1, high].astype(F32) + corner[1].astype(F32)).astype(BF16)
    copies[4].start()
    copies[0].wait_recv()
    onward[1] = (parts_ref[2, low].astype(F32) + corner[0].astype(F32)).astype(BF16)
    copies[5].start()
    lax.fori_loop(1, chips, pass_on, 0)
    for copy in copies[2:]:
        copy.wait_recv()
    row_sum_ref[...] = (
        parts_ref[0].astype(F32) + from_side[0].astype(F32) + from_side[1].astype(F32)
    )
    across(z).wait_recv()
    sum_ref[...] = chip_term(z)

    @pl.when(z > 0)
    def _():
        upward(z).wait_recv()
        sum_ref[...] += coming[z].astype(F32)

    @pl.when(z < chips - 1)
    def _():
        downward(z, z).wait_recv()
        sum_ref[...] += coming[chips].astype(F32)

    for copy in copies:
        copy.wait_send()

    def finish(target, carry):
        across(target).wait_send()

        @pl.when(target > z)
        def _():
            upward(target).wait_send()

        @pl.when(target < z)
        def _():
            downward(target, z - 1).wait_send()

        return carry

    lax.fori_loop(0, chips, finish, 0)


def combine(terms, parts, cid):
    ne = terms.shape[0]
    chips = ne // 2
    parts = parts.reshape(4, parts.shape[0] // 4, parts.shape[1])
    block = terms.shape[1:]
    halves = (2, parts.shape[1] // 2, parts.shape[2])
    sides = (2,) + parts.shape[1:]
    dma = pltpu.SemaphoreType.DMA
    return pl.pallas_call(
        functools.partial(combine_kernel, chips),
        out_shape=[
            jax.ShapeDtypeStruct(terms.shape[1:], F32),
            jax.ShapeDtypeStruct(parts.shape[1:], F32),
        ],
        in_specs=[pl.BlockSpec(memory_space=pltpu.VMEM)] * 2,
        out_specs=[pl.BlockSpec(memory_space=pltpu.VMEM)] * 2,
        scratch_shapes=[pltpu.VMEM((chips,) + block, BF16)] * 2
        + [pltpu.VMEM((chips + 1,) + block, BF16)]
        + [pltpu.VMEM(halves, BF16)] * 2
        + [pltpu.VMEM(sides, BF16)]
        + [dma((chips,))] * 6
        + [dma((6,))] * 2,
        compiler_params=pltpu.CompilerParams(
            collective_id=cid, has_side_effects=True, vmem_limit_bytes=60 * 1024 * 1024
        ),
        cost_estimate=WIRE,
        name=f"combine{cid}",
    )(terms, parts)


def on_device(
    inputs,
    teacher,
    lengths,
    deal_order,
    routes,
    route_weights,
    norm_gains,
    mixer_weights,
    shared_weights,
    shared_gate,
    expert_gate,
    expert_up,
    expert_down,
):
    tokens_dev = inputs.shape[1]
    width = inputs.shape[2]
    nf = lax.axis_size("fsdp")
    ne = lax.axis_size("expert")
    devices = nf * ne
    row_len = tokens_dev * nf
    capacity = 3 * tokens_dev * TOP // (2 * ne)
    total_tokens = row_len * ne
    columns = mixer_weights.shape[2]
    heads_local = columns // HD
    f_index = lax.axis_index("fsdp")
    e_index = lax.axis_index("expert")

    piece = norm_gains.shape[1]
    slot = (f_index * ne + e_index) % (128 // piece)
    vector = jnp.concatenate([norm_gains, shared_gate[None]], axis=0).astype(F32)
    vector = lax.dynamic_update_slice(jnp.zeros((8, 128), F32), vector, (0, slot * piece))
    chosen = routes[0]
    weights_route = route_weights[0]
    expert_ids = jnp.arange(ne, dtype=jnp.int32)
    routed = jnp.sum(
        jnp.where(chosen.T[None] == expert_ids[:, None, None], weights_route.T[None], 0.0), axis=1
    )
    mixer_shard = jnp.transpose(mixer_weights, (1, 0, 2))
    gains, tables, row_blocks, mixer_in, mixer_out, gates = opening(
        inputs[0], vector, routed, mixer_shard, expert_gate[0], nf
    )
    first_gain, second_gain, gate_vector = gains[0], gains[1], gains[2]
    token_weight = lax.dynamic_index_in_dim(tables, e_index, axis=1, keepdims=False)
    mixer_in = mixer_in.reshape(3, width, columns)
    mixer_out = mixer_out.reshape(width, columns)
    gate_rows = gates.reshape(width, gates.shape[2])
    row_normed = row_blocks.reshape(row_len, width)

    shared_shard, up_shard, down_shard, gains = lax.optimization_barrier(
        (shared_weights, expert_up[0], expert_down[0], gains)
    )
    shared_shard = jnp.transpose(shared_shard, (1, 0, 2))
    shared_first = lax.all_gather(shared_shard[0], "expert", axis=0, tiled=True)
    up_sides = gather_sides(up_shard)

    first_len = lengths[deal_order[2 * e_index]]
    second_len = lengths[deal_order[2 * e_index + 1]]
    row_places = (
        (f_index ^ jnp.arange(nf, dtype=jnp.int32))[:, None] * tokens_dev
        + jnp.arange(tokens_dev, dtype=jnp.int32)[None]
    ).reshape(row_len)
    row_segment = (row_places >= first_len).astype(jnp.int32) + (
        row_places >= first_len + second_len
    ).astype(jnp.int32)
    row_position = (
        row_places
        - first_len * (row_segment >= 1).astype(jnp.int32)
        - second_len * (row_segment >= 2).astype(jnp.int32)
    )
    own_segment = row_segment[:tokens_dev]
    allowed = (row_segment[:, None] == row_segment[None, :]) & (
        row_places[None, :] <= row_places[:, None]
    )
    inverse = THETA ** (-(jnp.arange(HD // 2, dtype=F32) * 2.0) / HD)
    angles = row_position.astype(F32)[:, None] * inverse[None, :]
    cosine = jnp.concatenate([jnp.cos(angles)] * 2, axis=1)[:, None, :]
    sine = jnp.concatenate([jnp.sin(angles)] * 2, axis=1)[:, None, :]

    flat_inputs = inputs[0].astype(F32)
    first_scale = lax.rsqrt(jnp.mean(flat_inputs * flat_inputs, axis=1) + EPSILON)
    projected = dot("td,kde->kte", row_normed, mixer_in)

    def heads(values):
        return values.reshape(row_len, heads_local, HD)

    raw_query, raw_key = heads(projected[0]), heads(projected[1])
    queries = (raw_query * cosine + turn(raw_query) * sine).astype(BF16)
    keys = (raw_key * cosine + turn(raw_key) * sine).astype(BF16)
    values = heads(projected[2].astype(BF16))
    score_factor = HD ** (-0.5)

    def score():
        raw = dot("qhd,khd->hqk", queries, keys)
        return jnp.where(allowed[None], raw * score_factor, NEG_LARGE)

    scores = score()
    top_score = jnp.max(scores, axis=2, keepdims=True)
    shifted = jnp.exp(scores - top_score)
    row_total = jnp.sum(shifted, axis=2, keepdims=True)
    probabilities = shifted / row_total
    log_total = top_score + jnp.log(row_total)
    context = dot("hqk,khd->qhd", probabilities.astype(BF16), values)
    context = context.reshape(row_len, columns).astype(BF16)
    attn_out = row_scatter(dot("tc,dc->td", context, mixer_out))
    residual = flat_inputs + attn_out
    second_scale = lax.rsqrt(jnp.mean(residual * residual, axis=1) + EPSILON)
    mixed_in = (residual * second_scale[:, None] * second_gain[None, :]).astype(BF16)

    down_shard, mixed_in = lax.optimization_barrier((down_shard, mixed_in))
    up_rows = gather_shards(up_shard, up_sides, f_index)
    down_rows = gather_shards(down_shard, gather_sides(down_shard), f_index)
    tokens_all, row_mixed = spread(mixed_in, mixed_in, nf, ne, 3)
    row_mixed = row_mixed.reshape(row_len, width)
    second_shard, third_shard, tokens_all = lax.optimization_barrier(
        (shared_shard[1], shared_shard[2], tokens_all)
    )
    shared_second = lax.all_gather(second_shard, "expert", axis=0, tiled=True)
    shared_down = lax.all_gather(third_shard, "expert", axis=0, tiled=True)
    routed_here = token_weight > 0.0
    marks = routed_here.astype(BF16)
    upper = (
        jnp.arange(tokens_dev, dtype=jnp.int32)[:, None]
        <= jnp.arange(tokens_dev, dtype=jnp.int32)[None, :]
    ).astype(BF16)
    order = dot("st,tu->su", marks, upper) - 1.0
    slots = jnp.arange(capacity, dtype=jnp.int32).astype(F32)
    hit = (order[:, None, :] == slots[None, :, None]) & routed_here[:, None, :]
    picker = hit.astype(BF16)
    slot_weight = jnp.sum(jnp.where(hit, token_weight[:, None, :], 0.0), axis=2).reshape(
        ne * capacity, 1
    )

    def pick(blocks):
        return dot("srt,std->srd", picker, blocks).reshape(ne * capacity, width)

    def unpick(rows):
        return dot("srt,srd->std", picker, rows.reshape(ne, capacity, width)).astype(BF16)

    rows_in = pick(tokens_all).astype(BF16)
    gate_pre = dot("rd,df->rf", rows_in, gate_rows)
    up_pre = dot("rd,df->rf", rows_in, up_rows)
    hidden = (jax.nn.silu(gate_pre) * up_pre).astype(BF16)
    result = (slot_weight * dot("rf,fd->rd", hidden, down_rows)).astype(BF16)

    shared_pre = (dot("td,df->tf", row_mixed, shared_first), dot("td,df->tf", row_mixed, shared_second))
    shared_hidden = (jax.nn.silu(shared_pre[0]) * shared_pre[1]).astype(BF16)
    routed_sum, shared_out = combine(
        unpick(result), dot("tf,df->td", shared_hidden, shared_down).astype(BF16), 4
    )
    gate_value = jax.nn.sigmoid(
        jnp.sum(mixed_in.astype(F32) * gate_vector[None, :], axis=1)
    )

    block_total = residual + gate_value[:, None] * shared_out + routed_sum
    out_block = block_total.astype(BF16)[None]
    valid_mask = (own_segment < 2).astype(F32)
    valid_count = jnp.sum(lengths).astype(F32)
    dtotal = (
        total_tokens
        / valid_count
        * valid_mask[:, None]
        * (block_total - teacher[0].astype(F32))
    )

    dshared_out = (gate_value[:, None] * dtotal).astype(BF16)
    dlogit = jnp.sum(dtotal * shared_out, axis=1) * gate_value * (1.0 - gate_value)
    dtotal_all, row_dout = spread(dtotal.astype(BF16), dshared_out, nf, ne, 5)
    row_dout = row_dout.reshape(row_len, width)
    down_term = dot("td,tf->df", row_dout, shared_hidden).astype(BF16)
    row_dout, dtotal_all, down_term = lax.optimization_barrier((row_dout, dtotal_all, down_term))
    shared_sigmoid = jax.nn.sigmoid(shared_pre[0])
    dshared_hidden = dot("td,df->tf", row_dout, shared_down)
    dshared_gate = (
        dshared_hidden * shared_pre[1] * shared_sigmoid * (1.0 + shared_pre[0] * (1.0 - shared_sigmoid))
    ).astype(BF16)
    dshared_up = (dshared_hidden * shared_pre[0] * shared_sigmoid).astype(BF16)
    dmixed_terms = (
        dot("tf,df->td", dshared_gate, shared_first) + dot("tf,df->td", dshared_up, shared_second)
    ).astype(BF16)

    def scatter_columns(term):
        return lax.psum_scatter(term.astype(BF16), "expert", scatter_dimension=0, tiled=True)

    grad_shared_down = scatter_columns(down_term)
    gate_term = dot("td,tf->df", row_mixed, dshared_gate).astype(BF16)
    up_term = dot("td,tf->df", row_mixed, dshared_up).astype(BF16)

    dresult = (slot_weight * pick(dtotal_all)).astype(BF16)
    gate_sigmoid = jax.nn.sigmoid(gate_pre)
    activated = gate_pre * gate_sigmoid
    dhidden = dot("rd,fd->rf", dresult, down_rows)
    dgate = (dhidden * up_pre * gate_sigmoid * (1.0 + gate_pre * (1.0 - gate_sigmoid))).astype(BF16)
    dup = (dhidden * activated).astype(BF16)
    dreturn = (dot("rf,df->rd", dgate, gate_rows) + dot("rf,df->rd", dup, up_rows)).astype(BF16)
    grad_gate_term = dot("rd,rf->df", rows_in, dgate).astype(BF16)
    grad_down_term = dot("rf,rd->fd", hidden, dresult).astype(BF16)
    terms = [scatter_terms(term, f_index) for term in (grad_down_term, grad_gate_term)]
    corners = [scatter_corner(terms[0])]
    dreturned, up_term, gate_term, terms, corners = lax.optimization_barrier(
        (unpick(dreturn), up_term, gate_term, terms, corners)
    )
    grad_shared_gates = scatter_columns(gate_term)
    corners.append(scatter_corner(terms[1]))
    sides = [scatter_sides(terms[0], corners[0])]
    from_experts, dmixed_shared = combine(dreturned, dmixed_terms, 6)
    from_experts, up_term, corners, sides, grad_shared_down = lax.optimization_barrier(
        (from_experts, up_term, corners, sides, grad_shared_down)
    )
    grad_shared_ups = scatter_columns(up_term)

    dmixed = dmixed_shared + dlogit[:, None] * gate_vector[None, :] + from_experts
    vector_term = jnp.sum(dlogit[:, None] * mixed_in.astype(F32), axis=0)
    dresidual_norm, second_gain_grad = norm_back(dmixed, residual, second_scale, second_gain)
    dresidual = dtotal + dresidual_norm
    dattn = dresidual.astype(BF16)
    dattn, rows_again, dup = lax.optimization_barrier((dattn, rows_in, dup))
    row_dattn = row_tokens(dattn)
    grad_up_term = dot("rd,rf->df", rows_again, dup).astype(BF16)
    row_dattn, corners, grad_up_term, grad_shared_gates = lax.optimization_barrier(
        (row_dattn, corners, grad_up_term, grad_shared_gates)
    )
    sides.append(scatter_sides(terms[1], corners[1]))
    terms.append(scatter_terms(grad_up_term, f_index))
    corners.append(scatter_corner(terms[2]))

    dcontext = dot("td,dc->tc", row_dattn, mixer_out).astype(BF16)
    mixer_out_term = dot("td,tc->dc", row_dattn, context).astype(BF16)
    dcontext, mixer_out_term, sides = lax.optimization_barrier((dcontext, mixer_out_term, sides))
    dcontext = heads(dcontext)
    probabilities_again = jnp.exp(score() - log_total)
    dprobs = dot("qhd,khd->hqk", dcontext, values)
    delta_rows = jnp.sum(probabilities_again * dprobs, axis=2, keepdims=True)
    dscores = (probabilities_again * (dprobs - delta_rows)).astype(BF16)
    dqueries = dot("hqk,khd->qhd", dscores, keys) * score_factor
    dkeys = dot("hqk,qhd->khd", dscores, queries) * score_factor
    dvalues = dot("hqk,qhd->khd", probabilities_again.astype(BF16), dcontext)

    def back(incoming):
        return (incoming * cosine + turn_back(incoming * sine)).reshape(row_len, columns)

    dprojected = jnp.stack(
        [back(dqueries), back(dkeys), dvalues.reshape(row_len, columns)], axis=0
    ).astype(BF16)
    dprojected, grad_shared_ups, corners[2] = lax.optimization_barrier(
        (dprojected, grad_shared_ups, corners[2])
    )
    sides.append(scatter_sides(terms[2], corners[2]))
    mixer_term = dot("td,kte->kde", row_normed, dprojected).astype(BF16)
    mixer_term = jnp.concatenate([mixer_term, mixer_out_term[None]], axis=0)
    grad_mixer = lax.psum_scatter(mixer_term, "expert", scatter_dimension=1, tiled=True)
    dnormed = dot("kte,kde->td", dprojected, mixer_in).astype(BF16)
    dnormed, sides[2] = lax.optimization_barrier((row_scatter(dnormed), sides[2]))
    grad_expert_down, grad_expert_gate, grad_expert_up = [
        scatter_end(parts, side)[None] for parts, side in zip(terms, sides)
    ]
    dflat, first_gain_grad = norm_back(dnormed, flat_inputs, first_scale, first_gain)
    grad_input = (dresidual + dflat)[None]

    grad_shared = jnp.stack([grad_shared_gates, grad_shared_ups, grad_shared_down], axis=1)
    grad_shared = grad_shared.astype(F32)
    terms = jnp.stack([first_gain_grad, second_gain_grad, vector_term]).reshape(3, devices, piece)
    terms = jnp.pad(jnp.transpose(terms, (1, 0, 2)), ((0, 0), (0, 5), (0, 128 - piece)))
    sums = collect(terms)
    (grad_mixer, sums, grad_shared, grad_expert_down, grad_expert_gate, grad_expert_up) = (
        lax.optimization_barrier(
            (grad_mixer, sums, grad_shared, grad_expert_down, grad_expert_gate, grad_expert_up)
        )
    )
    grad_mixer = jnp.transpose(grad_mixer, (1, 0, 2)).astype(F32)
    grad_gains = sums[:2, :piece]
    grad_shared_gate = sums[2, :piece]
    return (
        out_block,
        grad_input,
        grad_gains,
        grad_mixer,
        grad_shared,
        grad_shared_gate,
        grad_expert_gate,
        grad_expert_up,
        grad_expert_down,
    )


def solution(mesh):
    rows = P("expert", "fsdp", None)
    both = P(("fsdp", "expert"))
    gains = P(None, ("fsdp", "expert"))
    shared = P("expert", None, "fsdp")
    return jax.shard_map(
        on_device,
        mesh=mesh,
        in_specs=(rows, rows, P(), P(), rows, rows, gains, shared, shared, both, rows, rows, rows),
        out_specs=(rows, rows, gains, shared, shared, both, rows, rows, rows),
        check_vma=False,
    )
```

```python
import functools

import jax
import jax.numpy as jnp
from jax import lax
from jax.experimental import pallas as pl
from jax.experimental.pallas import tpu as pltpu
from jax.sharding import PartitionSpec as P

HD = 128
TOP = 4
THETA = 1000000.0
EPSILON = 1e-06
NEG_LARGE = -1e30
MESH = pl.DeviceIdType.MESH
WIRE = pl.CostEstimate(flops=0, bytes_accessed=120_000_000, transcendentals=0)
F32 = jnp.float32
BF16 = jnp.bfloat16


def turn(values):
    half = values.shape[-1] // 2
    return jnp.concatenate([-values[..., half:], values[..., :half]], axis=-1)


def turn_back(values):
    half = values.shape[-1] // 2
    return jnp.concatenate([values[..., half:], -values[..., :half]], axis=-1)


def norm_back(incoming, values, scale_rows, gain_row):
    unit_rows = values * scale_rows[:, None]
    gain_grad = jnp.sum(incoming * unit_rows, axis=0)
    dunit = incoming * gain_row[None, :]
    back_rows = scale_rows[:, None] * (
        dunit - unit_rows * jnp.mean(dunit * unit_rows, axis=1, keepdims=True)
    )
    return (back_rows, gain_grad)


def dot(form, left, right):
    return jnp.einsum(form, left, right, preferred_element_type=F32)


def swap_x(values):
    return lax.ppermute(values, "fsdp", [(0, 1), (1, 0), (2, 3), (3, 2)])


def swap_y(values):
    return lax.ppermute(values, "fsdp", [(0, 2), (2, 0), (1, 3), (3, 1)])


def gather_sides(block):
    return [swap_x(block), swap_y(block)]


def gather_rest(block, sides):
    half = block.shape[0] // 2
    return [block, *sides, swap_y(sides[0][:half]), swap_x(sides[1][half:])]


def scatter_corner(parts):
    half = parts[0].shape[0] // 2
    return [swap_x(parts[3][:half].astype(BF16)), swap_y(parts[3][half:].astype(BF16))]


def scatter_sides(parts, corner):
    half = parts[0].shape[0] // 2
    low, high = corner
    to_y = jnp.concatenate(
        [(parts[2][:half].astype(F32) + low.astype(F32)).astype(BF16), parts[2][half:].astype(BF16)]
    )
    to_x = jnp.concatenate(
        [parts[1][:half].astype(BF16), (parts[1][half:].astype(F32) + high.astype(F32)).astype(BF16)]
    )
    return [swap_x(to_x), swap_y(to_y)]


def scatter_end(parts, sides):
    return parts[0].astype(F32) + sides[0].astype(F32) + sides[1].astype(F32)


def square_scatter(parts):
    return scatter_end(parts, scatter_sides(parts, scatter_corner(parts)))


def row_tokens(block):
    return jnp.concatenate(gather_rest(block, gather_sides(block)), axis=0)


def row_scatter(product):
    quarter = product.shape[0] // 4
    return square_scatter([product[j * quarter : (j + 1) * quarter] for j in range(4)])


def gather_shards(shard, sides, index):
    rows = shard.shape[0]
    half = rows // 2
    own, from_x, from_y, low, high = gather_rest(shard, sides)
    whole = jnp.zeros((4 * rows,) + shard.shape[1:], shard.dtype)
    for piece, start in (
        (own, index * rows),
        (from_x, (index ^ 1) * rows),
        (from_y, (index ^ 2) * rows),
        (low, (index ^ 3) * rows),
        (high, (index ^ 3) * rows + half),
    ):
        whole = lax.dynamic_update_slice(whole, piece, (start, 0))
    return whole


def scatter_terms(whole, index):
    rows = whole.shape[0] // 4
    return [lax.dynamic_slice_in_dim(whole, (index ^ j) * rows, rows) for j in range(4)]


def opening_kernel(
    chips,
    x_ref, vector_ref, routed_ref, mixer_ref, gate_ref,
    gains_ref, tables_ref, row_ref, mixers_ref, last_ref, gates_ref,
    vectors, send_v, receive_v, send_t, receive_t,
    send_n, receive_n, send_g, receive_g,
    up_sem, down_sem, in_low, in_high, to_partner, in_partner, local,
):
    nf, ne = lax.axis_size("fsdp"), lax.axis_size("expert")
    total = nf * ne
    f, e = lax.axis_index("fsdp"), lax.axis_index("expert")
    me = f * ne + e
    z, c = e // 2, lax.rem(e, 2)
    xn, yn = f ^ 1, f ^ 2
    up = (f, jnp.minimum(z + 1, chips - 1) * 2 + c)
    down = (f, jnp.maximum(z - 1, 0) * 2 + c)
    partner = (f, z * 2 + 1 - c)
    parts = ((pl.ds(0, 3), mixers_ref), (pl.ds(3, 1), last_ref))
    own_gate = pltpu.make_async_copy(gate_ref, gates_ref.at[f], local.at[2])
    own_mixer = [
        pltpu.make_async_copy(mixer_ref.at[span], ref.at[:, e], local.at[k])
        for k, (span, ref) in enumerate(parts)
    ]
    for copy in own_mixer + [own_gate]:
        copy.start()
    barrier = pltpu.get_barrier_semaphore()

    def greet(step, carry):
        peer = lax.rem(me + step, total)
        pl.semaphore_signal(
            barrier, inc=1, device_id=(peer // ne, lax.rem(peer, ne)), device_id_type=MESH
        )
        return carry

    lax.fori_loop(1, total, greet, 0)
    pl.semaphore_wait(barrier, total - 1)

    def remote(source, target, send, receive, device):
        return pltpu.make_async_remote_copy(
            src_ref=source,
            dst_ref=target,
            send_sem=send,
            recv_sem=receive,
            device_id=device,
            device_id_type=MESH,
        )

    def vector_copy(slot, peer):
        return remote(
            vector_ref, vectors.at[slot], send_v.at[peer], receive_v.at[slot],
            (peer // ne, lax.rem(peer, ne)),
        )

    def table_copy(slot, peer):
        return remote(routed_ref, tables_ref.at[slot], send_t.at[peer], receive_t.at[slot], (f, peer))

    def start_vector(step, carry):
        vector_copy(me, lax.rem(me + step, total)).start()
        return carry

    def start_table(step, carry):
        table_copy(e, lax.rem(e + step, ne)).start()
        return carry

    lax.fori_loop(1, total, start_vector, 0)
    lax.fori_loop(1, ne, start_table, 0)
    vectors[me] = vector_ref[...]
    tables_ref[e] = routed_ref[...]

    def shard(k, origin, target, send, receive, own):
        span, ref = parts[k]
        place = ref.at[:, origin * 2 + c]
        return remote(mixer_ref.at[span] if own else place, place, send, receive, target)

    def upward(k, origin, r, own=False):
        return shard(k, origin, up, up_sem.at[k, r], in_low.at[k, r], own)

    def downward(k, origin, r, own=False):
        return shard(k, origin, down, down_sem.at[k, r], in_high.at[k, r], own)

    def across(k, origin, own=False):
        return shard(k, origin, partner, to_partner.at[k, origin], in_partner.at[k, origin], own)

    for k in (0, 1):

        @pl.when(z < chips - 1)
        def _():
            upward(k, z, 0, True).start()

        @pl.when(z > 0)
        def _():
            downward(k, z, 0, True).start()

        across(k, z, True).start()

    def end_vector(step, carry):
        peer = lax.rem(me + step, total)
        vector_copy(peer, peer).wait_recv()
        return carry

    lax.fori_loop(1, total, end_vector, 0)
    blocks = gains_ref.shape[1] // 128
    per = total // blocks
    for block in range(blocks):
        gains_ref[:, block * 128 : (block + 1) * 128] = jnp.sum(
            vectors[block * per : (block + 1) * per], axis=0
        )
    half = x_ref.shape[0] // 2
    low, high = pl.ds(0, half), pl.ds(half, half)

    def piece(index, ref, origin, rows, device, slot):
        send, receive = (send_n, receive_n) if index == 0 else (send_g, receive_g)
        here, there = (origin ^ f, origin ^ device) if index == 0 else (origin, origin)
        return remote(
            ref.at[here, rows], ref.at[there, rows], send.at[slot], receive.at[slot], (device, e)
        )

    def arrived(index, ref, origin, rows, slot):
        send, receive = (send_n, receive_n) if index == 0 else (send_g, receive_g)
        place = ref.at[origin ^ f if index == 0 else origin, rows]
        return remote(place, place, send.at[slot], receive.at[slot], (xn, e))

    def outgoing(index, ref, first, second):
        return [
            piece(index, ref, f, first, xn, 0),
            piece(index, ref, f, second, yn, 1),
            piece(index, ref, f, second, xn, 2),
            piece(index, ref, f, first, yn, 3),
        ]

    def relays(index, ref, first, second):
        return [piece(index, ref, xn, first, yn, 4), piece(index, ref, yn, second, xn, 5)]

    for rows in (low, high):
        values = x_ref[rows].astype(F32)
        scale = lax.rsqrt(jnp.mean(values * values, axis=1, keepdims=True) + EPSILON)
        row_ref[0, rows] = (values * scale * gains_ref[0:1]).astype(BF16)
    own_gate.wait()
    row_out = outgoing(0, row_ref, low, high)
    row_relay = relays(0, row_ref, low, high)
    depth = gate_ref.shape[0] // 2
    first, second = pl.ds(0, depth), pl.ds(depth, depth)
    gate_out = outgoing(1, gates_ref, first, second)
    gate_relay = relays(1, gates_ref, first, second)
    for copy in row_out + gate_out:
        copy.start()
    arrived(0, row_ref, xn, low, 0).wait_recv()
    row_relay[0].start()
    arrived(0, row_ref, yn, high, 1).wait_recv()
    row_relay[1].start()

    def hop(r, carry):
        before, after = z - r, z + r
        for k in (0, 1):

            @pl.when(before >= 0)
            def _():
                upward(k, before, r - 1).wait_recv()

                @pl.when(z < chips - 1)
                def _():
                    upward(k, before, r).start()

                across(k, before).start()

            @pl.when(after < chips)
            def _():
                downward(k, after, r - 1).wait_recv()

                @pl.when(z > 0)
                def _():
                    downward(k, after, r).start()

                across(k, after).start()

        return carry

    lax.fori_loop(1, 3, hop, 0)
    arrived(1, gates_ref, xn, first, 0).wait_recv()
    gate_relay[0].start()
    arrived(1, gates_ref, yn, second, 1).wait_recv()
    gate_relay[1].start()
    lax.fori_loop(3, chips, hop, 0)

    for index, ref, (one, two) in ((0, row_ref, (low, high)), (1, gates_ref, (first, second))):
        arrived(index, ref, xn, two, 2).wait_recv()
        arrived(index, ref, yn, one, 3).wait_recv()
        arrived(index, ref, f ^ 3, one, 4).wait_recv()
        arrived(index, ref, f ^ 3, two, 5).wait_recv()
    for copy in row_out + gate_out + row_relay + gate_relay:
        copy.wait_send()
    for k in (0, 1):
        own_mixer[k].wait()

        @pl.when(z < chips - 1)
        def _():
            upward(k, z, 0, True).wait_send()

        @pl.when(z > 0)
        def _():
            downward(k, z, 0, True).wait_send()

    def finish(r, carry):
        before, after = z - r, z + r
        for k in (0, 1):

            @pl.when((before >= 0) & (z < chips - 1))
            def _():
                upward(k, before, r).wait_send()

            @pl.when((after < chips) & (z > 0))
            def _():
                downward(k, after, r).wait_send()

        return carry

    lax.fori_loop(1, chips, finish, 0)

    def shared(origin, carry):
        for k in (0, 1):
            across(k, origin).wait_send()
            across(k, origin).wait_recv()
        return carry

    lax.fori_loop(0, chips, shared, 0)

    def sent_vector(step, carry):
        peer = lax.rem(me + step, total)
        vector_copy(peer, peer).wait_send()
        return carry

    def end_table(step, carry):
        peer = lax.rem(e + step, ne)
        copy = table_copy(peer, peer)
        copy.wait_recv()
        copy.wait_send()
        return carry

    lax.fori_loop(1, total, sent_vector, 0)
    lax.fori_loop(1, ne, end_table, 0)


def opening(x, vector, routed, mixer, gate, nf):
    ne = routed.shape[0]
    chips, devices = ne // 2, nf * ne
    whole = pl.BlockSpec(memory_space=pltpu.VMEM)
    far = pl.BlockSpec(memory_space=pl.ANY)
    dma = pltpu.SemaphoreType.DMA
    return pl.pallas_call(
        functools.partial(opening_kernel, chips),
        out_shape=[
            jax.ShapeDtypeStruct((8, x.shape[1]), F32),
            jax.ShapeDtypeStruct((ne,) + routed.shape, F32),
            jax.ShapeDtypeStruct((nf,) + x.shape, BF16),
            jax.ShapeDtypeStruct((3, ne) + mixer.shape[1:], BF16),
            jax.ShapeDtypeStruct((1, ne) + mixer.shape[1:], BF16),
            jax.ShapeDtypeStruct((nf,) + gate.shape, BF16),
        ],
        in_specs=[whole] * 5,
        out_specs=[whole, whole, whole, far, far, far],
        scratch_shapes=[pltpu.VMEM((devices,) + vector.shape, F32)]
        + [dma((devices,))] * 2
        + [dma((ne,))] * 2
        + [dma((6,))] * 4
        + [dma((2, chips))] * 6
        + [dma((3,))],
        compiler_params=pltpu.CompilerParams(
            collective_id=1, has_side_effects=True, vmem_limit_bytes=24 * 1024 * 1024
        ),
        name="opening",
    )(x, vector, routed, mixer, gate)


def collect_kernel(terms_ref, sum_ref, arrived, send, receive):
    nf, ne = lax.axis_size("fsdp"), lax.axis_size("expert")
    total = nf * ne
    me = lax.axis_index("fsdp") * ne + lax.axis_index("expert")
    barrier = pltpu.get_barrier_semaphore()

    def greet(step, carry):
        peer = lax.rem(me + step, total)
        pl.semaphore_signal(
            barrier, inc=1, device_id=(peer // ne, lax.rem(peer, ne)), device_id_type=MESH
        )
        return carry

    lax.fori_loop(1, total, greet, 0)
    pl.semaphore_wait(barrier, total - 1)

    def copy_of(slot, peer):
        return pltpu.make_async_remote_copy(
            src_ref=terms_ref.at[peer],
            dst_ref=arrived.at[slot],
            send_sem=send.at[peer],
            recv_sem=receive.at[slot],
            device_id=(peer // ne, lax.rem(peer, ne)),
            device_id_type=MESH,
        )

    def begin(step, carry):
        copy_of(me, lax.rem(me + step, total)).start()
        return carry

    lax.fori_loop(1, total, begin, 0)
    arrived[me] = terms_ref[me]

    def end(step, carry):
        peer = lax.rem(me + step, total)
        copy = copy_of(peer, peer)
        copy.wait_recv()
        copy.wait_send()
        return carry

    lax.fori_loop(1, total, end, 0)
    sum_ref[...] = jnp.sum(arrived[...], axis=0)


def collect(terms):
    devices = terms.shape[0]
    return pl.pallas_call(
        collect_kernel,
        out_shape=jax.ShapeDtypeStruct(terms.shape[1:], terms.dtype),
        in_specs=[pl.BlockSpec(memory_space=pltpu.VMEM)],
        out_specs=pl.BlockSpec(memory_space=pltpu.VMEM),
        scratch_shapes=[pltpu.VMEM(terms.shape, terms.dtype)]
        + [pltpu.SemaphoreType.DMA((devices,))] * 2,
        compiler_params=pltpu.CompilerParams(collective_id=2, has_side_effects=True),
        name="collect",
    )(terms)


def places(chips):
    f, e = lax.axis_index("fsdp"), lax.axis_index("expert")
    z, c = e // 2, lax.rem(e, 2)
    up = (f, jnp.minimum(z + 1, chips - 1) * 2 + c)
    down = (f, jnp.maximum(z - 1, 0) * 2 + c)
    return f, e, z, c, up, down, (f, z * 2 + 1 - c), (f ^ 1, e), (f ^ 2, e)


def meet(chips, z, up, down, others):
    barrier = pltpu.get_barrier_semaphore()
    for peer in others:
        pl.semaphore_signal(barrier, inc=1, device_id=peer, device_id_type=MESH)

    @pl.when(z < chips - 1)
    def _():
        pl.semaphore_signal(barrier, inc=1, device_id=up, device_id_type=MESH)

    @pl.when(z > 0)
    def _():
        pl.semaphore_signal(barrier, inc=1, device_id=down, device_id_type=MESH)

    known = len(others) + jnp.where(z < chips - 1, 1, 0) + jnp.where(z > 0, 1, 0)
    pl.semaphore_wait(barrier, known)


def remote_copy(source, target, send, receive, device):
    return pltpu.make_async_remote_copy(
        src_ref=source,
        dst_ref=target,
        send_sem=send,
        recv_sem=receive,
        device_id=device,
        device_id_type=MESH,
    )


def spread_kernel(
    chips, block_ref, tokens_ref, all_ref, row_ref,
    up_sem, down_sem, in_low, in_high, to_partner, in_partner, send_n, receive_n, local,
):
    f, e, z, c, up, down, partner, side_x, side_y = places(chips)
    xn, yn = f ^ 1, f ^ 2
    own = [
        pltpu.make_async_copy(block_ref, all_ref.at[e], local.at[0]),
        pltpu.make_async_copy(tokens_ref, row_ref.at[0], local.at[1]),
    ]
    for copy in own:
        copy.start()
    meet(chips, z, up, down, (partner, side_x, side_y))

    def shard(origin, target, send, receive, first):
        place = all_ref.at[origin * 2 + c]
        return remote_copy(block_ref if first else place, place, send, receive, target)

    def upward(origin, r, first=False):
        return shard(origin, up, up_sem.at[r], in_low.at[r], first)

    def downward(origin, r, first=False):
        return shard(origin, down, down_sem.at[r], in_high.at[r], first)

    def across(origin, first=False):
        return shard(origin, partner, to_partner.at[origin], in_partner.at[origin], first)

    @pl.when(z < chips - 1)
    def _():
        upward(z, 0, True).start()

    @pl.when(z > 0)
    def _():
        downward(z, 0, True).start()

    across(z, True).start()
    half = tokens_ref.shape[0] // 2
    low, high = pl.ds(0, half), pl.ds(half, half)

    def piece(origin, rows, device, slot):
        source = tokens_ref.at[rows] if slot < 4 else row_ref.at[origin ^ f, rows]
        return remote_copy(
            source, row_ref.at[origin ^ device, rows], send_n.at[slot], receive_n.at[slot], (device, e)
        )

    def arrived(origin, rows, slot):
        place = row_ref.at[origin ^ f, rows]
        return remote_copy(place, place, send_n.at[slot], receive_n.at[slot], side_x)

    copies = [piece(f, low, xn, 0), piece(f, high, yn, 1), piece(f, high, xn, 2), piece(f, low, yn, 3)]
    relays = [piece(xn, low, yn, 4), piece(yn, high, xn, 5)]
    for copy in copies:
        copy.start()
    arrived(xn, low, 0).wait_recv()
    relays[0].start()
    arrived(yn, high, 1).wait_recv()
    relays[1].start()

    def hop(r, carry):
        before, after = z - r, z + r

        @pl.when(before >= 0)
        def _():
            upward(before, r - 1).wait_recv()

            @pl.when(z < chips - 1)
            def _():
                upward(before, r).start()

            across(before).start()

        @pl.when(after < chips)
        def _():
            downward(after, r - 1).wait_recv()

            @pl.when(z > 0)
            def _():
                downward(after, r).start()

            across(after).start()

        return carry

    lax.fori_loop(1, chips, hop, 0)
    arrived(xn, high, 2).wait_recv()
    arrived(yn, low, 3).wait_recv()
    arrived(f ^ 3, low, 4).wait_recv()
    arrived(f ^ 3, high, 5).wait_recv()
    for copy in copies + relays:
        copy.wait_send()
    for copy in own:
        copy.wait()

    @pl.when(z < chips - 1)
    def _():
        upward(z, 0, True).wait_send()

    @pl.when(z > 0)
    def _():
        downward(z, 0, True).wait_send()

    def finish(r, carry):
        before, after = z - r, z + r

        @pl.when((before >= 0) & (z < chips - 1))
        def _():
            upward(before, r).wait_send()

        @pl.when((after < chips) & (z > 0))
        def _():
            downward(after, r).wait_send()

        return carry

    lax.fori_loop(1, chips, finish, 0)

    def shared(origin, carry):
        across(origin).wait_send()
        across(origin).wait_recv()
        return carry

    lax.fori_loop(0, chips, shared, 0)


def spread(block, tokens, nf, ne, cid):
    chips = ne // 2
    dma = pltpu.SemaphoreType.DMA
    return pl.pallas_call(
        functools.partial(spread_kernel, chips),
        out_shape=[
            jax.ShapeDtypeStruct((ne,) + block.shape, block.dtype),
            jax.ShapeDtypeStruct((nf,) + tokens.shape, tokens.dtype),
        ],
        in_specs=[pl.BlockSpec(memory_space=pltpu.VMEM)] * 2,
        out_specs=[pl.BlockSpec(memory_space=pltpu.VMEM)] * 2,
        scratch_shapes=[dma((chips,))] * 6 + [dma((6,))] * 2 + [dma((2,))],
        compiler_params=pltpu.CompilerParams(
            collective_id=cid, has_side_effects=True, vmem_limit_bytes=40 * 1024 * 1024
        ),
        cost_estimate=WIRE,
        name=f"spread{cid}",
    )(block, tokens)


def combine_kernel(
    chips, terms_ref, parts_ref, sum_ref, row_sum_ref,
    theirs, going, coming, corner, onward, from_side,
    up_sem, down_sem, in_low, in_high, to_partner, in_partner, send_n, receive_n,
):
    f, e, z, c, up, down, partner, side_x, side_y = places(chips)
    meet(chips, z, up, down, (partner, side_x, side_y))

    def across(target):
        return remote_copy(
            terms_ref.at[target * 2 + 1 - c], theirs.at[target],
            to_partner.at[target], in_partner.at[target], partner,
        )

    def upward(target):
        return remote_copy(
            going.at[target], coming.at[target], up_sem.at[target], in_low.at[target], up
        )

    def downward(target, receiver):
        place = coming.at[jnp.where(target == receiver, chips, target)]
        return remote_copy(
            going.at[target], place, down_sem.at[target], in_high.at[target], down
        )

    def offer(r, carry):
        across(r).start()
        across(chips - 1 - r).start()
        return carry

    lax.fori_loop(0, chips // 2, offer, 0)
    half = parts_ref.shape[1] // 2
    low, high = pl.ds(0, half), pl.ds(half, half)

    def side(slot, source, target, device):
        return remote_copy(source, target, send_n.at[slot], receive_n.at[slot], device)

    copies = [
        side(0, parts_ref.at[3, low], corner.at[0], side_x),
        side(1, parts_ref.at[3, high], corner.at[1], side_y),
        side(2, parts_ref.at[1, low], from_side.at[0, low], side_x),
        side(3, parts_ref.at[2, high], from_side.at[1, high], side_y),
        side(4, onward.at[0], from_side.at[0, high], side_x),
        side(5, onward.at[1], from_side.at[1, low], side_y),
    ]
    for copy in copies[:4]:
        copy.start()

    def chip_term(target):
        return terms_ref[target * 2 + c].astype(F32) + theirs[target].astype(F32)

    def rise(r):
        target = chips - 1 - r

        @pl.when(target > z)
        def _():
            across(target).wait_recv()

            @pl.when(z > 0)
            def _():
                upward(target).wait_recv()
                going[target] = (chip_term(target) + coming[target].astype(F32)).astype(BF16)

            @pl.when(z == 0)
            def _():
                going[target] = chip_term(target).astype(BF16)

            upward(target).start()

    def fall(r):
        @pl.when(r < z)
        def _():
            across(r).wait_recv()

            @pl.when(z < chips - 1)
            def _():
                downward(r, z).wait_recv()
                going[r] = (chip_term(r) + coming[r].astype(F32)).astype(BF16)

            @pl.when(z == chips - 1)
            def _():
                going[r] = chip_term(r).astype(BF16)

            downward(r, z - 1).start()

    def pass_on(r, carry):
        @pl.when(z < chips // 2)
        def _():
            rise(r)

        fall(r)

        @pl.when(z >= chips // 2)
        def _():
            rise(r)

        return carry

    lax.fori_loop(0, 1, pass_on, 0)
    copies[1].wait_recv()
    onward[0] = (parts_ref[1, high].astype(F32) + corner[1].astype(F32)).astype(BF16)
    copies[4].start()
    copies[0].wait_recv()
    onward[1] = (parts_ref[2, low].astype(F32) + corner[0].astype(F32)).astype(BF16)
    copies[5].start()
    lax.fori_loop(1, chips, pass_on, 0)
    for copy in copies[2:]:
        copy.wait_recv()
    row_sum_ref[...] = (
        parts_ref[0].astype(F32) + from_side[0].astype(F32) + from_side[1].astype(F32)
    )
    across(z).wait_recv()
    sum_ref[...] = chip_term(z)

    @pl.when(z > 0)
    def _():
        upward(z).wait_recv()
        sum_ref[...] += coming[z].astype(F32)

    @pl.when(z < chips - 1)
    def _():
        downward(z, z).wait_recv()
        sum_ref[...] += coming[chips].astype(F32)

    for copy in copies:
        copy.wait_send()

    def finish(target, carry):
        across(target).wait_send()

        @pl.when(target > z)
        def _():
            upward(target).wait_send()

        @pl.when(target < z)
        def _():
            downward(target, z - 1).wait_send()

        return carry

    lax.fori_loop(0, chips, finish, 0)


def combine(terms, parts, cid):
    ne = terms.shape[0]
    chips = ne // 2
    parts = parts.reshape(4, parts.shape[0] // 4, parts.shape[1])
    block = terms.shape[1:]
    halves = (2, parts.shape[1] // 2, parts.shape[2])
    sides = (2,) + parts.shape[1:]
    dma = pltpu.SemaphoreType.DMA
    return pl.pallas_call(
        functools.partial(combine_kernel, chips),
        out_shape=[
            jax.ShapeDtypeStruct(terms.shape[1:], F32),
            jax.ShapeDtypeStruct(parts.shape[1:], F32),
        ],
        in_specs=[pl.BlockSpec(memory_space=pltpu.VMEM)] * 2,
        out_specs=[pl.BlockSpec(memory_space=pltpu.VMEM)] * 2,
        scratch_shapes=[pltpu.VMEM((chips,) + block, BF16)] * 2
        + [pltpu.VMEM((chips + 1,) + block, BF16)]
        + [pltpu.VMEM(halves, BF16)] * 2
        + [pltpu.VMEM(sides, BF16)]
        + [dma((chips,))] * 6
        + [dma((6,))] * 2,
        compiler_params=pltpu.CompilerParams(
            collective_id=cid, has_side_effects=True, vmem_limit_bytes=60 * 1024 * 1024
        ),
        cost_estimate=WIRE,
        name=f"combine{cid}",
    )(terms, parts)


def on_device(
    inputs,
    teacher,
    lengths,
    deal_order,
    routes,
    route_weights,
    norm_gains,
    mixer_weights,
    shared_weights,
    shared_gate,
    expert_gate,
    expert_up,
    expert_down,
):
    tokens_dev = inputs.shape[1]
    width = inputs.shape[2]
    nf = lax.axis_size("fsdp")
    ne = lax.axis_size("expert")
    devices = nf * ne
    row_len = tokens_dev * nf
    capacity = 3 * tokens_dev * TOP // (2 * ne)
    total_tokens = row_len * ne
    columns = mixer_weights.shape[2]
    heads_local = columns // HD
    f_index = lax.axis_index("fsdp")
    e_index = lax.axis_index("expert")

    piece = norm_gains.shape[1]
    slot = (f_index * ne + e_index) % (128 // piece)
    vector = jnp.concatenate([norm_gains, shared_gate[None]], axis=0).astype(F32)
    vector = lax.dynamic_update_slice(jnp.zeros((8, 128), F32), vector, (0, slot * piece))
    chosen = routes[0]
    weights_route = route_weights[0]
    expert_ids = jnp.arange(ne, dtype=jnp.int32)
    routed = jnp.sum(
        jnp.where(chosen.T[None] == expert_ids[:, None, None], weights_route.T[None], 0.0), axis=1
    )
    mixer_shard = jnp.transpose(mixer_weights, (1, 0, 2))
    gains, tables, row_blocks, mixer_in, mixer_out, gates = opening(
        inputs[0], vector, routed, mixer_shard, expert_gate[0], nf
    )
    first_gain, second_gain, gate_vector = gains[0], gains[1], gains[2]
    token_weight = lax.dynamic_index_in_dim(tables, e_index, axis=1, keepdims=False)
    mixer_in = mixer_in.reshape(3, width, columns)
    mixer_out = mixer_out.reshape(width, columns)
    gate_rows = gates.reshape(width, gates.shape[2])
    row_normed = row_blocks.reshape(row_len, width)

    shared_shard, up_shard, down_shard, gains = lax.optimization_barrier(
        (shared_weights, expert_up[0], expert_down[0], gains)
    )
    shared_shard = jnp.transpose(shared_shard, (1, 0, 2))
    shared_first = lax.all_gather(shared_shard[0], "expert", axis=0, tiled=True)
    up_sides = gather_sides(up_shard)

    first_len = lengths[deal_order[2 * e_index]]
    second_len = lengths[deal_order[2 * e_index + 1]]
    row_places = (
        (f_index ^ jnp.arange(nf, dtype=jnp.int32))[:, None] * tokens_dev
        + jnp.arange(tokens_dev, dtype=jnp.int32)[None]
    ).reshape(row_len)
    row_segment = (row_places >= first_len).astype(jnp.int32) + (
        row_places >= first_len + second_len
    ).astype(jnp.int32)
    row_position = (
        row_places
        - first_len * (row_segment >= 1).astype(jnp.int32)
        - second_len * (row_segment >= 2).astype(jnp.int32)
    )
    own_segment = row_segment[:tokens_dev]
    allowed = (row_segment[:, None] == row_segment[None, :]) & (
        row_places[None, :] <= row_places[:, None]
    )
    inverse = THETA ** (-(jnp.arange(HD // 2, dtype=F32) * 2.0) / HD)
    angles = row_position.astype(F32)[:, None] * inverse[None, :]
    cosine = jnp.concatenate([jnp.cos(angles)] * 2, axis=1)[:, None, :]
    sine = jnp.concatenate([jnp.sin(angles)] * 2, axis=1)[:, None, :]

    flat_inputs = inputs[0].astype(F32)
    first_scale = lax.rsqrt(jnp.mean(flat_inputs * flat_inputs, axis=1) + EPSILON)
    projected = dot("td,kde->kte", row_normed, mixer_in)

    def heads(values):
        return values.reshape(row_len, heads_local, HD)

    raw_query, raw_key = heads(projected[0]), heads(projected[1])
    queries = (raw_query * cosine + turn(raw_query) * sine).astype(BF16)
    keys = (raw_key * cosine + turn(raw_key) * sine).astype(BF16)
    values = heads(projected[2].astype(BF16))
    score_factor = HD ** (-0.5)

    def score():
        raw = dot("qhd,khd->hqk", queries, keys)
        return jnp.where(allowed[None], raw * score_factor, NEG_LARGE)

    scores = score()
    top_score = jnp.max(scores, axis=2, keepdims=True)
    shifted = jnp.exp(scores - top_score)
    row_total = jnp.sum(shifted, axis=2, keepdims=True)
    probabilities = shifted / row_total
    log_total = top_score + jnp.log(row_total)
    context = dot("hqk,khd->qhd", probabilities.astype(BF16), values)
    context = context.reshape(row_len, columns).astype(BF16)
    attn_out = row_scatter(dot("tc,dc->td", context, mixer_out))
    residual = flat_inputs + attn_out
    second_scale = lax.rsqrt(jnp.mean(residual * residual, axis=1) + EPSILON)
    mixed_in = (residual * second_scale[:, None] * second_gain[None, :]).astype(BF16)

    down_shard, mixed_in = lax.optimization_barrier((down_shard, mixed_in))
    up_rows = gather_shards(up_shard, up_sides, f_index)
    down_rows = gather_shards(down_shard, gather_sides(down_shard), f_index)
    tokens_all, row_mixed = spread(mixed_in, mixed_in, nf, ne, 3)
    row_mixed = row_mixed.reshape(row_len, width)
    second_shard, third_shard, tokens_all = lax.optimization_barrier(
        (shared_shard[1], shared_shard[2], tokens_all)
    )
    shared_second = lax.all_gather(second_shard, "expert", axis=0, tiled=True)
    shared_down = lax.all_gather(third_shard, "expert", axis=0, tiled=True)
    routed_here = token_weight > 0.0
    marks = routed_here.astype(BF16)
    upper = (
        jnp.arange(tokens_dev, dtype=jnp.int32)[:, None]
        <= jnp.arange(tokens_dev, dtype=jnp.int32)[None, :]
    ).astype(BF16)
    order = dot("st,tu->su", marks, upper) - 1.0
    slots = jnp.arange(capacity, dtype=jnp.int32).astype(F32)
    hit = (order[:, None, :] == slots[None, :, None]) & routed_here[:, None, :]
    picker = hit.astype(BF16)
    slot_weight = jnp.sum(jnp.where(hit, token_weight[:, None, :], 0.0), axis=2).reshape(
        ne * capacity, 1
    )

    def pick(blocks):
        return dot("srt,std->srd", picker, blocks).reshape(ne * capacity, width)

    def unpick(rows):
        return dot("srt,srd->std", picker, rows.reshape(ne, capacity, width)).astype(BF16)

    rows_in = pick(tokens_all).astype(BF16)
    gate_pre = dot("rd,df->rf", rows_in, gate_rows)
    up_pre = dot("rd,df->rf", rows_in, up_rows)
    hidden = (jax.nn.silu(gate_pre) * up_pre).astype(BF16)
    result = (slot_weight * dot("rf,fd->rd", hidden, down_rows)).astype(BF16)


    shared_pre = (dot("td,df->tf", row_mixed, shared_first), dot("td,df->tf", row_mixed, shared_second))
    shared_hidden = (jax.nn.silu(shared_pre[0]) * shared_pre[1]).astype(BF16)
    routed_sum, shared_out = combine(
        unpick(result), dot("tf,df->td", shared_hidden, shared_down).astype(BF16), 4
    )
    gate_value = jax.nn.sigmoid(
        jnp.sum(mixed_in.astype(F32) * gate_vector[None, :], axis=1)
    )

    block_total = residual + gate_value[:, None] * shared_out + routed_sum
    out_block = block_total.astype(BF16)[None]
    valid_mask = (own_segment < 2).astype(F32)
    valid_count = jnp.sum(lengths).astype(F32)
    dtotal = (
        total_tokens
        / valid_count
        * valid_mask[:, None]
        * (block_total - teacher[0].astype(F32))
    )

    dshared_out = (gate_value[:, None] * dtotal).astype(BF16)
    dlogit = jnp.sum(dtotal * shared_out, axis=1) * gate_value * (1.0 - gate_value)
    dtotal_all, row_dout = spread(dtotal.astype(BF16), dshared_out, nf, ne, 5)
    row_dout = row_dout.reshape(row_len, width)
    down_term = dot("td,tf->df", row_dout, shared_hidden).astype(BF16)
    row_dout, dtotal_all, down_term = lax.optimization_barrier((row_dout, dtotal_all, down_term))
    shared_sigmoid = jax.nn.sigmoid(shared_pre[0])
    dshared_hidden = dot("td,df->tf", row_dout, shared_down)
    dshared_gate = (
        dshared_hidden * shared_pre[1] * shared_sigmoid * (1.0 + shared_pre[0] * (1.0 - shared_sigmoid))
    ).astype(BF16)
    dshared_up = (dshared_hidden * shared_pre[0] * shared_sigmoid).astype(BF16)
    dmixed_first = dot("tf,df->td", dshared_gate, shared_first)

    def scatter_columns(term):
        return lax.psum_scatter(term.astype(BF16), "expert", scatter_dimension=0, tiled=True)

    grad_shared_down = scatter_columns(down_term)
    gate_term = dot("td,tf->df", row_mixed, dshared_gate).astype(BF16)
    up_term = dot("td,tf->df", row_mixed, dshared_up).astype(BF16)

    dresult = (slot_weight * pick(dtotal_all)).astype(BF16)
    gate_sigmoid = jax.nn.sigmoid(gate_pre)
    activated = gate_pre * gate_sigmoid
    grad_down_term = dot("rf,rd->fd", hidden, dresult).astype(BF16)
    dresult, grad_down_term = lax.optimization_barrier((dresult, grad_down_term))
    terms = [scatter_terms(grad_down_term, f_index)]
    corners = [scatter_corner(terms[0])]
    dhidden = dot("rd,fd->rf", dresult, down_rows)
    dgate = (dhidden * up_pre * gate_sigmoid * (1.0 + gate_pre * (1.0 - gate_sigmoid))).astype(BF16)
    dup = (dhidden * activated).astype(BF16)
    dreturn = (dot("rf,df->rd", dgate, gate_rows) + dot("rf,df->rd", dup, up_rows)).astype(BF16)
    dreturn, corners = lax.optimization_barrier((dreturn, corners))
    sides = [scatter_sides(terms[0], corners[0])]
    grad_gate_term = dot("rd,rf->df", rows_in, dgate).astype(BF16)
    terms.append(scatter_terms(grad_gate_term, f_index))
    corners.append(scatter_corner(terms[1]))
    dmixed_terms = (dmixed_first + dot("tf,df->td", dshared_up, shared_second)).astype(BF16)
    dreturned, up_term, gate_term, corners = lax.optimization_barrier(
        (unpick(dreturn), up_term, gate_term, corners)
    )
    grad_shared_gates = scatter_columns(gate_term)
    sides.append(scatter_sides(terms[1], corners[1]))
    from_experts, dmixed_shared = combine(dreturned, dmixed_terms, 6)
    from_experts, up_term, corners, sides, grad_shared_down = lax.optimization_barrier(
        (from_experts, up_term, corners, sides, grad_shared_down)
    )
    grad_shared_ups = scatter_columns(up_term)

    dmixed = dmixed_shared + dlogit[:, None] * gate_vector[None, :] + from_experts
    vector_term = jnp.sum(dlogit[:, None] * mixed_in.astype(F32), axis=0)
    dresidual_norm, second_gain_grad = norm_back(dmixed, residual, second_scale, second_gain)
    dresidual = dtotal + dresidual_norm
    dattn = dresidual.astype(BF16)
    dattn, rows_again, dup = lax.optimization_barrier((dattn, rows_in, dup))
    row_dattn = row_tokens(dattn)
    grad_up_term = dot("rd,rf->df", rows_again, dup).astype(BF16)
    row_dattn, grad_up_term, grad_shared_gates = lax.optimization_barrier(
        (row_dattn, grad_up_term, grad_shared_gates)
    )
    terms.append(scatter_terms(grad_up_term, f_index))
    corners.append(scatter_corner(terms[2]))

    dcontext = dot("td,dc->tc", row_dattn, mixer_out).astype(BF16)
    mixer_out_term = dot("td,tc->dc", row_dattn, context).astype(BF16)
    dcontext, mixer_out_term = lax.optimization_barrier((dcontext, mixer_out_term))
    dcontext = heads(dcontext)
    probabilities_again = jnp.exp(score() - log_total)
    dprobs = dot("qhd,khd->hqk", dcontext, values)
    delta_rows = jnp.sum(probabilities_again * dprobs, axis=2, keepdims=True)
    dscores = (probabilities_again * (dprobs - delta_rows)).astype(BF16)
    dqueries = dot("hqk,khd->qhd", dscores, keys) * score_factor
    dkeys = dot("hqk,qhd->khd", dscores, queries) * score_factor
    dvalues = dot("hqk,qhd->khd", probabilities_again.astype(BF16), dcontext)

    def back(incoming):
        return (incoming * cosine + turn_back(incoming * sine)).reshape(row_len, columns)

    dprojected = jnp.stack(
        [back(dqueries), back(dkeys), dvalues.reshape(row_len, columns)], axis=0
    ).astype(BF16)
    dprojected, corners[2] = lax.optimization_barrier((dprojected, corners[2]))
    sides.append(scatter_sides(terms[2], corners[2]))
    mixer_term = dot("td,kte->kde", row_normed, dprojected).astype(BF16)
    mixer_term = jnp.concatenate([mixer_term, mixer_out_term[None]], axis=0)
    mixer_term, grad_shared_ups = lax.optimization_barrier((mixer_term, grad_shared_ups))
    grad_mixer = lax.psum_scatter(mixer_term, "expert", scatter_dimension=1, tiled=True)
    dnormed = dot("kte,kde->td", dprojected, mixer_in).astype(BF16)
    dnormed, sides[2] = lax.optimization_barrier((row_scatter(dnormed), sides[2]))
    grad_expert_down, grad_expert_gate, grad_expert_up = [
        scatter_end(parts, side)[None] for parts, side in zip(terms, sides)
    ]
    dflat, first_gain_grad = norm_back(dnormed, flat_inputs, first_scale, first_gain)
    grad_input = (dresidual + dflat)[None]

    grad_shared = jnp.stack([grad_shared_gates, grad_shared_ups, grad_shared_down], axis=1)
    grad_shared = grad_shared.astype(F32)
    terms = jnp.stack([first_gain_grad, second_gain_grad, vector_term]).reshape(3, devices, piece)
    terms = jnp.pad(jnp.transpose(terms, (1, 0, 2)), ((0, 0), (0, 5), (0, 128 - piece)))
    sums = collect(terms)
    (grad_mixer, sums, grad_shared, grad_expert_down, grad_expert_gate, grad_expert_up) = (
        lax.optimization_barrier(
            (grad_mixer, sums, grad_shared, grad_expert_down, grad_expert_gate, grad_expert_up)
        )
    )
    grad_mixer = jnp.transpose(grad_mixer, (1, 0, 2)).astype(F32)
    grad_gains = sums[:2, :piece]
    grad_shared_gate = sums[2, :piece]
    return (
        out_block,
        grad_input,
        grad_gains,
        grad_mixer,
        grad_shared,
        grad_shared_gate,
        grad_expert_gate,
        grad_expert_up,
        grad_expert_down,
    )


def solution(mesh):
    rows = P("expert", "fsdp", None)
    both = P(("fsdp", "expert"))
    gains = P(None, ("fsdp", "expert"))
    shared = P("expert", None, "fsdp")
    return jax.shard_map(
        on_device,
        mesh=mesh,
        in_specs=(rows, rows, P(), P(), rows, rows, gains, shared, shared, both, rows, rows, rows),
        out_specs=(rows, rows, gains, shared, shared, both, rows, rows, rows),
        check_vma=False,
    )
```

```python
import functools

import jax
import jax.numpy as jnp
from jax import lax
from jax.experimental import pallas as pl
from jax.experimental.pallas import tpu as pltpu
from jax.sharding import PartitionSpec as P

HD = 128
TOP = 4
THETA = 1000000.0
EPSILON = 1e-06
NEG_LARGE = -1e30
MESH = pl.DeviceIdType.MESH
WIRE = pl.CostEstimate(flops=0, bytes_accessed=120_000_000, transcendentals=0)
F32 = jnp.float32
BF16 = jnp.bfloat16


def turn(values):
    half = values.shape[-1] // 2
    return jnp.concatenate([-values[..., half:], values[..., :half]], axis=-1)


def turn_back(values):
    half = values.shape[-1] // 2
    return jnp.concatenate([values[..., half:], -values[..., :half]], axis=-1)


def norm_back(incoming, values, scale_rows, gain_row):
    unit_rows = values * scale_rows[:, None]
    gain_grad = jnp.sum(incoming * unit_rows, axis=0)
    dunit = incoming * gain_row[None, :]
    back_rows = scale_rows[:, None] * (
        dunit - unit_rows * jnp.mean(dunit * unit_rows, axis=1, keepdims=True)
    )
    return (back_rows, gain_grad)


def dot(form, left, right):
    return jnp.einsum(form, left, right, preferred_element_type=F32)


def swap_x(values):
    return lax.ppermute(values, "fsdp", [(0, 1), (1, 0), (2, 3), (3, 2)])


def swap_y(values):
    return lax.ppermute(values, "fsdp", [(0, 2), (2, 0), (1, 3), (3, 1)])


def gather_sides(block):
    return [swap_x(block), swap_y(block)]


def gather_rest(block, sides):
    half = block.shape[0] // 2
    return [block, *sides, swap_y(sides[0][:half]), swap_x(sides[1][half:])]


def scatter_corner(parts):
    half = parts[0].shape[0] // 2
    return [swap_x(parts[3][:half].astype(BF16)), swap_y(parts[3][half:].astype(BF16))]


def scatter_sides(parts, corner):
    half = parts[0].shape[0] // 2
    low, high = corner
    to_y = jnp.concatenate(
        [(parts[2][:half].astype(F32) + low.astype(F32)).astype(BF16), parts[2][half:].astype(BF16)]
    )
    to_x = jnp.concatenate(
        [parts[1][:half].astype(BF16), (parts[1][half:].astype(F32) + high.astype(F32)).astype(BF16)]
    )
    return [swap_x(to_x), swap_y(to_y)]


def scatter_end(parts, sides):
    return parts[0].astype(F32) + sides[0].astype(F32) + sides[1].astype(F32)


def square_scatter(parts):
    return scatter_end(parts, scatter_sides(parts, scatter_corner(parts)))


def row_tokens(block):
    return jnp.concatenate(gather_rest(block, gather_sides(block)), axis=0)


def row_scatter(product):
    quarter = product.shape[0] // 4
    return square_scatter([product[j * quarter : (j + 1) * quarter] for j in range(4)])


def gather_shards(shard, sides, index):
    rows = shard.shape[0]
    half = rows // 2
    own, from_x, from_y, low, high = gather_rest(shard, sides)
    whole = jnp.zeros((4 * rows,) + shard.shape[1:], shard.dtype)
    for piece, start in (
        (own, index * rows),
        (from_x, (index ^ 1) * rows),
        (from_y, (index ^ 2) * rows),
        (low, (index ^ 3) * rows),
        (high, (index ^ 3) * rows + half),
    ):
        whole = lax.dynamic_update_slice(whole, piece, (start, 0))
    return whole


def scatter_terms(whole, index):
    rows = whole.shape[0] // 4
    return [lax.dynamic_slice_in_dim(whole, (index ^ j) * rows, rows) for j in range(4)]


def opening_kernel(
    chips,
    x_ref, vector_ref, routed_ref, mixer_ref, gate_ref,
    gains_ref, tables_ref, row_ref, mixers_ref, last_ref, gates_ref,
    vectors, send_v, receive_v, send_t, receive_t,
    send_n, receive_n, send_g, receive_g,
    up_sem, down_sem, in_low, in_high, to_partner, in_partner, local,
):
    nf, ne = lax.axis_size("fsdp"), lax.axis_size("expert")
    total = nf * ne
    f, e = lax.axis_index("fsdp"), lax.axis_index("expert")
    me = f * ne + e
    z, c = e // 2, lax.rem(e, 2)
    xn, yn = f ^ 1, f ^ 2
    up = (f, jnp.minimum(z + 1, chips - 1) * 2 + c)
    down = (f, jnp.maximum(z - 1, 0) * 2 + c)
    partner = (f, z * 2 + 1 - c)
    parts = ((pl.ds(0, 3), mixers_ref), (pl.ds(3, 1), last_ref))
    own_gate = pltpu.make_async_copy(gate_ref, gates_ref.at[f], local.at[2])
    own_mixer = [
        pltpu.make_async_copy(mixer_ref.at[span], ref.at[:, e], local.at[k])
        for k, (span, ref) in enumerate(parts)
    ]
    for copy in own_mixer + [own_gate]:
        copy.start()
    barrier = pltpu.get_barrier_semaphore()

    def greet(step, carry):
        peer = lax.rem(me + step, total)
        pl.semaphore_signal(
            barrier, inc=1, device_id=(peer // ne, lax.rem(peer, ne)), device_id_type=MESH
        )
        return carry

    lax.fori_loop(1, total, greet, 0)
    pl.semaphore_wait(barrier, total - 1)

    def remote(source, target, send, receive, device):
        return pltpu.make_async_remote_copy(
            src_ref=source,
            dst_ref=target,
            send_sem=send,
            recv_sem=receive,
            device_id=device,
            device_id_type=MESH,
        )

    def vector_copy(slot, peer):
        return remote(
            vector_ref, vectors.at[slot], send_v.at[peer], receive_v.at[slot],
            (peer // ne, lax.rem(peer, ne)),
        )

    def table_copy(slot, peer):
        return remote(routed_ref, tables_ref.at[slot], send_t.at[peer], receive_t.at[slot], (f, peer))

    def start_vector(step, carry):
        vector_copy(me, lax.rem(me + step, total)).start()
        return carry

    def start_table(step, carry):
        table_copy(e, lax.rem(e + step, ne)).start()
        return carry

    lax.fori_loop(1, total, start_vector, 0)
    lax.fori_loop(1, ne, start_table, 0)
    vectors[me] = vector_ref[...]
    tables_ref[e] = routed_ref[...]

    def shard(k, origin, target, send, receive, own):
        span, ref = parts[k]
        place = ref.at[:, origin * 2 + c]
        return remote(mixer_ref.at[span] if own else place, place, send, receive, target)

    def upward(k, origin, r, own=False):
        return shard(k, origin, up, up_sem.at[k, r], in_low.at[k, r], own)

    def downward(k, origin, r, own=False):
        return shard(k, origin, down, down_sem.at[k, r], in_high.at[k, r], own)

    def across(k, origin, own=False):
        return shard(k, origin, partner, to_partner.at[k, origin], in_partner.at[k, origin], own)

    for k in (0, 1):

        @pl.when(z < chips - 1)
        def _():
            upward(k, z, 0, True).start()

        @pl.when(z > 0)
        def _():
            downward(k, z, 0, True).start()

        across(k, z, True).start()

    def end_vector(step, carry):
        peer = lax.rem(me + step, total)
        vector_copy(peer, peer).wait_recv()
        return carry

    lax.fori_loop(1, total, end_vector, 0)
    blocks = gains_ref.shape[1] // 128
    per = total // blocks
    for block in range(blocks):
        gains_ref[:, block * 128 : (block + 1) * 128] = jnp.sum(
            vectors[block * per : (block + 1) * per], axis=0
        )
    half = x_ref.shape[0] // 2
    low, high = pl.ds(0, half), pl.ds(half, half)

    def piece(index, ref, origin, rows, device, slot):
        send, receive = (send_n, receive_n) if index == 0 else (send_g, receive_g)
        here, there = (origin ^ f, origin ^ device) if index == 0 else (origin, origin)
        return remote(
            ref.at[here, rows], ref.at[there, rows], send.at[slot], receive.at[slot], (device, e)
        )

    def arrived(index, ref, origin, rows, slot):
        send, receive = (send_n, receive_n) if index == 0 else (send_g, receive_g)
        place = ref.at[origin ^ f if index == 0 else origin, rows]
        return remote(place, place, send.at[slot], receive.at[slot], (xn, e))

    def outgoing(index, ref, first, second):
        return [
            piece(index, ref, f, first, xn, 0),
            piece(index, ref, f, second, yn, 1),
            piece(index, ref, f, second, xn, 2),
            piece(index, ref, f, first, yn, 3),
        ]

    def relays(index, ref, first, second):
        return [piece(index, ref, xn, first, yn, 4), piece(index, ref, yn, second, xn, 5)]

    for rows in (low, high):
        values = x_ref[rows].astype(F32)
        scale = lax.rsqrt(jnp.mean(values * values, axis=1, keepdims=True) + EPSILON)
        row_ref[0, rows] = (values * scale * gains_ref[0:1]).astype(BF16)
    own_gate.wait()
    row_out = outgoing(0, row_ref, low, high)
    row_relay = relays(0, row_ref, low, high)
    depth = gate_ref.shape[0] // 2
    first, second = pl.ds(0, depth), pl.ds(depth, depth)
    gate_out = outgoing(1, gates_ref, first, second)
    gate_relay = relays(1, gates_ref, first, second)
    for copy in row_out + gate_out:
        copy.start()
    arrived(0, row_ref, xn, low, 0).wait_recv()
    row_relay[0].start()
    arrived(0, row_ref, yn, high, 1).wait_recv()
    row_relay[1].start()

    def hop(r, carry):
        before, after = z - r, z + r
        for k in (0, 1):

            @pl.when(before >= 0)
            def _():
                upward(k, before, r - 1).wait_recv()

                @pl.when(z < chips - 1)
                def _():
                    upward(k, before, r).start()

                across(k, before).start()

            @pl.when(after < chips)
            def _():
                downward(k, after, r - 1).wait_recv()

                @pl.when(z > 0)
                def _():
                    downward(k, after, r).start()

                across(k, after).start()

        return carry

    lax.fori_loop(1, 3, hop, 0)
    arrived(1, gates_ref, xn, first, 0).wait_recv()
    gate_relay[0].start()
    arrived(1, gates_ref, yn, second, 1).wait_recv()
    gate_relay[1].start()
    lax.fori_loop(3, chips, hop, 0)

    for index, ref, (one, two) in ((0, row_ref, (low, high)), (1, gates_ref, (first, second))):
        arrived(index, ref, xn, two, 2).wait_recv()
        arrived(index, ref, yn, one, 3).wait_recv()
        arrived(index, ref, f ^ 3, one, 4).wait_recv()
        arrived(index, ref, f ^ 3, two, 5).wait_recv()
    for copy in row_out + gate_out + row_relay + gate_relay:
        copy.wait_send()
    for k in (0, 1):
        own_mixer[k].wait()

        @pl.when(z < chips - 1)
        def _():
            upward(k, z, 0, True).wait_send()

        @pl.when(z > 0)
        def _():
            downward(k, z, 0, True).wait_send()

    def finish(r, carry):
        before, after = z - r, z + r
        for k in (0, 1):

            @pl.when((before >= 0) & (z < chips - 1))
            def _():
                upward(k, before, r).wait_send()

            @pl.when((after < chips) & (z > 0))
            def _():
                downward(k, after, r).wait_send()

        return carry

    lax.fori_loop(1, chips, finish, 0)

    def shared(origin, carry):
        for k in (0, 1):
            across(k, origin).wait_send()
            across(k, origin).wait_recv()
        return carry

    lax.fori_loop(0, chips, shared, 0)

    def sent_vector(step, carry):
        peer = lax.rem(me + step, total)
        vector_copy(peer, peer).wait_send()
        return carry

    def end_table(step, carry):
        peer = lax.rem(e + step, ne)
        copy = table_copy(peer, peer)
        copy.wait_recv()
        copy.wait_send()
        return carry

    lax.fori_loop(1, total, sent_vector, 0)
    lax.fori_loop(1, ne, end_table, 0)


def opening(x, vector, routed, mixer, gate, nf):
    ne = routed.shape[0]
    chips, devices = ne // 2, nf * ne
    whole = pl.BlockSpec(memory_space=pltpu.VMEM)
    far = pl.BlockSpec(memory_space=pl.ANY)
    dma = pltpu.SemaphoreType.DMA
    return pl.pallas_call(
        functools.partial(opening_kernel, chips),
        out_shape=[
            jax.ShapeDtypeStruct((8, x.shape[1]), F32),
            jax.ShapeDtypeStruct((ne,) + routed.shape, F32),
            jax.ShapeDtypeStruct((nf,) + x.shape, BF16),
            jax.ShapeDtypeStruct((3, ne) + mixer.shape[1:], BF16),
            jax.ShapeDtypeStruct((1, ne) + mixer.shape[1:], BF16),
            jax.ShapeDtypeStruct((nf,) + gate.shape, BF16),
        ],
        in_specs=[whole] * 5,
        out_specs=[whole, whole, whole, far, far, far],
        scratch_shapes=[pltpu.VMEM((devices,) + vector.shape, F32)]
        + [dma((devices,))] * 2
        + [dma((ne,))] * 2
        + [dma((6,))] * 4
        + [dma((2, chips))] * 6
        + [dma((3,))],
        compiler_params=pltpu.CompilerParams(
            collective_id=1, has_side_effects=True, vmem_limit_bytes=60 * 1024 * 1024
        ),
        name="opening",
    )(x, vector, routed, mixer, gate)


def collect_kernel(terms_ref, sum_ref, arrived, send, receive):
    nf, ne = lax.axis_size("fsdp"), lax.axis_size("expert")
    total = nf * ne
    me = lax.axis_index("fsdp") * ne + lax.axis_index("expert")
    barrier = pltpu.get_barrier_semaphore()

    def greet(step, carry):
        peer = lax.rem(me + step, total)
        pl.semaphore_signal(
            barrier, inc=1, device_id=(peer // ne, lax.rem(peer, ne)), device_id_type=MESH
        )
        return carry

    lax.fori_loop(1, total, greet, 0)
    pl.semaphore_wait(barrier, total - 1)

    def copy_of(slot, peer):
        return pltpu.make_async_remote_copy(
            src_ref=terms_ref.at[peer],
            dst_ref=arrived.at[slot],
            send_sem=send.at[peer],
            recv_sem=receive.at[slot],
            device_id=(peer // ne, lax.rem(peer, ne)),
            device_id_type=MESH,
        )

    def begin(step, carry):
        copy_of(me, lax.rem(me + step, total)).start()
        return carry

    lax.fori_loop(1, total, begin, 0)
    arrived[me] = terms_ref[me]

    def end(step, carry):
        peer = lax.rem(me + step, total)
        copy = copy_of(peer, peer)
        copy.wait_recv()
        copy.wait_send()
        return carry

    lax.fori_loop(1, total, end, 0)
    sum_ref[...] = jnp.sum(arrived[...], axis=0)


def collect(terms):
    devices = terms.shape[0]
    return pl.pallas_call(
        collect_kernel,
        out_shape=jax.ShapeDtypeStruct(terms.shape[1:], terms.dtype),
        in_specs=[pl.BlockSpec(memory_space=pltpu.VMEM)],
        out_specs=pl.BlockSpec(memory_space=pltpu.VMEM),
        scratch_shapes=[pltpu.VMEM(terms.shape, terms.dtype)]
        + [pltpu.SemaphoreType.DMA((devices,))] * 2,
        compiler_params=pltpu.CompilerParams(collective_id=2, has_side_effects=True),
        name="collect",
    )(terms)


def places(chips):
    f, e = lax.axis_index("fsdp"), lax.axis_index("expert")
    z, c = e // 2, lax.rem(e, 2)
    up = (f, jnp.minimum(z + 1, chips - 1) * 2 + c)
    down = (f, jnp.maximum(z - 1, 0) * 2 + c)
    return f, e, z, c, up, down, (f, z * 2 + 1 - c), (f ^ 1, e), (f ^ 2, e)


def meet(chips, z, up, down, others):
    barrier = pltpu.get_barrier_semaphore()
    for peer in others:
        pl.semaphore_signal(barrier, inc=1, device_id=peer, device_id_type=MESH)

    @pl.when(z < chips - 1)
    def _():
        pl.semaphore_signal(barrier, inc=1, device_id=up, device_id_type=MESH)

    @pl.when(z > 0)
    def _():
        pl.semaphore_signal(barrier, inc=1, device_id=down, device_id_type=MESH)

    known = len(others) + jnp.where(z < chips - 1, 1, 0) + jnp.where(z > 0, 1, 0)
    pl.semaphore_wait(barrier, known)


def remote_copy(source, target, send, receive, device):
    return pltpu.make_async_remote_copy(
        src_ref=source,
        dst_ref=target,
        send_sem=send,
        recv_sem=receive,
        device_id=device,
        device_id_type=MESH,
    )


def spread_kernel(
    chips, block_ref, tokens_ref, all_ref, row_ref,
    up_sem, down_sem, in_low, in_high, to_partner, in_partner, send_n, receive_n, local,
):
    f, e, z, c, up, down, partner, side_x, side_y = places(chips)
    xn, yn = f ^ 1, f ^ 2
    own = [
        pltpu.make_async_copy(block_ref, all_ref.at[e], local.at[0]),
        pltpu.make_async_copy(tokens_ref, row_ref.at[0], local.at[1]),
    ]
    for copy in own:
        copy.start()
    meet(chips, z, up, down, (partner, side_x, side_y))

    def shard(origin, target, send, receive, first):
        place = all_ref.at[origin * 2 + c]
        return remote_copy(block_ref if first else place, place, send, receive, target)

    def upward(origin, r, first=False):
        return shard(origin, up, up_sem.at[r], in_low.at[r], first)

    def downward(origin, r, first=False):
        return shard(origin, down, down_sem.at[r], in_high.at[r], first)

    def across(origin, first=False):
        return shard(origin, partner, to_partner.at[origin], in_partner.at[origin], first)

    @pl.when(z < chips - 1)
    def _():
        upward(z, 0, True).start()

    @pl.when(z > 0)
    def _():
        downward(z, 0, True).start()

    across(z, True).start()
    half = tokens_ref.shape[0] // 2
    low, high = pl.ds(0, half), pl.ds(half, half)

    def piece(origin, rows, device, slot):
        source = tokens_ref.at[rows] if slot < 4 else row_ref.at[origin ^ f, rows]
        return remote_copy(
            source, row_ref.at[origin ^ device, rows], send_n.at[slot], receive_n.at[slot], (device, e)
        )

    def arrived(origin, rows, slot):
        place = row_ref.at[origin ^ f, rows]
        return remote_copy(place, place, send_n.at[slot], receive_n.at[slot], side_x)

    copies = [piece(f, low, xn, 0), piece(f, high, yn, 1), piece(f, high, xn, 2), piece(f, low, yn, 3)]
    relays = [piece(xn, low, yn, 4), piece(yn, high, xn, 5)]
    for copy in copies:
        copy.start()
    arrived(xn, low, 0).wait_recv()
    relays[0].start()
    arrived(yn, high, 1).wait_recv()
    relays[1].start()

    def hop(r, carry):
        before, after = z - r, z + r

        @pl.when(before >= 0)
        def _():
            upward(before, r - 1).wait_recv()

            @pl.when(z < chips - 1)
            def _():
                upward(before, r).start()

            across(before).start()

        @pl.when(after < chips)
        def _():
            downward(after, r - 1).wait_recv()

            @pl.when(z > 0)
            def _():
                downward(after, r).start()

            across(after).start()

        return carry

    lax.fori_loop(1, chips, hop, 0)
    arrived(xn, high, 2).wait_recv()
    arrived(yn, low, 3).wait_recv()
    arrived(f ^ 3, low, 4).wait_recv()
    arrived(f ^ 3, high, 5).wait_recv()
    for copy in copies + relays:
        copy.wait_send()
    for copy in own:
        copy.wait()

    @pl.when(z < chips - 1)
    def _():
        upward(z, 0, True).wait_send()

    @pl.when(z > 0)
    def _():
        downward(z, 0, True).wait_send()

    def finish(r, carry):
        before, after = z - r, z + r

        @pl.when((before >= 0) & (z < chips - 1))
        def _():
            upward(before, r).wait_send()

        @pl.when((after < chips) & (z > 0))
        def _():
            downward(after, r).wait_send()

        return carry

    lax.fori_loop(1, chips, finish, 0)

    def shared(origin, carry):
        across(origin).wait_send()
        across(origin).wait_recv()
        return carry

    lax.fori_loop(0, chips, shared, 0)


def spread(block, tokens, nf, ne, cid):
    chips = ne // 2
    dma = pltpu.SemaphoreType.DMA
    return pl.pallas_call(
        functools.partial(spread_kernel, chips),
        out_shape=[
            jax.ShapeDtypeStruct((ne,) + block.shape, block.dtype),
            jax.ShapeDtypeStruct((nf,) + tokens.shape, tokens.dtype),
        ],
        in_specs=[pl.BlockSpec(memory_space=pltpu.VMEM)] * 2,
        out_specs=[pl.BlockSpec(memory_space=pltpu.VMEM)] * 2,
        scratch_shapes=[dma((chips,))] * 6 + [dma((6,))] * 2 + [dma((2,))],
        compiler_params=pltpu.CompilerParams(
            collective_id=cid, has_side_effects=True, vmem_limit_bytes=40 * 1024 * 1024
        ),
        cost_estimate=WIRE,
        name=f"spread{cid}",
    )(block, tokens)


def combine_kernel(
    chips, terms_ref, parts_ref, sum_ref, row_sum_ref,
    theirs, going, coming, corner, onward, from_side,
    up_sem, down_sem, in_low, in_high, to_partner, in_partner, send_n, receive_n,
):
    f, e, z, c, up, down, partner, side_x, side_y = places(chips)
    meet(chips, z, up, down, (partner, side_x, side_y))

    def across(target):
        return remote_copy(
            terms_ref.at[target * 2 + 1 - c], theirs.at[target],
            to_partner.at[target], in_partner.at[target], partner,
        )

    def upward(target):
        return remote_copy(
            going.at[target], coming.at[target], up_sem.at[target], in_low.at[target], up
        )

    def downward(target, receiver):
        place = coming.at[jnp.where(target == receiver, chips, target)]
        return remote_copy(
            going.at[target], place, down_sem.at[target], in_high.at[target], down
        )

    def offer(r, carry):
        across(r).start()
        across(chips - 1 - r).start()
        return carry

    lax.fori_loop(0, chips // 2, offer, 0)
    half = parts_ref.shape[1] // 2
    low, high = pl.ds(0, half), pl.ds(half, half)

    def side(slot, source, target, device):
        return remote_copy(source, target, send_n.at[slot], receive_n.at[slot], device)

    copies = [
        side(0, parts_ref.at[3, low], corner.at[0], side_x),
        side(1, parts_ref.at[3, high], corner.at[1], side_y),
        side(2, parts_ref.at[1, low], from_side.at[0, low], side_x),
        side(3, parts_ref.at[2, high], from_side.at[1, high], side_y),
        side(4, onward.at[0], from_side.at[0, high], side_x),
        side(5, onward.at[1], from_side.at[1, low], side_y),
    ]
    for copy in copies[:4]:
        copy.start()

    def chip_term(target):
        return terms_ref[target * 2 + c].astype(F32) + theirs[target].astype(F32)

    def rise(r):
        target = chips - 1 - r

        @pl.when(target > z)
        def _():
            across(target).wait_recv()

            @pl.when(z > 0)
            def _():
                upward(target).wait_recv()
                going[target] = (chip_term(target) + coming[target].astype(F32)).astype(BF16)

            @pl.when(z == 0)
            def _():
                going[target] = chip_term(target).astype(BF16)

            upward(target).start()

    def fall(r):
        @pl.when(r < z)
        def _():
            across(r).wait_recv()

            @pl.when(z < chips - 1)
            def _():
                downward(r, z).wait_recv()
                going[r] = (chip_term(r) + coming[r].astype(F32)).astype(BF16)

            @pl.when(z == chips - 1)
            def _():
                going[r] = chip_term(r).astype(BF16)

            downward(r, z - 1).start()

    def pass_on(r, carry):
        @pl.when(z < chips // 2)
        def _():
            rise(r)

        fall(r)

        @pl.when(z >= chips // 2)
        def _():
            rise(r)

        return carry

    lax.fori_loop(0, 1, pass_on, 0)
    copies[1].wait_recv()
    onward[0] = (parts_ref[1, high].astype(F32) + corner[1].astype(F32)).astype(BF16)
    copies[4].start()
    copies[0].wait_recv()
    onward[1] = (parts_ref[2, low].astype(F32) + corner[0].astype(F32)).astype(BF16)
    copies[5].start()
    lax.fori_loop(1, chips, pass_on, 0)
    for copy in copies[2:]:
        copy.wait_recv()
    row_sum_ref[...] = (
        parts_ref[0].astype(F32) + from_side[0].astype(F32) + from_side[1].astype(F32)
    )
    across(z).wait_recv()
    sum_ref[...] = chip_term(z)

    @pl.when(z > 0)
    def _():
        upward(z).wait_recv()
        sum_ref[...] += coming[z].astype(F32)

    @pl.when(z < chips - 1)
    def _():
        downward(z, z).wait_recv()
        sum_ref[...] += coming[chips].astype(F32)

    for copy in copies:
        copy.wait_send()

    def finish(target, carry):
        across(target).wait_send()

        @pl.when(target > z)
        def _():
            upward(target).wait_send()

        @pl.when(target < z)
        def _():
            downward(target, z - 1).wait_send()

        return carry

    lax.fori_loop(0, chips, finish, 0)


def combine(terms, parts, cid):
    ne = terms.shape[0]
    chips = ne // 2
    parts = parts.reshape(4, parts.shape[0] // 4, parts.shape[1])
    block = terms.shape[1:]
    halves = (2, parts.shape[1] // 2, parts.shape[2])
    sides = (2,) + parts.shape[1:]
    dma = pltpu.SemaphoreType.DMA
    return pl.pallas_call(
        functools.partial(combine_kernel, chips),
        out_shape=[
            jax.ShapeDtypeStruct(terms.shape[1:], F32),
            jax.ShapeDtypeStruct(parts.shape[1:], F32),
        ],
        in_specs=[pl.BlockSpec(memory_space=pltpu.VMEM)] * 2,
        out_specs=[pl.BlockSpec(memory_space=pltpu.VMEM)] * 2,
        scratch_shapes=[pltpu.VMEM((chips,) + block, BF16)] * 2
        + [pltpu.VMEM((chips + 1,) + block, BF16)]
        + [pltpu.VMEM(halves, BF16)] * 2
        + [pltpu.VMEM(sides, BF16)]
        + [dma((chips,))] * 6
        + [dma((6,))] * 2,
        compiler_params=pltpu.CompilerParams(
            collective_id=cid, has_side_effects=True, vmem_limit_bytes=60 * 1024 * 1024
        ),
        cost_estimate=WIRE,
        name=f"combine{cid}",
    )(terms, parts)


def on_device(
    inputs,
    teacher,
    lengths,
    deal_order,
    routes,
    route_weights,
    norm_gains,
    mixer_weights,
    shared_weights,
    shared_gate,
    expert_gate,
    expert_up,
    expert_down,
):
    tokens_dev = inputs.shape[1]
    width = inputs.shape[2]
    nf = lax.axis_size("fsdp")
    ne = lax.axis_size("expert")
    devices = nf * ne
    row_len = tokens_dev * nf
    capacity = 3 * tokens_dev * TOP // (2 * ne)
    total_tokens = row_len * ne
    columns = mixer_weights.shape[2]
    heads_local = columns // HD
    f_index = lax.axis_index("fsdp")
    e_index = lax.axis_index("expert")

    piece = norm_gains.shape[1]
    slot = (f_index * ne + e_index) % (128 // piece)
    vector = jnp.concatenate([norm_gains, shared_gate[None]], axis=0).astype(F32)
    vector = lax.dynamic_update_slice(jnp.zeros((8, 128), F32), vector, (0, slot * piece))
    chosen = routes[0]
    weights_route = route_weights[0]
    expert_ids = jnp.arange(ne, dtype=jnp.int32)
    routed = jnp.sum(
        jnp.where(chosen.T[None] == expert_ids[:, None, None], weights_route.T[None], 0.0), axis=1
    )
    mixer_shard = jnp.transpose(mixer_weights, (1, 0, 2))
    gains, tables, row_blocks, mixer_in, mixer_out, gates = opening(
        inputs[0], vector, routed, mixer_shard, expert_gate[0], nf
    )
    first_gain, second_gain, gate_vector = gains[0], gains[1], gains[2]
    token_weight = lax.dynamic_index_in_dim(tables, e_index, axis=1, keepdims=False)
    mixer_in = mixer_in.reshape(3, width, columns)
    mixer_out = mixer_out.reshape(width, columns)
    gate_rows = gates.reshape(width, gates.shape[2])
    row_normed = row_blocks.reshape(row_len, width)

    shared_shard, up_shard, down_shard, gains = lax.optimization_barrier(
        (shared_weights, expert_up[0], expert_down[0], gains)
    )
    shared_shard = jnp.transpose(shared_shard, (1, 0, 2))
    shared_first = lax.all_gather(shared_shard[0], "expert", axis=0, tiled=True)
    up_sides = gather_sides(up_shard)

    first_len = lengths[deal_order[2 * e_index]]
    second_len = lengths[deal_order[2 * e_index + 1]]
    row_places = (
        (f_index ^ jnp.arange(nf, dtype=jnp.int32))[:, None] * tokens_dev
        + jnp.arange(tokens_dev, dtype=jnp.int32)[None]
    ).reshape(row_len)
    row_segment = (row_places >= first_len).astype(jnp.int32) + (
        row_places >= first_len + second_len
    ).astype(jnp.int32)
    row_position = (
        row_places
        - first_len * (row_segment >= 1).astype(jnp.int32)
        - second_len * (row_segment >= 2).astype(jnp.int32)
    )
    own_segment = row_segment[:tokens_dev]
    allowed = (row_segment[:, None] == row_segment[None, :]) & (
        row_places[None, :] <= row_places[:, None]
    )
    inverse = THETA ** (-(jnp.arange(HD // 2, dtype=F32) * 2.0) / HD)
    angles = row_position.astype(F32)[:, None] * inverse[None, :]
    cosine = jnp.concatenate([jnp.cos(angles)] * 2, axis=1)[:, None, :]
    sine = jnp.concatenate([jnp.sin(angles)] * 2, axis=1)[:, None, :]

    flat_inputs = inputs[0].astype(F32)
    first_scale = lax.rsqrt(jnp.mean(flat_inputs * flat_inputs, axis=1) + EPSILON)
    projected = dot("td,kde->kte", row_normed, mixer_in)

    def heads(values):
        return values.reshape(row_len, heads_local, HD)

    raw_query, raw_key = heads(projected[0]), heads(projected[1])
    queries = (raw_query * cosine + turn(raw_query) * sine).astype(BF16)
    keys = (raw_key * cosine + turn(raw_key) * sine).astype(BF16)
    values = heads(projected[2].astype(BF16))
    score_factor = HD ** (-0.5)

    def score():
        raw = dot("qhd,khd->hqk", queries, keys)
        return jnp.where(allowed[None], raw * score_factor, NEG_LARGE)

    scores = score()
    top_score = jnp.max(scores, axis=2, keepdims=True)
    shifted = jnp.exp(scores - top_score)
    row_total = jnp.sum(shifted, axis=2, keepdims=True)
    probabilities = shifted / row_total
    log_total = top_score + jnp.log(row_total)
    context = dot("hqk,khd->qhd", probabilities.astype(BF16), values)
    context = context.reshape(row_len, columns).astype(BF16)
    attn_out = row_scatter(dot("tc,dc->td", context, mixer_out))
    residual = flat_inputs + attn_out
    second_scale = lax.rsqrt(jnp.mean(residual * residual, axis=1) + EPSILON)
    mixed_in = (residual * second_scale[:, None] * second_gain[None, :]).astype(BF16)

    down_shard, mixed_in = lax.optimization_barrier((down_shard, mixed_in))
    up_rows = gather_shards(up_shard, up_sides, f_index)
    down_rows = gather_shards(down_shard, gather_sides(down_shard), f_index)
    tokens_all, row_mixed = spread(mixed_in, mixed_in, nf, ne, 3)
    row_mixed = row_mixed.reshape(row_len, width)
    second_shard, third_shard, tokens_all = lax.optimization_barrier(
        (shared_shard[1], shared_shard[2], tokens_all)
    )
    shared_second = lax.all_gather(second_shard, "expert", axis=0, tiled=True)
    shared_down = lax.all_gather(third_shard, "expert", axis=0, tiled=True)
    routed_here = token_weight > 0.0
    marks = routed_here.astype(BF16)
    upper = (
        jnp.arange(tokens_dev, dtype=jnp.int32)[:, None]
        <= jnp.arange(tokens_dev, dtype=jnp.int32)[None, :]
    ).astype(BF16)
    order = dot("st,tu->su", marks, upper) - 1.0
    slots = jnp.arange(capacity, dtype=jnp.int32).astype(F32)
    hit = (order[:, None, :] == slots[None, :, None]) & routed_here[:, None, :]
    picker = hit.astype(BF16)
    slot_weight = jnp.sum(jnp.where(hit, token_weight[:, None, :], 0.0), axis=2).reshape(
        ne * capacity, 1
    )

    def pick(blocks):
        return dot("srt,std->srd", picker, blocks).reshape(ne * capacity, width)

    def unpick(rows):
        return dot("srt,srd->std", picker, rows.reshape(ne, capacity, width)).astype(BF16)

    rows_in = pick(tokens_all).astype(BF16)
    gate_pre = dot("rd,df->rf", rows_in, gate_rows)
    up_pre = dot("rd,df->rf", rows_in, up_rows)
    hidden = (jax.nn.silu(gate_pre) * up_pre).astype(BF16)
    result = (slot_weight * dot("rf,fd->rd", hidden, down_rows)).astype(BF16)


    shared_pre = (dot("td,df->tf", row_mixed, shared_first), dot("td,df->tf", row_mixed, shared_second))
    shared_hidden = (jax.nn.silu(shared_pre[0]) * shared_pre[1]).astype(BF16)
    routed_sum, shared_out = combine(
        unpick(result), dot("tf,df->td", shared_hidden, shared_down).astype(BF16), 4
    )
    gate_value = jax.nn.sigmoid(
        jnp.sum(mixed_in.astype(F32) * gate_vector[None, :], axis=1)
    )

    block_total = residual + gate_value[:, None] * shared_out + routed_sum
    out_block = block_total.astype(BF16)[None]
    valid_mask = (own_segment < 2).astype(F32)
    valid_count = jnp.sum(lengths).astype(F32)
    dtotal = (
        total_tokens
        / valid_count
        * valid_mask[:, None]
        * (block_total - teacher[0].astype(F32))
    )

    dshared_out = (gate_value[:, None] * dtotal).astype(BF16)
    dlogit = jnp.sum(dtotal * shared_out, axis=1) * gate_value * (1.0 - gate_value)
    dtotal_all, row_dout = spread(dtotal.astype(BF16), dshared_out, nf, ne, 5)
    row_dout = row_dout.reshape(row_len, width)
    down_term = dot("td,tf->df", row_dout, shared_hidden).astype(BF16)
    row_dout, dtotal_all, down_term = lax.optimization_barrier((row_dout, dtotal_all, down_term))
    shared_sigmoid = jax.nn.sigmoid(shared_pre[0])
    dshared_hidden = dot("td,df->tf", row_dout, shared_down)
    dshared_gate = (
        dshared_hidden * shared_pre[1] * shared_sigmoid * (1.0 + shared_pre[0] * (1.0 - shared_sigmoid))
    ).astype(BF16)
    dshared_up = (dshared_hidden * shared_pre[0] * shared_sigmoid).astype(BF16)
    dmixed_first = dot("tf,df->td", dshared_gate, shared_first)

    def scatter_columns(term):
        return lax.psum_scatter(term.astype(BF16), "expert", scatter_dimension=0, tiled=True)

    grad_shared_down = scatter_columns(down_term)
    gate_term = dot("td,tf->df", row_mixed, dshared_gate).astype(BF16)
    up_term = dot("td,tf->df", row_mixed, dshared_up).astype(BF16)

    dresult = (slot_weight * pick(dtotal_all)).astype(BF16)
    gate_sigmoid = jax.nn.sigmoid(gate_pre)
    activated = gate_pre * gate_sigmoid
    grad_down_term = dot("rf,rd->fd", hidden, dresult).astype(BF16)
    dresult, grad_down_term = lax.optimization_barrier((dresult, grad_down_term))
    terms = [scatter_terms(grad_down_term, f_index)]
    corners = [scatter_corner(terms[0])]
    dhidden = dot("rd,fd->rf", dresult, down_rows)
    dgate = (dhidden * up_pre * gate_sigmoid * (1.0 + gate_pre * (1.0 - gate_sigmoid))).astype(BF16)
    dup = (dhidden * activated).astype(BF16)
    dreturn = (dot("rf,df->rd", dgate, gate_rows) + dot("rf,df->rd", dup, up_rows)).astype(BF16)
    dreturn, corners = lax.optimization_barrier((dreturn, corners))
    sides = [scatter_sides(terms[0], corners[0])]
    grad_gate_term = dot("rd,rf->df", rows_in, dgate).astype(BF16)
    terms.append(scatter_terms(grad_gate_term, f_index))
    corners.append(scatter_corner(terms[1]))
    dmixed_terms = (dmixed_first + dot("tf,df->td", dshared_up, shared_second)).astype(BF16)
    dreturned, up_term, gate_term, corners = lax.optimization_barrier(
        (unpick(dreturn), up_term, gate_term, corners)
    )
    grad_shared_gates = scatter_columns(gate_term)
    sides.append(scatter_sides(terms[1], corners[1]))
    from_experts, dmixed_shared = combine(dreturned, dmixed_terms, 6)
    from_experts, up_term, corners, sides, grad_shared_down = lax.optimization_barrier(
        (from_experts, up_term, corners, sides, grad_shared_down)
    )
    grad_shared_ups = scatter_columns(up_term)

    dmixed = dmixed_shared + dlogit[:, None] * gate_vector[None, :] + from_experts
    vector_term = jnp.sum(dlogit[:, None] * mixed_in.astype(F32), axis=0)
    dresidual_norm, second_gain_grad = norm_back(dmixed, residual, second_scale, second_gain)
    dresidual = dtotal + dresidual_norm
    dattn = dresidual.astype(BF16)
    dattn, rows_again, dup = lax.optimization_barrier((dattn, rows_in, dup))
    row_dattn = row_tokens(dattn)
    grad_up_term = dot("rd,rf->df", rows_again, dup).astype(BF16)
    row_dattn, grad_up_term, grad_shared_gates = lax.optimization_barrier(
        (row_dattn, grad_up_term, grad_shared_gates)
    )
    terms.append(scatter_terms(grad_up_term, f_index))
    corners.append(scatter_corner(terms[2]))

    dcontext = dot("td,dc->tc", row_dattn, mixer_out).astype(BF16)
    mixer_out_term = dot("td,tc->dc", row_dattn, context).astype(BF16)
    mixer_base = jnp.pad(mixer_out_term[None], ((3, 0), (0, 0), (0, 0)))
    dcontext, mixer_base = lax.optimization_barrier((dcontext, mixer_base))
    dcontext = heads(dcontext)
    probabilities_again = jnp.exp(score() - log_total)
    dprobs = dot("qhd,khd->hqk", dcontext, values)
    delta_rows = jnp.sum(probabilities_again * dprobs, axis=2, keepdims=True)
    dscores = (probabilities_again * (dprobs - delta_rows)).astype(BF16)
    dqueries = dot("hqk,khd->qhd", dscores, keys) * score_factor
    dkeys = dot("hqk,qhd->khd", dscores, queries) * score_factor
    dvalues = dot("hqk,qhd->khd", probabilities_again.astype(BF16), dcontext)

    def back(incoming):
        return (incoming * cosine + turn_back(incoming * sine)).reshape(row_len, columns)

    dprojected = jnp.stack(
        [back(dqueries), back(dkeys), dvalues.reshape(row_len, columns)], axis=0
    ).astype(BF16)
    dprojected, corners[2] = lax.optimization_barrier((dprojected, corners[2]))
    sides.append(scatter_sides(terms[2], corners[2]))
    mixer_term = dot("td,kte->kde", row_normed, dprojected).astype(BF16)
    mixer_term = lax.dynamic_update_slice(mixer_base, mixer_term, (0, 0, 0))
    mixer_term, grad_shared_ups = lax.optimization_barrier((mixer_term, grad_shared_ups))
    grad_mixer = lax.psum_scatter(mixer_term, "expert", scatter_dimension=1, tiled=True)
    dnormed = dot("kte,kde->td", dprojected, mixer_in).astype(BF16)
    dnormed, sides[2] = lax.optimization_barrier((row_scatter(dnormed), sides[2]))
    grad_expert_down, grad_expert_gate, grad_expert_up = [
        scatter_end(parts, side)[None] for parts, side in zip(terms, sides)
    ]
    dflat, first_gain_grad = norm_back(dnormed, flat_inputs, first_scale, first_gain)
    grad_input = (dresidual + dflat)[None]

    grad_shared = jnp.stack([grad_shared_gates, grad_shared_ups, grad_shared_down], axis=1)
    grad_shared = grad_shared.astype(F32)
    terms = jnp.stack([first_gain_grad, second_gain_grad, vector_term]).reshape(3, devices, piece)
    terms = jnp.pad(jnp.transpose(terms, (1, 0, 2)), ((0, 0), (0, 5), (0, 128 - piece)))
    sums = collect(terms)
    (grad_mixer, sums, grad_shared, grad_expert_down, grad_expert_gate, grad_expert_up) = (
        lax.optimization_barrier(
            (grad_mixer, sums, grad_shared, grad_expert_down, grad_expert_gate, grad_expert_up)
        )
    )
    grad_mixer = jnp.transpose(grad_mixer, (1, 0, 2)).astype(F32)
    grad_gains = sums[:2, :piece]
    grad_shared_gate = sums[2, :piece]
    return (
        out_block,
        grad_input,
        grad_gains,
        grad_mixer,
        grad_shared,
        grad_shared_gate,
        grad_expert_gate,
        grad_expert_up,
        grad_expert_down,
    )


def solution(mesh):
    rows = P("expert", "fsdp", None)
    both = P(("fsdp", "expert"))
    gains = P(None, ("fsdp", "expert"))
    shared = P("expert", None, "fsdp")
    return jax.shard_map(
        on_device,
        mesh=mesh,
        in_specs=(rows, rows, P(), P(), rows, rows, gains, shared, shared, both, rows, rows, rows),
        out_specs=(rows, rows, gains, shared, shared, both, rows, rows, rows),
        check_vma=False,
    )
```

```python
import functools

import jax
import jax.numpy as jnp
from jax import lax
from jax.experimental import pallas as pl
from jax.experimental.pallas import tpu as pltpu
from jax.sharding import PartitionSpec as P

HD = 128
TOP = 4
THETA = 1000000.0
EPSILON = 1e-06
NEG_LARGE = -1e30
MESH = pl.DeviceIdType.MESH
WIRE = pl.CostEstimate(flops=0, bytes_accessed=120_000_000, transcendentals=0)
F32 = jnp.float32
BF16 = jnp.bfloat16


def turn(values):
    half = values.shape[-1] // 2
    return jnp.concatenate([-values[..., half:], values[..., :half]], axis=-1)


def turn_back(values):
    half = values.shape[-1] // 2
    return jnp.concatenate([values[..., half:], -values[..., :half]], axis=-1)


def norm_back(incoming, values, scale_rows, gain_row):
    unit_rows = values * scale_rows[:, None]
    gain_grad = jnp.sum(incoming * unit_rows, axis=0)
    dunit = incoming * gain_row[None, :]
    back_rows = scale_rows[:, None] * (
        dunit - unit_rows * jnp.mean(dunit * unit_rows, axis=1, keepdims=True)
    )
    return (back_rows, gain_grad)


def dot(form, left, right):
    return jnp.einsum(form, left, right, preferred_element_type=F32)


def swap_x(values):
    return lax.ppermute(values, "fsdp", [(0, 1), (1, 0), (2, 3), (3, 2)])


def swap_y(values):
    return lax.ppermute(values, "fsdp", [(0, 2), (2, 0), (1, 3), (3, 1)])


def gather_sides(block):
    return [swap_x(block), swap_y(block)]


def gather_rest(block, sides):
    half = block.shape[0] // 2
    return [block, *sides, swap_y(sides[0][:half]), swap_x(sides[1][half:])]


def scatter_corner(parts):
    half = parts[0].shape[0] // 2
    return [swap_x(parts[3][:half].astype(BF16)), swap_y(parts[3][half:].astype(BF16))]


def scatter_sides(parts, corner):
    half = parts[0].shape[0] // 2
    low, high = corner
    to_y = jnp.concatenate(
        [(parts[2][:half].astype(F32) + low.astype(F32)).astype(BF16), parts[2][half:].astype(BF16)]
    )
    to_x = jnp.concatenate(
        [parts[1][:half].astype(BF16), (parts[1][half:].astype(F32) + high.astype(F32)).astype(BF16)]
    )
    return [swap_x(to_x), swap_y(to_y)]


def scatter_end(parts, sides):
    return parts[0].astype(F32) + sides[0].astype(F32) + sides[1].astype(F32)


def square_scatter(parts):
    return scatter_end(parts, scatter_sides(parts, scatter_corner(parts)))


def row_tokens(block):
    return jnp.concatenate(gather_rest(block, gather_sides(block)), axis=0)


def row_scatter(product):
    quarter = product.shape[0] // 4
    return square_scatter([product[j * quarter : (j + 1) * quarter] for j in range(4)])


def gather_shards(shard, sides, index):
    rows = shard.shape[0]
    half = rows // 2
    own, from_x, from_y, low, high = gather_rest(shard, sides)
    whole = jnp.zeros((4 * rows,) + shard.shape[1:], shard.dtype)
    for piece, start in (
        (own, index * rows),
        (from_x, (index ^ 1) * rows),
        (from_y, (index ^ 2) * rows),
        (low, (index ^ 3) * rows),
        (high, (index ^ 3) * rows + half),
    ):
        whole = lax.dynamic_update_slice(whole, piece, (start, 0))
    return whole


def scatter_terms(whole, index):
    rows = whole.shape[0] // 4
    return [lax.dynamic_slice_in_dim(whole, (index ^ j) * rows, rows) for j in range(4)]


def opening_kernel(
    chips,
    x_ref, vector_ref, routed_ref, mixer_ref, gate_ref,
    gains_ref, tables_ref, row_ref, mixers_ref, last_ref, gates_ref,
    vectors, send_v, receive_v, send_t, receive_t,
    send_n, receive_n, send_g, receive_g,
    up_sem, down_sem, in_low, in_high, to_partner, in_partner, local,
):
    nf, ne = lax.axis_size("fsdp"), lax.axis_size("expert")
    total = nf * ne
    f, e = lax.axis_index("fsdp"), lax.axis_index("expert")
    me = f * ne + e
    z, c = e // 2, lax.rem(e, 2)
    xn, yn = f ^ 1, f ^ 2
    up = (f, jnp.minimum(z + 1, chips - 1) * 2 + c)
    down = (f, jnp.maximum(z - 1, 0) * 2 + c)
    partner = (f, z * 2 + 1 - c)
    parts = ((pl.ds(0, 3), mixers_ref), (pl.ds(3, 1), last_ref))
    own_gate = pltpu.make_async_copy(gate_ref, gates_ref.at[f], local.at[2])
    own_mixer = [
        pltpu.make_async_copy(mixer_ref.at[span], ref.at[:, e], local.at[k])
        for k, (span, ref) in enumerate(parts)
    ]
    for copy in own_mixer + [own_gate]:
        copy.start()
    barrier = pltpu.get_barrier_semaphore()

    def greet(step, carry):
        peer = lax.rem(me + step, total)
        pl.semaphore_signal(
            barrier, inc=1, device_id=(peer // ne, lax.rem(peer, ne)), device_id_type=MESH
        )
        return carry

    lax.fori_loop(1, total, greet, 0)
    pl.semaphore_wait(barrier, total - 1)

    def remote(source, target, send, receive, device):
        return pltpu.make_async_remote_copy(
            src_ref=source,
            dst_ref=target,
            send_sem=send,
            recv_sem=receive,
            device_id=device,
            device_id_type=MESH,
        )

    def vector_copy(slot, peer):
        return remote(
            vector_ref, vectors.at[slot], send_v.at[peer], receive_v.at[slot],
            (peer // ne, lax.rem(peer, ne)),
        )

    def table_copy(slot, peer):
        return remote(routed_ref, tables_ref.at[slot], send_t.at[peer], receive_t.at[slot], (f, peer))

    def start_vector(step, carry):
        vector_copy(me, lax.rem(me + step, total)).start()
        return carry

    def start_table(step, carry):
        table_copy(e, lax.rem(e + step, ne)).start()
        return carry

    lax.fori_loop(1, total, start_vector, 0)
    lax.fori_loop(1, ne, start_table, 0)
    vectors[me] = vector_ref[...]
    tables_ref[e] = routed_ref[...]

    def shard(k, origin, target, send, receive, own):
        span, ref = parts[k]
        place = ref.at[:, origin * 2 + c]
        return remote(mixer_ref.at[span] if own else place, place, send, receive, target)

    def upward(k, origin, r, own=False):
        return shard(k, origin, up, up_sem.at[k, r], in_low.at[k, r], own)

    def downward(k, origin, r, own=False):
        return shard(k, origin, down, down_sem.at[k, r], in_high.at[k, r], own)

    def across(k, origin, own=False):
        return shard(k, origin, partner, to_partner.at[k, origin], in_partner.at[k, origin], own)

    for k in (0, 1):

        @pl.when(z < chips - 1)
        def _():
            upward(k, z, 0, True).start()

        @pl.when(z > 0)
        def _():
            downward(k, z, 0, True).start()

        across(k, z, True).start()

    def end_vector(step, carry):
        peer = lax.rem(me + step, total)
        vector_copy(peer, peer).wait_recv()
        return carry

    lax.fori_loop(1, total, end_vector, 0)
    blocks = gains_ref.shape[1] // 128
    per = total // blocks
    for block in range(blocks):
        gains_ref[:, block * 128 : (block + 1) * 128] = jnp.sum(
            vectors[block * per : (block + 1) * per], axis=0
        )
    half = x_ref.shape[0] // 2
    low, high = pl.ds(0, half), pl.ds(half, half)

    def piece(index, ref, origin, rows, device, slot):
        send, receive = (send_n, receive_n) if index == 0 else (send_g, receive_g)
        here, there = (origin ^ f, origin ^ device) if index == 0 else (origin, origin)
        return remote(
            ref.at[here, rows], ref.at[there, rows], send.at[slot], receive.at[slot], (device, e)
        )

    def arrived(index, ref, origin, rows, slot):
        send, receive = (send_n, receive_n) if index == 0 else (send_g, receive_g)
        place = ref.at[origin ^ f if index == 0 else origin, rows]
        return remote(place, place, send.at[slot], receive.at[slot], (xn, e))

    def outgoing(index, ref, first, second):
        return [
            piece(index, ref, f, first, xn, 0),
            piece(index, ref, f, second, yn, 1),
            piece(index, ref, f, second, xn, 2),
            piece(index, ref, f, first, yn, 3),
        ]

    def relays(index, ref, first, second):
        return [piece(index, ref, xn, first, yn, 4), piece(index, ref, yn, second, xn, 5)]

    for rows in (low, high):
        values = x_ref[rows].astype(F32)
        scale = lax.rsqrt(jnp.mean(values * values, axis=1, keepdims=True) + EPSILON)
        row_ref[0, rows] = (values * scale * gains_ref[0:1]).astype(BF16)
    own_gate.wait()
    row_out = outgoing(0, row_ref, low, high)
    row_relay = relays(0, row_ref, low, high)
    depth = gate_ref.shape[0] // 2
    first, second = pl.ds(0, depth), pl.ds(depth, depth)
    gate_out = outgoing(1, gates_ref, first, second)
    gate_relay = relays(1, gates_ref, first, second)
    for copy in row_out + gate_out:
        copy.start()
    arrived(0, row_ref, xn, low, 0).wait_recv()
    row_relay[0].start()
    arrived(0, row_ref, yn, high, 1).wait_recv()
    row_relay[1].start()

    def hop(r, carry):
        before, after = z - r, z + r
        for k in (0, 1):

            @pl.when(before >= 0)
            def _():
                upward(k, before, r - 1).wait_recv()

                @pl.when(z < chips - 1)
                def _():
                    upward(k, before, r).start()

                across(k, before).start()

            @pl.when(after < chips)
            def _():
                downward(k, after, r - 1).wait_recv()

                @pl.when(z > 0)
                def _():
                    downward(k, after, r).start()

                across(k, after).start()

        return carry

    lax.fori_loop(1, 3, hop, 0)
    arrived(1, gates_ref, xn, first, 0).wait_recv()
    gate_relay[0].start()
    arrived(1, gates_ref, yn, second, 1).wait_recv()
    gate_relay[1].start()
    lax.fori_loop(3, chips, hop, 0)

    for index, ref, (one, two) in ((0, row_ref, (low, high)), (1, gates_ref, (first, second))):
        arrived(index, ref, xn, two, 2).wait_recv()
        arrived(index, ref, yn, one, 3).wait_recv()
        arrived(index, ref, f ^ 3, one, 4).wait_recv()
        arrived(index, ref, f ^ 3, two, 5).wait_recv()
    for copy in row_out + gate_out + row_relay + gate_relay:
        copy.wait_send()
    for k in (0, 1):
        own_mixer[k].wait()

        @pl.when(z < chips - 1)
        def _():
            upward(k, z, 0, True).wait_send()

        @pl.when(z > 0)
        def _():
            downward(k, z, 0, True).wait_send()

    def finish(r, carry):
        before, after = z - r, z + r
        for k in (0, 1):

            @pl.when((before >= 0) & (z < chips - 1))
            def _():
                upward(k, before, r).wait_send()

            @pl.when((after < chips) & (z > 0))
            def _():
                downward(k, after, r).wait_send()

        return carry

    lax.fori_loop(1, chips, finish, 0)

    def shared(origin, carry):
        for k in (0, 1):
            across(k, origin).wait_send()
            across(k, origin).wait_recv()
        return carry

    lax.fori_loop(0, chips, shared, 0)

    def sent_vector(step, carry):
        peer = lax.rem(me + step, total)
        vector_copy(peer, peer).wait_send()
        return carry

    def end_table(step, carry):
        peer = lax.rem(e + step, ne)
        copy = table_copy(peer, peer)
        copy.wait_recv()
        copy.wait_send()
        return carry

    lax.fori_loop(1, total, sent_vector, 0)
    lax.fori_loop(1, ne, end_table, 0)


def opening(x, vector, routed, mixer, gate, nf):
    ne = routed.shape[0]
    chips, devices = ne // 2, nf * ne
    whole = pl.BlockSpec(memory_space=pltpu.VMEM)
    far = pl.BlockSpec(memory_space=pl.ANY)
    dma = pltpu.SemaphoreType.DMA
    return pl.pallas_call(
        functools.partial(opening_kernel, chips),
        out_shape=[
            jax.ShapeDtypeStruct((8, x.shape[1]), F32),
            jax.ShapeDtypeStruct((ne,) + routed.shape, F32),
            jax.ShapeDtypeStruct((nf,) + x.shape, BF16),
            jax.ShapeDtypeStruct((3, ne) + mixer.shape[1:], BF16),
            jax.ShapeDtypeStruct((1, ne) + mixer.shape[1:], BF16),
            jax.ShapeDtypeStruct((nf,) + gate.shape, BF16),
        ],
        in_specs=[whole] * 5,
        out_specs=[whole, whole, whole, far, far, far],
        scratch_shapes=[pltpu.VMEM((devices,) + vector.shape, F32)]
        + [dma((devices,))] * 2
        + [dma((ne,))] * 2
        + [dma((6,))] * 4
        + [dma((2, chips))] * 6
        + [dma((3,))],
        compiler_params=pltpu.CompilerParams(
            collective_id=1, has_side_effects=True, vmem_limit_bytes=60 * 1024 * 1024
        ),
        name="opening",
    )(x, vector, routed, mixer, gate)


def collect_kernel(terms_ref, sum_ref, arrived, send, receive):
    nf, ne = lax.axis_size("fsdp"), lax.axis_size("expert")
    total = nf * ne
    me = lax.axis_index("fsdp") * ne + lax.axis_index("expert")
    barrier = pltpu.get_barrier_semaphore()

    def greet(step, carry):
        peer = lax.rem(me + step, total)
        pl.semaphore_signal(
            barrier, inc=1, device_id=(peer // ne, lax.rem(peer, ne)), device_id_type=MESH
        )
        return carry

    lax.fori_loop(1, total, greet, 0)
    pl.semaphore_wait(barrier, total - 1)

    def copy_of(slot, peer):
        return pltpu.make_async_remote_copy(
            src_ref=terms_ref.at[peer],
            dst_ref=arrived.at[slot],
            send_sem=send.at[peer],
            recv_sem=receive.at[slot],
            device_id=(peer // ne, lax.rem(peer, ne)),
            device_id_type=MESH,
        )

    def begin(step, carry):
        copy_of(me, lax.rem(me + step, total)).start()
        return carry

    lax.fori_loop(1, total, begin, 0)
    arrived[me] = terms_ref[me]

    def end(step, carry):
        peer = lax.rem(me + step, total)
        copy = copy_of(peer, peer)
        copy.wait_recv()
        copy.wait_send()
        return carry

    lax.fori_loop(1, total, end, 0)
    sum_ref[...] = jnp.sum(arrived[...], axis=0)


def collect(terms):
    devices = terms.shape[0]
    return pl.pallas_call(
        collect_kernel,
        out_shape=jax.ShapeDtypeStruct(terms.shape[1:], terms.dtype),
        in_specs=[pl.BlockSpec(memory_space=pltpu.VMEM)],
        out_specs=pl.BlockSpec(memory_space=pltpu.VMEM),
        scratch_shapes=[pltpu.VMEM(terms.shape, terms.dtype)]
        + [pltpu.SemaphoreType.DMA((devices,))] * 2,
        compiler_params=pltpu.CompilerParams(collective_id=2, has_side_effects=True),
        name="collect",
    )(terms)


def places(chips):
    f, e = lax.axis_index("fsdp"), lax.axis_index("expert")
    z, c = e // 2, lax.rem(e, 2)
    up = (f, jnp.minimum(z + 1, chips - 1) * 2 + c)
    down = (f, jnp.maximum(z - 1, 0) * 2 + c)
    return f, e, z, c, up, down, (f, z * 2 + 1 - c), (f ^ 1, e), (f ^ 2, e)


def meet(chips, z, up, down, others):
    barrier = pltpu.get_barrier_semaphore()
    for peer in others:
        pl.semaphore_signal(barrier, inc=1, device_id=peer, device_id_type=MESH)

    @pl.when(z < chips - 1)
    def _():
        pl.semaphore_signal(barrier, inc=1, device_id=up, device_id_type=MESH)

    @pl.when(z > 0)
    def _():
        pl.semaphore_signal(barrier, inc=1, device_id=down, device_id_type=MESH)

    known = len(others) + jnp.where(z < chips - 1, 1, 0) + jnp.where(z > 0, 1, 0)
    pl.semaphore_wait(barrier, known)


def remote_copy(source, target, send, receive, device):
    return pltpu.make_async_remote_copy(
        src_ref=source,
        dst_ref=target,
        send_sem=send,
        recv_sem=receive,
        device_id=device,
        device_id_type=MESH,
    )


def spread_kernel(
    chips, block_ref, tokens_ref, all_ref, row_ref,
    up_sem, down_sem, in_low, in_high, to_partner, in_partner, send_n, receive_n, local,
):
    f, e, z, c, up, down, partner, side_x, side_y = places(chips)
    xn, yn = f ^ 1, f ^ 2
    own = [
        pltpu.make_async_copy(block_ref, all_ref.at[e], local.at[0]),
        pltpu.make_async_copy(tokens_ref, row_ref.at[0], local.at[1]),
    ]
    for copy in own:
        copy.start()
    meet(chips, z, up, down, (partner, side_x, side_y))

    def shard(origin, target, send, receive, first):
        place = all_ref.at[origin * 2 + c]
        return remote_copy(block_ref if first else place, place, send, receive, target)

    def upward(origin, r, first=False):
        return shard(origin, up, up_sem.at[r], in_low.at[r], first)

    def downward(origin, r, first=False):
        return shard(origin, down, down_sem.at[r], in_high.at[r], first)

    def across(origin, first=False):
        return shard(origin, partner, to_partner.at[origin], in_partner.at[origin], first)

    @pl.when(z < chips - 1)
    def _():
        upward(z, 0, True).start()

    @pl.when(z > 0)
    def _():
        downward(z, 0, True).start()

    across(z, True).start()
    half = tokens_ref.shape[0] // 2
    low, high = pl.ds(0, half), pl.ds(half, half)

    def piece(origin, rows, device, slot):
        source = tokens_ref.at[rows] if slot < 4 else row_ref.at[origin ^ f, rows]
        return remote_copy(
            source, row_ref.at[origin ^ device, rows], send_n.at[slot], receive_n.at[slot], (device, e)
        )

    def arrived(origin, rows, slot):
        place = row_ref.at[origin ^ f, rows]
        return remote_copy(place, place, send_n.at[slot], receive_n.at[slot], side_x)

    copies = [piece(f, low, xn, 0), piece(f, high, yn, 1), piece(f, high, xn, 2), piece(f, low, yn, 3)]
    relays = [piece(xn, low, yn, 4), piece(yn, high, xn, 5)]
    for copy in copies:
        copy.start()
    arrived(xn, low, 0).wait_recv()
    relays[0].start()
    arrived(yn, high, 1).wait_recv()
    relays[1].start()

    def hop(r, carry):
        before, after = z - r, z + r

        @pl.when(before >= 0)
        def _():
            upward(before, r - 1).wait_recv()

            @pl.when(z < chips - 1)
            def _():
                upward(before, r).start()

            across(before).start()

        @pl.when(after < chips)
        def _():
            downward(after, r - 1).wait_recv()

            @pl.when(z > 0)
            def _():
                downward(after, r).start()

            across(after).start()

        return carry

    lax.fori_loop(1, chips, hop, 0)
    arrived(xn, high, 2).wait_recv()
    arrived(yn, low, 3).wait_recv()
    arrived(f ^ 3, low, 4).wait_recv()
    arrived(f ^ 3, high, 5).wait_recv()
    for copy in copies + relays:
        copy.wait_send()
    for copy in own:
        copy.wait()

    @pl.when(z < chips - 1)
    def _():
        upward(z, 0, True).wait_send()

    @pl.when(z > 0)
    def _():
        downward(z, 0, True).wait_send()

    def finish(r, carry):
        before, after = z - r, z + r

        @pl.when((before >= 0) & (z < chips - 1))
        def _():
            upward(before, r).wait_send()

        @pl.when((after < chips) & (z > 0))
        def _():
            downward(after, r).wait_send()

        return carry

    lax.fori_loop(1, chips, finish, 0)

    def shared(origin, carry):
        across(origin).wait_send()
        across(origin).wait_recv()
        return carry

    lax.fori_loop(0, chips, shared, 0)


def spread(block, tokens, nf, ne, cid):
    chips = ne // 2
    dma = pltpu.SemaphoreType.DMA
    return pl.pallas_call(
        functools.partial(spread_kernel, chips),
        out_shape=[
            jax.ShapeDtypeStruct((ne,) + block.shape, block.dtype),
            jax.ShapeDtypeStruct((nf,) + tokens.shape, tokens.dtype),
        ],
        in_specs=[pl.BlockSpec(memory_space=pltpu.VMEM)] * 2,
        out_specs=[pl.BlockSpec(memory_space=pltpu.VMEM)] * 2,
        scratch_shapes=[dma((chips,))] * 6 + [dma((6,))] * 2 + [dma((2,))],
        compiler_params=pltpu.CompilerParams(
            collective_id=cid, has_side_effects=True, vmem_limit_bytes=60 * 1024 * 1024
        ),
        cost_estimate=WIRE,
        name=f"spread{cid}",
    )(block, tokens)


def combine_kernel(
    chips, terms_ref, parts_ref, sum_ref, row_sum_ref,
    theirs, going, coming, corner, onward, from_side,
    up_sem, down_sem, in_low, in_high, to_partner, in_partner, send_n, receive_n,
):
    f, e, z, c, up, down, partner, side_x, side_y = places(chips)
    meet(chips, z, up, down, (partner, side_x, side_y))

    def across(target):
        return remote_copy(
            terms_ref.at[target * 2 + 1 - c], theirs.at[target],
            to_partner.at[target], in_partner.at[target], partner,
        )

    def upward(target):
        return remote_copy(
            going.at[target], coming.at[target], up_sem.at[target], in_low.at[target], up
        )

    def downward(target, receiver):
        place = coming.at[jnp.where(target == receiver, chips, target)]
        return remote_copy(
            going.at[target], place, down_sem.at[target], in_high.at[target], down
        )

    def offer(r, carry):
        across(r).start()
        across(chips - 1 - r).start()
        return carry

    lax.fori_loop(0, chips // 2, offer, 0)
    half = parts_ref.shape[1] // 2
    low, high = pl.ds(0, half), pl.ds(half, half)

    def side(slot, source, target, device):
        return remote_copy(source, target, send_n.at[slot], receive_n.at[slot], device)

    copies = [
        side(0, parts_ref.at[3, low], corner.at[0], side_x),
        side(1, parts_ref.at[3, high], corner.at[1], side_y),
        side(2, parts_ref.at[1, low], from_side.at[0, low], side_x),
        side(3, parts_ref.at[2, high], from_side.at[1, high], side_y),
        side(4, onward.at[0], from_side.at[0, high], side_x),
        side(5, onward.at[1], from_side.at[1, low], side_y),
    ]
    for copy in copies[:4]:
        copy.start()

    def chip_term(target):
        return terms_ref[target * 2 + c].astype(F32) + theirs[target].astype(F32)

    def rise(r):
        target = chips - 1 - r

        @pl.when(target > z)
        def _():
            across(target).wait_recv()

            @pl.when(z > 0)
            def _():
                upward(target).wait_recv()
                going[target] = (chip_term(target) + coming[target].astype(F32)).astype(BF16)

            @pl.when(z == 0)
            def _():
                going[target] = chip_term(target).astype(BF16)

            upward(target).start()

    def fall(r):
        @pl.when(r < z)
        def _():
            across(r).wait_recv()

            @pl.when(z < chips - 1)
            def _():
                downward(r, z).wait_recv()
                going[r] = (chip_term(r) + coming[r].astype(F32)).astype(BF16)

            @pl.when(z == chips - 1)
            def _():
                going[r] = chip_term(r).astype(BF16)

            downward(r, z - 1).start()

    def pass_on(r, carry):
        @pl.when(z < chips // 2)
        def _():
            rise(r)

        fall(r)

        @pl.when(z >= chips // 2)
        def _():
            rise(r)

        return carry

    lax.fori_loop(0, 1, pass_on, 0)
    copies[1].wait_recv()
    onward[0] = (parts_ref[1, high].astype(F32) + corner[1].astype(F32)).astype(BF16)
    copies[4].start()
    copies[0].wait_recv()
    onward[1] = (parts_ref[2, low].astype(F32) + corner[0].astype(F32)).astype(BF16)
    copies[5].start()
    lax.fori_loop(1, chips, pass_on, 0)
    for copy in copies[2:]:
        copy.wait_recv()
    row_sum_ref[...] = (
        parts_ref[0].astype(F32) + from_side[0].astype(F32) + from_side[1].astype(F32)
    )
    across(z).wait_recv()
    sum_ref[...] = chip_term(z)

    @pl.when(z > 0)
    def _():
        upward(z).wait_recv()
        sum_ref[...] += coming[z].astype(F32)

    @pl.when(z < chips - 1)
    def _():
        downward(z, z).wait_recv()
        sum_ref[...] += coming[chips].astype(F32)

    for copy in copies:
        copy.wait_send()

    def finish(target, carry):
        across(target).wait_send()

        @pl.when(target > z)
        def _():
            upward(target).wait_send()

        @pl.when(target < z)
        def _():
            downward(target, z - 1).wait_send()

        return carry

    lax.fori_loop(0, chips, finish, 0)


def combine(terms, parts, cid):
    ne = terms.shape[0]
    chips = ne // 2
    parts = parts.reshape(4, parts.shape[0] // 4, parts.shape[1])
    block = terms.shape[1:]
    halves = (2, parts.shape[1] // 2, parts.shape[2])
    sides = (2,) + parts.shape[1:]
    dma = pltpu.SemaphoreType.DMA
    return pl.pallas_call(
        functools.partial(combine_kernel, chips),
        out_shape=[
            jax.ShapeDtypeStruct(terms.shape[1:], F32),
            jax.ShapeDtypeStruct(parts.shape[1:], F32),
        ],
        in_specs=[pl.BlockSpec(memory_space=pltpu.VMEM)] * 2,
        out_specs=[pl.BlockSpec(memory_space=pltpu.VMEM)] * 2,
        scratch_shapes=[pltpu.VMEM((chips,) + block, BF16)] * 2
        + [pltpu.VMEM((chips + 1,) + block, BF16)]
        + [pltpu.VMEM(halves, BF16)] * 2
        + [pltpu.VMEM(sides, BF16)]
        + [dma((chips,))] * 6
        + [dma((6,))] * 2,
        compiler_params=pltpu.CompilerParams(
            collective_id=cid, has_side_effects=True, vmem_limit_bytes=60 * 1024 * 1024
        ),
        cost_estimate=WIRE,
        name=f"combine{cid}",
    )(terms, parts)


def on_device(
    inputs,
    teacher,
    lengths,
    deal_order,
    routes,
    route_weights,
    norm_gains,
    mixer_weights,
    shared_weights,
    shared_gate,
    expert_gate,
    expert_up,
    expert_down,
):
    tokens_dev = inputs.shape[1]
    width = inputs.shape[2]
    nf = lax.axis_size("fsdp")
    ne = lax.axis_size("expert")
    devices = nf * ne
    row_len = tokens_dev * nf
    capacity = 3 * tokens_dev * TOP // (2 * ne)
    total_tokens = row_len * ne
    columns = mixer_weights.shape[2]
    heads_local = columns // HD
    f_index = lax.axis_index("fsdp")
    e_index = lax.axis_index("expert")

    piece = norm_gains.shape[1]
    slot = (f_index * ne + e_index) % (128 // piece)
    vector = jnp.concatenate([norm_gains, shared_gate[None]], axis=0).astype(F32)
    vector = lax.dynamic_update_slice(jnp.zeros((8, 128), F32), vector, (0, slot * piece))
    chosen = routes[0]
    weights_route = route_weights[0]
    expert_ids = jnp.arange(ne, dtype=jnp.int32)
    routed = jnp.sum(
        jnp.where(chosen.T[None] == expert_ids[:, None, None], weights_route.T[None], 0.0), axis=1
    )
    mixer_shard = jnp.transpose(mixer_weights, (1, 0, 2))
    gains, tables, row_blocks, mixer_in, mixer_out, gates = opening(
        inputs[0], vector, routed, mixer_shard, expert_gate[0], nf
    )
    first_gain, second_gain, gate_vector = gains[0], gains[1], gains[2]
    token_weight = lax.dynamic_index_in_dim(tables, e_index, axis=1, keepdims=False)
    mixer_in = mixer_in.reshape(3, width, columns)
    mixer_out = mixer_out.reshape(width, columns)
    gate_rows = gates.reshape(width, gates.shape[2])
    row_normed = row_blocks.reshape(row_len, width)

    shared_shard, up_shard, down_shard, gains = lax.optimization_barrier(
        (shared_weights, expert_up[0], expert_down[0], gains)
    )
    shared_shard = jnp.transpose(shared_shard, (1, 0, 2))
    shared_first = lax.all_gather(shared_shard[0], "expert", axis=0, tiled=True)
    up_sides = gather_sides(up_shard)

    first_len = lengths[deal_order[2 * e_index]]
    second_len = lengths[deal_order[2 * e_index + 1]]
    row_places = (
        (f_index ^ jnp.arange(nf, dtype=jnp.int32))[:, None] * tokens_dev
        + jnp.arange(tokens_dev, dtype=jnp.int32)[None]
    ).reshape(row_len)
    row_segment = (row_places >= first_len).astype(jnp.int32) + (
        row_places >= first_len + second_len
    ).astype(jnp.int32)
    row_position = (
        row_places
        - first_len * (row_segment >= 1).astype(jnp.int32)
        - second_len * (row_segment >= 2).astype(jnp.int32)
    )
    own_segment = row_segment[:tokens_dev]
    allowed = (row_segment[:, None] == row_segment[None, :]) & (
        row_places[None, :] <= row_places[:, None]
    )
    inverse = THETA ** (-(jnp.arange(HD // 2, dtype=F32) * 2.0) / HD)
    angles = row_position.astype(F32)[:, None] * inverse[None, :]
    cosine = jnp.concatenate([jnp.cos(angles)] * 2, axis=1)[:, None, :]
    sine = jnp.concatenate([jnp.sin(angles)] * 2, axis=1)[:, None, :]

    flat_inputs = inputs[0].astype(F32)
    first_scale = lax.rsqrt(jnp.mean(flat_inputs * flat_inputs, axis=1) + EPSILON)
    projected = dot("td,kde->kte", row_normed, mixer_in)

    def heads(values):
        return values.reshape(row_len, heads_local, HD)

    raw_query, raw_key = heads(projected[0]), heads(projected[1])
    queries = (raw_query * cosine + turn(raw_query) * sine).astype(BF16)
    keys = (raw_key * cosine + turn(raw_key) * sine).astype(BF16)
    values = heads(projected[2].astype(BF16))
    score_factor = HD ** (-0.5)

    def score():
        raw = dot("qhd,khd->hqk", queries, keys)
        return jnp.where(allowed[None], raw * score_factor, NEG_LARGE)

    scores = score()
    top_score = jnp.max(scores, axis=2, keepdims=True)
    shifted = jnp.exp(scores - top_score)
    row_total = jnp.sum(shifted, axis=2, keepdims=True)
    probabilities = shifted / row_total
    log_total = top_score + jnp.log(row_total)
    context = dot("hqk,khd->qhd", probabilities.astype(BF16), values)
    context = context.reshape(row_len, columns).astype(BF16)
    attn_out = row_scatter(dot("tc,dc->td", context, mixer_out))
    residual = flat_inputs + attn_out
    second_scale = lax.rsqrt(jnp.mean(residual * residual, axis=1) + EPSILON)
    mixed_in = (residual * second_scale[:, None] * second_gain[None, :]).astype(BF16)

    down_shard, mixed_in = lax.optimization_barrier((down_shard, mixed_in))
    up_rows = gather_shards(up_shard, up_sides, f_index)
    down_rows = gather_shards(down_shard, gather_sides(down_shard), f_index)
    tokens_all, row_mixed = spread(mixed_in, mixed_in, nf, ne, 3)
    row_mixed = row_mixed.reshape(row_len, width)
    second_shard, third_shard, tokens_all = lax.optimization_barrier(
        (shared_shard[1], shared_shard[2], tokens_all)
    )
    shared_second = lax.all_gather(second_shard, "expert", axis=0, tiled=True)
    shared_down = lax.all_gather(third_shard, "expert", axis=0, tiled=True)
    routed_here = token_weight > 0.0
    marks = routed_here.astype(BF16)
    upper = (
        jnp.arange(tokens_dev, dtype=jnp.int32)[:, None]
        <= jnp.arange(tokens_dev, dtype=jnp.int32)[None, :]
    ).astype(BF16)
    order = dot("st,tu->su", marks, upper) - 1.0
    slots = jnp.arange(capacity, dtype=jnp.int32).astype(F32)
    hit = (order[:, None, :] == slots[None, :, None]) & routed_here[:, None, :]
    picker = hit.astype(BF16)
    slot_weight = jnp.sum(jnp.where(hit, token_weight[:, None, :], 0.0), axis=2).reshape(
        ne * capacity, 1
    )

    def pick(blocks):
        return dot("srt,std->srd", picker, blocks).reshape(ne * capacity, width)

    def unpick(rows):
        return dot("srt,srd->std", picker, rows.reshape(ne, capacity, width)).astype(BF16)

    rows_in = pick(tokens_all).astype(BF16)
    gate_pre = dot("rd,df->rf", rows_in, gate_rows)
    up_pre = dot("rd,df->rf", rows_in, up_rows)
    hidden = (jax.nn.silu(gate_pre) * up_pre).astype(BF16)
    result = (slot_weight * dot("rf,fd->rd", hidden, down_rows)).astype(BF16)


    shared_pre = (dot("td,df->tf", row_mixed, shared_first), dot("td,df->tf", row_mixed, shared_second))
    shared_hidden = (jax.nn.silu(shared_pre[0]) * shared_pre[1]).astype(BF16)
    routed_sum, shared_out = combine(
        unpick(result), dot("tf,df->td", shared_hidden, shared_down).astype(BF16), 4
    )
    gate_value = jax.nn.sigmoid(
        jnp.sum(mixed_in.astype(F32) * gate_vector[None, :], axis=1)
    )

    block_total = residual + gate_value[:, None] * shared_out + routed_sum
    out_block = block_total.astype(BF16)[None]
    valid_mask = (own_segment < 2).astype(F32)
    valid_count = jnp.sum(lengths).astype(F32)
    dtotal = (
        total_tokens
        / valid_count
        * valid_mask[:, None]
        * (block_total - teacher[0].astype(F32))
    )

    dshared_out = (gate_value[:, None] * dtotal).astype(BF16)
    dlogit = jnp.sum(dtotal * shared_out, axis=1) * gate_value * (1.0 - gate_value)
    dtotal_all, row_dout = spread(dtotal.astype(BF16), dshared_out, nf, ne, 5)
    row_dout = row_dout.reshape(row_len, width)
    down_term = dot("td,tf->df", row_dout, shared_hidden).astype(BF16)
    row_dout, dtotal_all, down_term = lax.optimization_barrier((row_dout, dtotal_all, down_term))
    shared_sigmoid = jax.nn.sigmoid(shared_pre[0])
    dshared_hidden = dot("td,df->tf", row_dout, shared_down)
    dshared_gate = (
        dshared_hidden * shared_pre[1] * shared_sigmoid * (1.0 + shared_pre[0] * (1.0 - shared_sigmoid))
    ).astype(BF16)
    dshared_up = (dshared_hidden * shared_pre[0] * shared_sigmoid).astype(BF16)
    dmixed_first = dot("tf,df->td", dshared_gate, shared_first)

    def scatter_columns(term):
        return lax.psum_scatter(term.astype(BF16), "expert", scatter_dimension=0, tiled=True)

    grad_shared_down = scatter_columns(down_term)
    gate_term = dot("td,tf->df", row_mixed, dshared_gate).astype(BF16)
    up_term = dot("td,tf->df", row_mixed, dshared_up).astype(BF16)

    dresult = (slot_weight * pick(dtotal_all)).astype(BF16)
    gate_sigmoid = jax.nn.sigmoid(gate_pre)
    activated = gate_pre * gate_sigmoid
    grad_down_term = dot("rf,rd->fd", hidden, dresult).astype(BF16)
    dresult, grad_down_term = lax.optimization_barrier((dresult, grad_down_term))
    terms = [scatter_terms(grad_down_term, f_index)]
    corners = [scatter_corner(terms[0])]
    dhidden = dot("rd,fd->rf", dresult, down_rows)
    dgate = (dhidden * up_pre * gate_sigmoid * (1.0 + gate_pre * (1.0 - gate_sigmoid))).astype(BF16)
    dup = (dhidden * activated).astype(BF16)
    dreturn = (dot("rf,df->rd", dgate, gate_rows) + dot("rf,df->rd", dup, up_rows)).astype(BF16)
    dreturn, corners = lax.optimization_barrier((dreturn, corners))
    sides = [scatter_sides(terms[0], corners[0])]
    grad_gate_term = dot("rd,rf->df", rows_in, dgate).astype(BF16)
    terms.append(scatter_terms(grad_gate_term, f_index))
    corners.append(scatter_corner(terms[1]))
    dmixed_terms = (dmixed_first + dot("tf,df->td", dshared_up, shared_second)).astype(BF16)
    dreturned, up_term, gate_term, corners = lax.optimization_barrier(
        (unpick(dreturn), up_term, gate_term, corners)
    )
    grad_shared_gates = scatter_columns(gate_term)
    sides.append(scatter_sides(terms[1], corners[1]))
    from_experts, dmixed_shared = combine(dreturned, dmixed_terms, 6)
    from_experts, up_term, corners, sides, grad_shared_down = lax.optimization_barrier(
        (from_experts, up_term, corners, sides, grad_shared_down)
    )
    grad_shared_ups = scatter_columns(up_term)

    dmixed = dmixed_shared + dlogit[:, None] * gate_vector[None, :] + from_experts
    vector_term = jnp.sum(dlogit[:, None] * mixed_in.astype(F32), axis=0)
    dresidual_norm, second_gain_grad = norm_back(dmixed, residual, second_scale, second_gain)
    dresidual = dtotal + dresidual_norm
    dattn = dresidual.astype(BF16)
    dattn, rows_again, dup = lax.optimization_barrier((dattn, rows_in, dup))
    row_dattn = row_tokens(dattn)
    grad_up_term = dot("rd,rf->df", rows_again, dup).astype(BF16)
    row_dattn, grad_up_term, grad_shared_gates = lax.optimization_barrier(
        (row_dattn, grad_up_term, grad_shared_gates)
    )
    terms.append(scatter_terms(grad_up_term, f_index))
    corners.append(scatter_corner(terms[2]))

    dcontext = dot("td,dc->tc", row_dattn, mixer_out).astype(BF16)
    mixer_out_term = dot("td,tc->dc", row_dattn, context).astype(BF16)
    mixer_base = jnp.pad(mixer_out_term[None], ((3, 0), (0, 0), (0, 0)))
    dcontext, mixer_base = lax.optimization_barrier((dcontext, mixer_base))
    dcontext = heads(dcontext)
    probabilities_again = jnp.exp(score() - log_total)
    dprobs = dot("qhd,khd->hqk", dcontext, values)
    delta_rows = jnp.sum(probabilities_again * dprobs, axis=2, keepdims=True)
    dscores = (probabilities_again * (dprobs - delta_rows)).astype(BF16)
    dqueries = dot("hqk,khd->qhd", dscores, keys) * score_factor
    dkeys = dot("hqk,qhd->khd", dscores, queries) * score_factor
    dvalues = dot("hqk,qhd->khd", probabilities_again.astype(BF16), dcontext)

    def back(incoming):
        return (incoming * cosine + turn_back(incoming * sine)).reshape(row_len, columns)

    dprojected = jnp.stack(
        [back(dqueries), back(dkeys), dvalues.reshape(row_len, columns)], axis=0
    ).astype(BF16)
    dprojected, corners[2] = lax.optimization_barrier((dprojected, corners[2]))
    sides.append(scatter_sides(terms[2], corners[2]))
    mixer_term = dot("td,kte->kde", row_normed, dprojected).astype(BF16)
    mixer_term = lax.dynamic_update_slice(mixer_base, mixer_term, (0, 0, 0))
    mixer_term, grad_shared_ups = lax.optimization_barrier((mixer_term, grad_shared_ups))
    grad_mixer = lax.psum_scatter(mixer_term, "expert", scatter_dimension=1, tiled=True)
    dnormed = dot("kte,kde->td", dprojected, mixer_in).astype(BF16)
    dnormed, sides[2] = lax.optimization_barrier((row_scatter(dnormed), sides[2]))
    grad_expert_down, grad_expert_gate, grad_expert_up = [
        scatter_end(parts, side)[None] for parts, side in zip(terms, sides)
    ]
    dflat, first_gain_grad = norm_back(dnormed, flat_inputs, first_scale, first_gain)
    grad_input = (dresidual + dflat)[None]

    grad_shared = jnp.stack([grad_shared_gates, grad_shared_ups, grad_shared_down], axis=1)
    grad_shared = grad_shared.astype(F32)
    terms = jnp.stack([first_gain_grad, second_gain_grad, vector_term]).reshape(3, devices, piece)
    terms = jnp.pad(jnp.transpose(terms, (1, 0, 2)), ((0, 0), (0, 5), (0, 128 - piece)))
    sums = collect(terms)
    (grad_mixer, sums, grad_shared, grad_expert_down, grad_expert_gate, grad_expert_up) = (
        lax.optimization_barrier(
            (grad_mixer, sums, grad_shared, grad_expert_down, grad_expert_gate, grad_expert_up)
        )
    )
    grad_mixer = jnp.transpose(grad_mixer, (1, 0, 2)).astype(F32)
    grad_gains = sums[:2, :piece]
    grad_shared_gate = sums[2, :piece]
    return (
        out_block,
        grad_input,
        grad_gains,
        grad_mixer,
        grad_shared,
        grad_shared_gate,
        grad_expert_gate,
        grad_expert_up,
        grad_expert_down,
    )


def solution(mesh):
    rows = P("expert", "fsdp", None)
    both = P(("fsdp", "expert"))
    gains = P(None, ("fsdp", "expert"))
    shared = P("expert", None, "fsdp")
    return jax.shard_map(
        on_device,
        mesh=mesh,
        in_specs=(rows, rows, P(), P(), rows, rows, gains, shared, shared, both, rows, rows, rows),
        out_specs=(rows, rows, gains, shared, shared, both, rows, rows, rows),
        check_vma=False,
    )
```
